32 devices in a mesh: dp: 2 (over x), ctx: 4 (over y, core), tp: 4 (over z).
Axes of the slice: x: 2, y: 2, z: 4, core: 2. Of those that a mesh axis runs over, the one named last changes fastest.
Arguments:
- layer_input: bfloat16 [8192, 2048], P(('dp', 'ctx'), 'tp'), may hold values from -6 to 6
- gain_attn: float32 [2048], P('tp'), may hold values from 0.5 to 1.5
- w_query: bfloat16 [2048, 2048], P(('dp', 'ctx'), 'tp'), may hold values from -0.125 to 0.125
- w_key: bfloat16 [2048, 2048], P(('dp', 'ctx'), 'tp'), may hold values from -0.125 to 0.125
- w_value: bfloat16 [2048, 4096], P(('dp', 'ctx'), 'tp'), may hold values from -0.125 to 0.125
- w_retgate: bfloat16 [2048, 4096], P(('dp', 'ctx'), 'tp'), may hold values from -0.125 to 0.125
- w_out: bfloat16 [2048, 4096], P(('dp', 'ctx'), 'tp'), may hold values from -0.125 to 0.125
- gain_mlp: float32 [2048], P('tp'), may hold values from 0.5 to 1.5
- w_gate: bfloat16 [2048, 4096], P(('dp', 'ctx'), 'tp'), may hold values from -0.125 to 0.125
- w_up: bfloat16 [2048, 4096], P(('dp', 'ctx'), 'tp'), may hold values from -0.125 to 0.125
- w_down: bfloat16 [2048, 4096], P(('dp', 'ctx'), 'tp'), may hold values from -0.09375 to 0.09375
- cotangent: bfloat16 [8192, 2048], P(('dp', 'ctx'), 'tp'), may hold values from -6 to 6
Outputs:
- layer_output: bfloat16 [8192, 2048], P(('dp', 'ctx'), 'tp')
- grad_input: bfloat16 [8192, 2048], P(('dp', 'ctx'), 'tp')
- grad_gain_attn: float32 [2048], P('tp')
- grad_w_query: float32 [2048, 2048], P(('dp', 'ctx'), 'tp')
- grad_w_key: float32 [2048, 2048], P(('dp', 'ctx'), 'tp')
- grad_w_value: float32 [2048, 4096], P(('dp', 'ctx'), 'tp')
- grad_w_retgate: float32 [2048, 4096], P(('dp', 'ctx'), 'tp')
- grad_w_out: float32 [2048, 4096], P(('dp', 'ctx'), 'tp')
- grad_gain_mlp: float32 [2048], P('tp')
- grad_w_gate: float32 [2048, 4096], P(('dp', 'ctx'), 'tp')
- grad_w_up: float32 [2048, 4096], P(('dp', 'ctx'), 'tp')
- grad_w_down: float32 [2048, 4096], P(('dp', 'ctx'), 'tp')
The draws below stay inside these ranges and needn't reach their ends.
All inputs are finite; a program needn't handle non-finite values.
Results may differ from the reference program's by a relative error of at most 0.019.
Values may be sent and summed in bfloat16 or wider, within the bound.
No kernel may reach another device: no remote copies, remote signals or barrier semaphores. Data moves between devices by JAX's collectives and lax.ppermute only.
A program may use at most 192 MiB of HBM per device.

```python
import math
from functools import partial
import jax
import jax.numpy as jnp
from jax import lax

D = 2048
HEADS = 8
HK = 256
HV = 512
FF = 4096
TOK_DEV = 1024
LENGTH = 4096
SEQS = 2
TOKENS = 8192


def with_spikes(values, rng, source, target, parts, factor):
    def block_of(axis_at):
        return (jnp.arange(values.shape[axis_at]) // (values.shape[axis_at] // parts)).reshape((-1,) + (1,) * (values.ndim - 1 - axis_at))

    near = jax.random.permutation(rng, parts)[block_of(target)]
    far = (block_of(target) + parts // 2) % parts
    return jnp.where((block_of(source) == near) | (block_of(source) == far), factor * values, values)


def block_levels(own_key, dims, shards, smallest, high):
    loudness = 1.0
    for position, blocks in shards:
        draws = jax.random.uniform(jax.random.fold_in(jax.random.fold_in(own_key, 6), position), (blocks,), jnp.float32, smallest / len(shards), high / len(shards))
        loudness = loudness * jnp.repeat(jnp.exp(draws), dims[position] // blocks).reshape((-1,) + (1,) * (len(dims) - 1 - position))
    return loudness


def noise(rng, dims, spread, limit, shards=(), kind=jnp.bfloat16):
    gain = block_levels(rng, dims, shards, -0.22, 0.18) if shards else 1.0
    values = jax.random.normal(rng, dims, jnp.float32) * spread * gain
    return jnp.minimum(jnp.maximum(values, -limit), limit).astype(kind)


def gaussian_with(stream_key, dims, width, most, cuts, heavy, kind=jnp.bfloat16):
    values = width * jax.random.normal(stream_key, dims, jnp.float32)
    if cuts:
        values = values * block_levels(stream_key, dims, cuts, -0.22, 0.18)
    return jnp.clip(with_spikes(values, jax.random.fold_in(stream_key, 3), *heavy), -most, most).astype(kind)


def setup_inputs(seed: int = 0) -> dict:
    streams_of = jax.random.split(jax.random.key(seed), 13)
    return {
        "layer_input": noise(streams_of[0], (TOKENS, D), 1.0, 6.0, ((0, 8), (1, 4))),
        "gain_attn": jnp.clip(1.0 + 0.1 * jax.random.normal(streams_of[1], (D,), jnp.float32), 0.5, 1.5),
        "w_query": noise(streams_of[2], (D, HEADS * HK), D ** -0.5, 0.125, ((0, 8), (1, 4))),
        "w_key": noise(streams_of[3], (D, HEADS * HK), D ** -0.5, 0.125, ((0, 8), (1, 4))),
        "w_value": noise(streams_of[4], (D, HEADS * HV), D ** -0.5, 0.125, ((0, 8), (1, 4))),
        "w_retgate": noise(streams_of[5], (D, HEADS * HV), D ** -0.5, 0.125, ((0, 8), (1, 4))),
        "w_out": noise(streams_of[6], (D, HEADS * HV), D ** -0.5, 0.125, ((0, 8), (1, 4))),
        "gain_mlp": jnp.clip(1.0 + 0.1 * jax.random.normal(streams_of[7], (D,), jnp.float32), 0.5, 1.5),
        "w_gate": noise(streams_of[8], (D, FF), D ** -0.5, 0.125, ((0, 8), (1, 4))),
        "w_up": noise(streams_of[9], (D, FF), D ** -0.5, 0.125, ((0, 8), (1, 4))),
        "w_down": noise(streams_of[10], (D, FF), FF ** -0.5, 0.09375, ((0, 8), (1, 4))),
        "cotangent": gaussian_with(streams_of[11], (TOKENS, D), 1.0, 6.0, ((0, 8), (1, 4)), (0, 1, 8, 2.0)),
    }


@jax.custom_vjp
def low(v):
    return lax.optimization_barrier(v.astype(jnp.bfloat16)).astype(jnp.float32)

@jax.custom_vjp
def low_back(v):
    return v

def low_keep(v):
    return (low(v), None)

def low_pass(kept, grad):
    return (grad,)

def back_keep(v):
    return (v, None)

def back_low(kept, grad):
    return (low(grad),)
low.defvjp(low_keep, low_pass)
low_back.defvjp(back_keep, back_low)
EPSILON = 1e-06
HIGHEST = lax.Precision.HIGHEST

def product(left, right):
    return jnp.dot(left, right, precision=HIGHEST, preferred_element_type=jnp.float32)

def rms_norm(value_rows, gain_vec):
    norm_scale = lax.rsqrt(lax.optimization_barrier(jnp.mean(value_rows * value_rows, axis=-1, keepdims=True)) + EPSILON)
    return value_rows * norm_scale * gain_vec

def rotate(value_rows, cosine, sine_table):
    full_shape = value_rows.shape
    pair_view = value_rows.reshape(full_shape[:-1] + (full_shape[-1] // 2, 2))
    first_half = pair_view[..., 0]
    second_half = pair_view[..., 1]
    cos_rows = cosine[:, None, :]
    sin_rows = sine_table[:, None, :]
    turned = jnp.stack([first_half * cos_rows - second_half * sin_rows, second_half * cos_rows + first_half * sin_rows], axis=-1)
    return turned.reshape(full_shape)

def rotation_tables(positions, pair_count):
    frequencies = jnp.exp(-math.log(10000.0) * jnp.linspace(0.0, 1.0, pair_count, dtype=jnp.float32))
    angles = positions.astype(jnp.float32)[:, None] * frequencies[None, :]
    return (jnp.cos(angles), jnp.sin(angles))

def log_decays(first_head, head_total):
    indices = (first_head + jnp.arange(head_total)).astype(jnp.float32)
    return jnp.log1p(-jnp.exp2(-5.0 - indices))

def block_step(log_gamma, span, carry_state, pieces):
    query_rows, key_rows, value_rows = pieces
    steps_pos = jnp.arange(span).astype(jnp.float32)
    offsets = steps_pos[:, None] - steps_pos[None, :]
    decay_mask = jnp.where(offsets[None] >= 0.0, jnp.exp(jnp.maximum(offsets, 0.0)[None] * log_gamma[:, None, None]), 0.0)
    head_decay = jnp.exp(steps_pos[:, None] * log_gamma[None, :])
    tail_decay = jnp.exp((span - steps_pos)[:, None] * log_gamma[None, :])
    block_decay = jnp.exp(span * log_gamma)
    scores = low_back(jnp.einsum('snhk,smhk->shnm', query_rows, key_rows, precision=HIGHEST))
    weights = low(scores * decay_mask[None])
    inner_sum = jnp.einsum('shnm,smhv->snhv', weights, value_rows, precision=HIGHEST)
    cross_term = jnp.einsum('snhk,shkv->snhv', query_rows, low(carry_state), precision=HIGHEST) * head_decay[None, :, :, None]
    keyed_token_rows = low(key_rows * tail_decay[None, :, :, None])
    block_local_state = low_back(jnp.einsum('smhk,smhv->shkv', keyed_token_rows, value_rows, precision=HIGHEST))
    new_state = block_decay[None, :, None, None] * carry_state + block_local_state
    return (new_state, low_back(inner_sum + cross_term))

def forward(layer_input, gain_attn, w_query, w_key, w_value, w_retgate, w_out, gain_mlp, w_gate, w_up, w_down):
    total_rows = TOKENS
    normed = low(rms_norm(layer_input, gain_attn))
    positions = jnp.arange(total_rows) % LENGTH
    cosine, sine_table = rotation_tables(positions, HK // 2)
    q_pre = low_back(product(normed, w_query)).reshape(total_rows, HEADS, HK)
    k_pre = low_back(product(normed, w_key)).reshape(total_rows, HEADS, HK)
    query_rows = low(rotate(q_pre, cosine, sine_table))
    key_rows = low(rotate(k_pre, cosine, sine_table) * (1.0 / math.sqrt(HK)))
    value_rows = low(low_back(product(normed, w_value))).reshape(total_rows, HEADS, HV)
    gate_pre = low_back(product(normed, w_retgate))
    block_total = LENGTH // TOK_DEV

    def by_blocks(array_in):
        return jnp.moveaxis(array_in.reshape((SEQS, block_total, TOK_DEV) + array_in.shape[1:]), 1, 0)
    log_gamma = log_decays(0, HEADS)
    block_fn = jax.checkpoint(partial(block_step, log_gamma, TOK_DEV))
    zero_state = jnp.zeros((SEQS, HEADS, HK, HV), jnp.float32)
    _, retained = lax.scan(block_fn, zero_state, (by_blocks(query_rows), by_blocks(key_rows), by_blocks(value_rows)))
    retained = jnp.moveaxis(retained, 0, 1).reshape(total_rows, HEADS, HV)
    grouped = retained * lax.rsqrt(lax.optimization_barrier(jnp.mean(retained * retained, axis=-1, keepdims=True)) + EPSILON)
    gated = low(jax.nn.silu(gate_pre) * grouped.reshape(total_rows, HEADS * HV))
    attn_out = low_back(product(gated, w_out.T))
    middle = layer_input + attn_out
    normed_mlp = low(rms_norm(middle, gain_mlp))
    gate_act = low_back(product(normed_mlp, w_gate))
    up_act = low_back(product(normed_mlp, w_up))
    hidden = low(jax.nn.gelu(gate_act, approximate=False) * up_act)
    return middle + low_back(product(hidden, w_down.T))

def reference(layer_input, gain_attn, w_query, w_key, w_value, w_retgate, w_out, gain_mlp, w_gate, w_up, w_down, cotangent):
    result, pullback = jax.vjp(forward, layer_input.astype(jnp.float32), gain_attn.astype(jnp.float32), w_query.astype(jnp.float32), w_key.astype(jnp.float32), w_value.astype(jnp.float32), w_retgate.astype(jnp.float32), w_out.astype(jnp.float32), gain_mlp.astype(jnp.float32), w_gate.astype(jnp.float32), w_up.astype(jnp.float32), w_down.astype(jnp.float32))
    grads = pullback(cotangent.astype(jnp.float32))
    return (result.astype(jnp.bfloat16), grads[0].astype(jnp.bfloat16), grads[1], grads[2], grads[3], grads[4], grads[5], grads[6], grads[7], grads[8], grads[9], grads[10])
```

```python
import math

import jax
import jax.numpy as jnp
from jax import lax
from jax.sharding import PartitionSpec as P

HK = 256
HV = 512
EPSILON = 1e-06
F32 = jnp.float32
BF16 = jnp.bfloat16


def nn(a, b):
    return lax.dot_general(a, b, (((1,), (0,)), ((), ())), preferred_element_type=F32)


def tn(a, b):
    return lax.dot_general(a, b, (((0,), (0,)), ((), ())), preferred_element_type=F32)


def nt(a, b):
    return lax.dot_general(a, b, (((1,), (1,)), ((), ())), preferred_element_type=F32)


def right(n, lo, hi):
    return [(i, i + 1) for i in range(lo, hi)]


def left(n, lo, hi):
    return [(i, i - 1) for i in range(hi, lo, -1)]


def line_gather(x, axis):
    n, i = lax.axis_size(axis), lax.axis_index(axis)
    rights, lefts = [x], [x]
    for k in range(1, n):
        r_pairs = right(n, k - 1, n - 1)
        l_pairs = left(n, 0, n - k)
        if 2 * k > n + 1:
            both = lax.ppermute(jnp.where(i >= k - 1, rights[-1], lefts[-1]), axis, r_pairs + l_pairs)
            rights.append(both)
            lefts.append(both)
        else:
            rights.append(lax.ppermute(rights[-1], axis, r_pairs))
            lefts.append(lax.ppermute(lefts[-1], axis, l_pairs))
    return [x] + [jnp.where(i >= k, rights[k], lefts[n - k]) for k in range(1, n)]


def place(blocks, axis, dtype):
    n, i = lax.axis_size(axis), lax.axis_index(axis)
    rows, width = blocks[0].shape
    full = jnp.zeros((rows, n * width), dtype)
    for k, block in enumerate(blocks):
        at = ((i - k) % n) * width
        full = lax.dynamic_update_slice(full, block.astype(dtype), (0, at))
    return full


def line_scatter(parts, axis):
    n, i = lax.axis_size(axis), lax.axis_index(axis)
    width = parts.shape[1] // n

    def block(j):
        return lax.dynamic_slice(parts, (0, jnp.clip(j, 0, n - 1) * width), (parts.shape[0], width))

    from_left = from_right = None
    for k in range(1, n):
        r_pairs = right(n, 0, k)
        l_pairs = left(n, n - 1 - k, n - 1)
        r_data, l_data = block(i + n - k), block(i - n + k)
        if from_left is not None:
            r_data = (r_data.astype(F32) + from_left.astype(F32)).astype(BF16)
            l_data = (l_data.astype(F32) + from_right.astype(F32)).astype(BF16)
        if 2 * k < n - 1:
            from_left = from_right = lax.ppermute(jnp.where(i < k, r_data, l_data), axis, r_pairs + l_pairs)
            from_left = jnp.where(i <= k, from_left, jnp.zeros_like(from_left))
            from_right = jnp.where(i >= n - 1 - k, from_right, jnp.zeros_like(from_right))
        else:
            from_left = lax.ppermute(r_data, axis, r_pairs)
            from_right = lax.ppermute(l_data, axis, l_pairs)
    return block(i).astype(F32) + from_left.astype(F32) + from_right.astype(F32)


def small_sum(x, axis):
    n = lax.axis_size(axis)
    total = x
    for s in range(1, n):
        total = total + lax.ppermute(x, axis, [(j, (j + s) % n) for j in range(n)])
    return total


def small_gather(x, axis):
    n, i = lax.axis_size(axis), lax.axis_index(axis)
    blocks = [x] + [lax.ppermute(x, axis, [(j, (j + s) % n) for j in range(n)]) for s in range(1, n)]
    return place(blocks, axis, x.dtype)


def swap_sum(x, axis):
    n = lax.axis_size(axis)
    g = 1
    while g < n:
        x = x + lax.ppermute(x, axis, [(j, j ^ g) for j in range(n)])
        g *= 2
    return x


def states_before(local, log_block, axis):
    n, b = lax.axis_size(axis), lax.axis_index(axis)
    total, prefix, g = local, jnp.zeros_like(local), 1
    while g < n:
        got = lax.ppermute(total.astype(BF16), axis, [(j, j ^ g) for j in range(n)]).astype(F32)
        upper = (b // g) % 2 == 1
        mine = jnp.exp((b % g).astype(F32) * log_block)[:, None, None]
        whole = jnp.exp(g * log_block)[:, None, None]
        prefix = jnp.where(upper, prefix + mine * got, prefix)
        total = jnp.where(upper, whole * got + total, whole * total + got)
        g *= 2
    return prefix


def states_after(local, log_block, axis):
    n, b = lax.axis_size(axis), lax.axis_index(axis)
    total, suffix, g = local, jnp.zeros_like(local), 1
    while g < n:
        got = lax.ppermute(total.astype(BF16), axis, [(j, j ^ g) for j in range(n)]).astype(F32)
        upper = (b // g) % 2 == 1
        mine = jnp.exp((g - 1 - b % g).astype(F32) * log_block)[:, None, None]
        whole = jnp.exp(g * log_block)[:, None, None]
        suffix = jnp.where(upper, suffix, suffix + mine * got)
        total = jnp.where(upper, got + whole * total, total + whole * got)
        g *= 2
    return suffix


def halves_matrix():
    row = lax.broadcasted_iota(jnp.int32, (HK, HK), 0)
    col = lax.broadcasted_iota(jnp.int32, (HK, HK), 1)
    source = jnp.where(col < HK // 2, 2 * col, 2 * (col - HK // 2) + 1)
    return (row == source).astype(BF16)


def per_head(fn, x):
    heads = x.shape[1] // HK
    return jnp.concatenate([fn(x[:, h * HK : (h + 1) * HK]) for h in range(heads)], axis=1)


def turn(x, cosine, sine):
    a, b = x[:, : HK // 2], x[:, HK // 2 :]
    return jnp.concatenate([a * cosine - b * sine, b * cosine + a * sine], axis=1)


def on_device(
    layer_input,
    gain_attn,
    w_query,
    w_key,
    w_value,
    w_retgate,
    w_out,
    gain_mlp,
    w_gate,
    w_up,
    w_down,
    cotangent,
):
    data = ("dp", "ctx")
    rows, width = layer_input.shape
    n_tp, at_tp = lax.axis_size("tp"), lax.axis_index("tp")
    features = width * n_tp
    heads = w_query.shape[1] // HK
    units = w_gate.shape[1]
    key_scale = 1.0 / math.sqrt(HK)

    halves = halves_matrix()
    qk = heads * HK
    vw = heads * HV
    w_attn = jnp.concatenate(
        [
            per_head(lambda w: nn(w, halves).astype(BF16), w_query),
            per_head(lambda w: nn(w, halves).astype(BF16), w_key),
            w_value,
            w_retgate,
        ],
        axis=1,
    )
    attn_full = lax.all_gather(w_attn, data, axis=0, tiled=True)
    out_full = lax.all_gather(w_out, data, axis=0, tiled=True)
    mlp_full = lax.all_gather(jnp.concatenate([w_gate, w_up, w_down], axis=1), data, axis=0, tiled=True)
    gate_up_full, down_full = mlp_full[:, : 2 * units], mlp_full[:, 2 * units :]

    gains = small_gather(jnp.stack([gain_attn, gain_mlp]), "tp")

    def normed_full(own, gain_all):
        blocks = line_gather(own, "tp")
        squares = sum(jnp.sum(jnp.square(b.astype(F32)), axis=1, keepdims=True) for b in blocks)
        scale = lax.rsqrt(squares / features + EPSILON)
        done = []
        for k, b in enumerate(blocks):
            gain = lax.dynamic_slice(gain_all, (0, ((at_tp - k) % n_tp) * width), (1, width))
            done.append((b.astype(F32) * scale * gain).astype(BF16))
        return place(done, "tp", BF16), scale

    log_gamma = jnp.log1p(-jnp.exp2(-5.0 - (at_tp * heads + jnp.arange(heads)).astype(F32)))
    log_block = rows * log_gamma
    positions = lax.axis_index("ctx") * rows + jnp.arange(rows)
    frequencies = jnp.exp(-math.log(10000.0) * jnp.linspace(0.0, 1.0, HK // 2, dtype=F32))
    angles = positions.astype(F32)[:, None] * frequencies[None, :]
    cosine, sine = jnp.cos(angles), jnp.sin(angles)
    steps = jnp.arange(rows).astype(F32)
    half_way = rows // 2
    grow = [jnp.exp((steps - half_way) * log_gamma[h]) for h in range(heads)]
    fall = [jnp.exp((half_way - steps) * log_gamma[h]) for h in range(heads)]
    head_decay = [jnp.exp(steps * log_gamma[h])[:, None] for h in range(heads)]
    tail_decay = [jnp.exp((rows - steps) * log_gamma[h])[:, None] for h in range(heads)]
    causal = lax.broadcasted_iota(jnp.int32, (rows, rows), 0) >= lax.broadcasted_iota(jnp.int32, (rows, rows), 1)

    def decayed(scores, h):
        return jnp.where(causal, scores * grow[h][:, None] * fall[h][None, :], 0.0).astype(BF16)

    normed, scale_attn = normed_full(layer_input, gains[0:1])
    qk_pre = nn(normed, attn_full[:, : 2 * qk])
    value_rows = nn(normed, attn_full[:, 2 * qk : 2 * qk + vw]).astype(BF16)
    gate_pre = nn(normed, attn_full[:, 2 * qk + vw :])
    q, k, v, keyed = [], [], [], []
    for h in range(heads):
        q.append(turn(qk_pre[:, h * HK : (h + 1) * HK], cosine, sine).astype(BF16))
        k.append((turn(qk_pre[:, qk + h * HK : qk + (h + 1) * HK], cosine, sine) * key_scale).astype(BF16))
        v.append(value_rows[:, h * HV : (h + 1) * HV])
        keyed.append((k[h].astype(F32) * tail_decay[h]).astype(BF16))
    local_state = jnp.stack([tn(keyed[h], v[h]) for h in range(heads)])
    state_in = states_before(local_state, log_block, "ctx").astype(BF16)
    weights = [decayed(nt(q[h], k[h]), h) for h in range(heads)]
    retained = [nn(weights[h], v[h]) + nn(q[h], state_in[h]) * head_decay[h] for h in range(heads)]
    ret_scale = [lax.rsqrt(jnp.mean(jnp.square(r), axis=1, keepdims=True) + EPSILON) for r in retained]
    gate_h = [gate_pre[:, h * HV : (h + 1) * HV] for h in range(heads)]
    gated = jnp.concatenate(
        [(jax.nn.silu(gate_h[h]) * (retained[h] * ret_scale[h])).astype(BF16) for h in range(heads)], axis=1
    )
    x_own = layer_input.astype(F32)
    middle = x_own + line_scatter(nt(gated, out_full).astype(BF16), "tp")

    grad_full = place(line_gather(cotangent, "tp"), "tp", BF16)
    normed_mlp, scale_mlp = normed_full(middle.astype(BF16), gains[1:2])
    gate_up = nn(normed_mlp, gate_up_full)
    gate_act, up_act = gate_up[:, :units], gate_up[:, units:]
    grad_hidden = nn(grad_full, down_full)
    cdf = 0.5 * (1.0 + lax.erf(gate_act * math.sqrt(0.5)))
    gelu = gate_act * cdf
    density = jnp.exp(-0.5 * gate_act * gate_act) * (1.0 / math.sqrt(2.0 * math.pi))
    hidden = (gelu * up_act).astype(BF16)
    grad_gate_act = (grad_hidden * up_act * (cdf + gate_act * density)).astype(BF16)
    grad_up_act = (grad_hidden * gelu).astype(BF16)
    inner_mlp = jnp.sum(grad_gate_act.astype(F32) * gate_act + grad_up_act.astype(F32) * up_act, axis=1)
    grad_acts = jnp.concatenate([grad_gate_act, grad_up_act], axis=1)
    mlp_out = line_scatter(nt(hidden, down_full).astype(BF16), "tp")
    layer_output = (middle + mlp_out).astype(BF16)
    grad_down = tn(grad_full, hidden).astype(BF16)
    grad_gate_up = tn(normed_mlp, grad_acts).astype(BF16)

    def norm_back(own, scale, gain, inner, partial):
        grad_normed = line_scatter(partial, "tp")
        hat = own * scale
        grad = scale * (grad_normed * gain[None, :] - hat * (inner[:, None] / features))
        return grad, jnp.sum(grad_normed * hat, axis=0)

    def row_total(inner):
        lanes = 128
        return small_sum(inner.reshape(rows // lanes, lanes), "tp").reshape(rows)

    grad_mid, gain_mlp_sum = norm_back(
        middle, scale_mlp, gain_mlp, row_total(inner_mlp), nt(grad_acts, gate_up_full).astype(BF16)
    )
    grad_middle = cotangent.astype(F32) + grad_mid

    grad_attn = place(line_gather(grad_middle.astype(BF16), "tp"), "tp", BF16)
    grad_gated = nn(grad_attn, out_full)
    grad_out = tn(grad_attn, gated).astype(BF16)
    g_gate, g_ret = [], []
    for h in range(heads):
        gg = grad_gated[:, h * HV : (h + 1) * HV]
        sig = jax.nn.sigmoid(gate_h[h])
        silu = gate_h[h] * sig
        grouped = retained[h] * ret_scale[h]
        g_gate.append((gg * grouped * (sig * (1.0 + gate_h[h] * (1.0 - sig)))).astype(BF16))
        g = gg * silu
        g_ret.append(
            (ret_scale[h] * (g - grouped * jnp.mean(g * grouped, axis=1, keepdims=True))).astype(BF16)
        )
    decayed_q = [(q[h].astype(F32) * head_decay[h]).astype(BF16) for h in range(heads)]
    partial_state = jnp.stack([tn(decayed_q[h], g_ret[h]) for h in range(heads)])
    state_grad = states_after(partial_state, log_block, "ctx").astype(BF16)
    g_q, g_k, g_v = [], [], []
    inner_attn = 0.0
    for h in range(heads):
        g_scores = decayed(nt(g_ret[h], v[h]), h)
        gv = (tn(weights[h], g_ret[h]) + nn(keyed[h], state_grad[h])).astype(BF16)
        gk = tn(g_scores, q[h]) + nt(v[h], state_grad[h]) * tail_decay[h]
        gq = nn(g_scores, k[h]) + nt(g_ret[h], state_in[h]) * head_decay[h]
        inner_attn = (
            inner_attn
            + jnp.sum(gq * q[h].astype(F32) + gk * k[h].astype(F32), axis=1)
            + jnp.sum(gv.astype(F32) * v[h].astype(F32) + g_gate[h].astype(F32) * gate_h[h], axis=1)
        )
        g_q.append(turn(gq, cosine, -sine).astype(BF16))
        g_k.append((turn(gk, cosine, -sine) * key_scale).astype(BF16))
        g_v.append(gv)
    grads_attn = jnp.concatenate(g_q + g_k + g_v + g_gate, axis=1)
    grad_input_norm, gain_attn_sum = norm_back(
        x_own, scale_attn, gain_attn, row_total(inner_attn), nt(grads_attn, attn_full).astype(BF16)
    )
    grad_attn_w = tn(normed, grads_attn).astype(BF16)
    grad_input = (grad_middle + grad_input_norm).astype(BF16)

    def shard(grad):
        return lax.psum_scatter(grad, data, scatter_dimension=0, tiled=True)

    s_down = shard(grad_down).astype(F32)
    s_gate_up = shard(grad_gate_up).astype(F32)
    s_out = shard(grad_out).astype(F32)
    s_attn = shard(grad_attn_w)
    s_query = per_head(lambda g: nt(g, halves), s_attn[:, :qk])
    s_key = per_head(lambda g: nt(g, halves), s_attn[:, qk : 2 * qk])
    s_value = s_attn[:, 2 * qk : 2 * qk + vw].astype(F32)
    s_retgate = s_attn[:, 2 * qk + vw :].astype(F32)
    gain_sums = swap_sum(swap_sum(jnp.stack([gain_attn_sum, gain_mlp_sum]), "ctx"), "dp")
    return (
        layer_output,
        grad_input,
        gain_sums[0],
        s_query,
        s_key,
        s_value,
        s_retgate,
        s_out,
        gain_sums[1],
        s_gate_up[:, :units],
        s_gate_up[:, units:],
        s_down,
    )


def solution(mesh):
    tokens = P(("dp", "ctx"), "tp")
    gain = P("tp")
    weight = P(("dp", "ctx"), "tp")
    return jax.shard_map(
        on_device,
        mesh=mesh,
        in_specs=(tokens, gain, weight, weight, weight, weight, weight, gain, weight, weight, weight, tokens),
        out_specs=(tokens, tokens, gain, weight, weight, weight, weight, weight, gain, weight, weight, weight),
        check_vma=False,
    )
```

```python
import math

import jax
import jax.numpy as jnp
from jax import lax
from jax.experimental import pallas as pl
from jax.experimental.pallas import tpu as pltpu
from jax.sharding import PartitionSpec as P


HK = 256
HV = 512
EPSILON = 1e-06
BLOCK = 256
F32 = jnp.float32
BF16 = jnp.bfloat16


def nn(a, b):
    return lax.dot_general(a, b, (((1,), (0,)), ((), ())), preferred_element_type=F32)


def tn(a, b):
    return lax.dot_general(a, b, (((0,), (0,)), ((), ())), preferred_element_type=F32)


def nt(a, b):
    return lax.dot_general(a, b, (((1,), (1,)), ((), ())), preferred_element_type=F32)


def right(lo, hi):
    return [(i, i + 1) for i in range(lo, hi)]


def left(lo, hi):
    return [(i, i - 1) for i in range(hi, lo, -1)]


def line_gather(x, axis):
    n, i = lax.axis_size(axis), lax.axis_index(axis)
    rights, lefts = [x], [x]
    for k in range(1, n):
        r_pairs = right(k - 1, n - 1)
        l_pairs = left(0, n - k)
        if 2 * k > n + 1:
            both = lax.ppermute(jnp.where(i >= k - 1, rights[-1], lefts[-1]), axis, r_pairs + l_pairs)
            rights.append(both)
            lefts.append(both)
        else:
            rights.append(lax.ppermute(rights[-1], axis, r_pairs))
            lefts.append(lax.ppermute(lefts[-1], axis, l_pairs))
    return [x] + [jnp.where(i >= k, rights[k], lefts[n - k]) for k in range(1, n)]


def place(blocks, axis, dtype):
    n, i = lax.axis_size(axis), lax.axis_index(axis)
    rows, width = blocks[0].shape
    full = jnp.zeros((rows, n * width), dtype)
    for k, block in enumerate(blocks):
        at = ((i - k) % n) * width
        full = lax.dynamic_update_slice(full, block.astype(dtype), (0, at))
    return full


def line_scatter(parts, axis):
    n, i = lax.axis_size(axis), lax.axis_index(axis)
    width = parts.shape[1] // n

    def block(j):
        return lax.dynamic_slice(parts, (0, jnp.clip(j, 0, n - 1) * width), (parts.shape[0], width))

    from_left = from_right = None
    early = []
    for k in range(1, n):
        r_pairs = right(0, k)
        l_pairs = left(n - 1 - k, n - 1)
        if 2 * k < n - 1:
            data = block(jnp.where(i < k, i + n - k, i - n + k))
            if from_left is not None:
                data = (data.astype(F32) + jnp.where(i < k, from_left, from_right).astype(F32)).astype(BF16)
            from_left = from_right = lax.ppermute(data, axis, r_pairs + l_pairs)
            from_left = jnp.where(i <= k, from_left, jnp.zeros_like(from_left))
            from_right = jnp.where(i >= n - 1 - k, from_right, jnp.zeros_like(from_right))
        else:
            r_data, l_data = block(i + n - k), block(i - n + k)
            if from_left is not None:
                r_data = (r_data.astype(F32) + from_left.astype(F32)).astype(BF16)
                l_data = (l_data.astype(F32) + from_right.astype(F32)).astype(BF16)
            from_left = lax.ppermute(r_data, axis, r_pairs)
            from_right = lax.ppermute(l_data, axis, l_pairs)
        if k < n - 1:
            early.append((from_left, from_right))
    return block(i).astype(F32) + from_left.astype(F32) + from_right.astype(F32), early


def small_gather(x, axis):
    n = lax.axis_size(axis)
    blocks = [x] + [lax.ppermute(x, axis, [(j, (j + s) % n) for j in range(n)]) for s in range(1, n)]
    return place(blocks, axis, x.dtype)


def swap_sum(x, axis):
    n = lax.axis_size(axis)
    g = 1
    while g < n:
        x = x + lax.ppermute(x, axis, [(j, j ^ g) for j in range(n)])
        g *= 2
    return x


def states_before(local, log_block, axis):
    n, b = lax.axis_size(axis), lax.axis_index(axis)
    total, prefix, g = local, jnp.zeros_like(local), 1
    while g < n:
        got = lax.ppermute(total.astype(BF16), axis, [(j, j ^ g) for j in range(n)]).astype(F32)
        upper = (b // g) % 2 == 1
        mine = jnp.exp((b % g).astype(F32) * log_block)[:, None, None]
        whole = jnp.exp(g * log_block)[:, None, None]
        prefix = jnp.where(upper, prefix + mine * got, prefix)
        total = jnp.where(upper, whole * got + total, whole * total + got)
        g *= 2
    return prefix


def states_after(local, log_block, axis):
    first = None
    n, b = lax.axis_size(axis), lax.axis_index(axis)
    total, suffix, g = local, jnp.zeros_like(local), 1
    while g < n:
        got = lax.ppermute(total.astype(BF16), axis, [(j, j ^ g) for j in range(n)]).astype(F32)
        first = got if first is None else first
        upper = (b // g) % 2 == 1
        mine = jnp.exp((g - 1 - b % g).astype(F32) * log_block)[:, None, None]
        whole = jnp.exp(g * log_block)[:, None, None]
        suffix = jnp.where(upper, suffix, suffix + mine * got)
        total = jnp.where(upper, got + whole * total, total + whole * got)
        g *= 2
    return suffix, first


def pair_swap(x):
    lane = lax.broadcasted_iota(jnp.int32, x.shape, 1)
    width = x.shape[1]
    return jnp.where(lane % 2 == 0, pltpu.roll(x, width - 1, 1), pltpu.roll(x, 1, 1))


def project_kernel(heads, x_ref, w_ref, cos_ref, sin_ref, q_ref, k_ref):
    out = nn(x_ref[...], w_ref[...])
    c, s = cos_ref[...], sin_ref[...]
    for h in range(2 * heads):
        one = out[:, h * HK : (h + 1) * HK]
        turned = one * c + pair_swap(one) * s
        if h < heads:
            q_ref[:, h * HK : (h + 1) * HK] = turned.astype(BF16)
        else:
            k_ref[:, (h - heads) * HK : (h - heads + 1) * HK] = (turned * (1.0 / math.sqrt(HK))).astype(BF16)


def project(x, w, heads, cosine, sine):
    rows, features = x.shape
    out = pl.BlockSpec((BLOCK, heads * HK), lambda r: (r, 0))
    table = pl.BlockSpec((BLOCK, HK), lambda r: (r, 0))
    return pl.pallas_call(
        lambda *refs: project_kernel(heads, *refs),
        grid=(rows // BLOCK,),
        in_specs=[
            pl.BlockSpec((BLOCK, features), lambda r: (r, 0)),
            pl.BlockSpec((features, 2 * heads * HK), lambda r: (0, 0)),
            table,
            table,
        ],
        out_specs=[out, out],
        out_shape=[jax.ShapeDtypeStruct((rows, heads * HK), BF16)] * 2,
        cost_estimate=pl.CostEstimate(
            flops=4 * rows * features * heads * HK,
            bytes_accessed=2 * rows * features + 4 * features * heads * HK + 4 * rows * heads * HK,
            transcendentals=0,
        ),
        name="project",
    )(x, w, cosine, sine)


def decay_vectors(log_gamma):
    down = lax.broadcasted_iota(jnp.int32, (BLOCK, 1), 0).astype(F32)
    across = lax.broadcasted_iota(jnp.int32, (1, BLOCK), 1).astype(F32)
    return jnp.exp(down * log_gamma), jnp.exp(-across * log_gamma)


def block_decay(scores, r, j, log_gamma, down, across):
    out = scores * (down * jnp.exp(log_gamma * (BLOCK * (r - j)))) * across
    if r == j:
        n = lax.broadcasted_iota(jnp.int32, scores.shape, 0)
        m = lax.broadcasted_iota(jnp.int32, scores.shape, 1)
        out = jnp.where(n >= m, out, 0.0)
    return out.astype(BF16)


def cut(r):
    return slice(r * BLOCK, (r + 1) * BLOCK)


def forward_kernel(first, count, lg_ref, q_ref, k_ref, v_ref, gate_ref, state_ref, gated_ref, ret_ref):
    log_gamma = lg_ref[pl.program_id(0)]
    down, across = decay_vectors(log_gamma)
    state = state_ref[0]
    for at in range(count):
        r = first + at
        q = q_ref[cut(at), :]
        ret = nn(q, state) * (down * jnp.exp(log_gamma * (BLOCK * r)))
        for j in range(r + 1):
            weights = block_decay(nt(q, k_ref[cut(j), :]), r, j, log_gamma, down, across)
            ret = ret + nn(weights, v_ref[cut(j), :])
        ret_ref[cut(at), :] = ret
        scale = lax.rsqrt(jnp.mean(ret * ret, axis=1, keepdims=True) + EPSILON)
        gate = gate_ref[cut(at), :]
        gated_ref[cut(at), :] = (gate / (1.0 + jnp.exp(-gate)) * (ret * scale)).astype(BF16)


def retention_forward(part, parts, log_gamma, q, k, v, gate, state):
    rows = q.shape[0]
    heads = q.shape[1] // HK
    own = rows // parts
    seen = own * (part + 1)
    count = own // BLOCK
    pairs = sum(part * count + at + 1 for at in range(count))
    flops = heads * (pairs * 2 * BLOCK * BLOCK * (HK + HV) + 2 * own * HK * HV)
    return pl.pallas_call(
        lambda *refs: forward_kernel(part * count, count, *refs),
        grid=(heads,),
        in_specs=[
            pl.BlockSpec(memory_space=pltpu.SMEM),
            pl.BlockSpec((own, HK), lambda h: (part, h)),
            pl.BlockSpec((seen, HK), lambda h: (0, h)),
            pl.BlockSpec((seen, HV), lambda h: (0, h)),
            pl.BlockSpec((own, HV), lambda h: (part, h)),
            pl.BlockSpec((1, HK, HV), lambda h: (h, 0, 0)),
        ],
        out_specs=[pl.BlockSpec((own, HV), lambda h: (0, h)), pl.BlockSpec((own, HV), lambda h: (0, h))],
        out_shape=[
            jax.ShapeDtypeStruct((own, heads * HV), BF16),
            jax.ShapeDtypeStruct((own, heads * HV), F32),
        ],
        cost_estimate=pl.CostEstimate(flops=flops, bytes_accessed=16 * own * heads * HV, transcendentals=own * heads * HV),
        name="retention_forward",
    )(log_gamma, q, k, v, gate, state)


def gate_backward_kernel(first, count, lg_ref, q_ref, grad_ref, gate_ref, ret_ref, g_gate_ref, g_ret_ref, state_ref, inner_ref):
    log_gamma = lg_ref[pl.program_id(0)]
    down, _ = decay_vectors(log_gamma)
    state = None
    for at in range(count):
        r = first + at
        ret = ret_ref[cut(at), :]
        gate = gate_ref[cut(at), :]
        grad = grad_ref[cut(at), :]
        scale = lax.rsqrt(jnp.mean(ret * ret, axis=1, keepdims=True) + EPSILON)
        grouped = ret * scale
        sig = 1.0 / (1.0 + jnp.exp(-gate))
        g_gate = (grad * grouped * (sig * (1.0 + gate * (1.0 - sig)))).astype(BF16)
        g = grad * (gate * sig)
        g_ret = (scale * (g - grouped * jnp.mean(g * grouped, axis=1, keepdims=True))).astype(BF16)
        g_gate_ref[cut(at), :] = g_gate
        g_ret_ref[cut(at), :] = g_ret
        inner_ref[0, cut(at), :] = jnp.sum(g_gate.astype(F32) * gate, axis=1, keepdims=True)
        q = (q_ref[cut(at), :].astype(F32) * (down * jnp.exp(log_gamma * (BLOCK * r)))).astype(BF16)
        add = tn(q, g_ret)
        state = add if state is None else state + add
    state_ref[0] = state


def gate_backward(part, parts, log_gamma, q, grad, gate, ret):
    rows = q.shape[0]
    heads = q.shape[1] // HK
    own = rows // parts
    count = own // BLOCK
    return pl.pallas_call(
        lambda *refs: gate_backward_kernel(part * count, count, *refs),
        grid=(heads,),
        in_specs=[
            pl.BlockSpec(memory_space=pltpu.SMEM),
            pl.BlockSpec((own, HK), lambda h: (part, h)),
            pl.BlockSpec((own, HV), lambda h: (0, h)),
            pl.BlockSpec((own, HV), lambda h: (part, h)),
            pl.BlockSpec((own, HV), lambda h: (0, h)),
        ],
        out_specs=[
            pl.BlockSpec((own, HV), lambda h: (0, h)),
            pl.BlockSpec((own, HV), lambda h: (0, h)),
            pl.BlockSpec((1, HK, HV), lambda h: (h, 0, 0)),
            pl.BlockSpec((1, own, 1), lambda h: (h, 0, 0)),
        ],
        out_shape=[
            jax.ShapeDtypeStruct((own, heads * HV), BF16),
            jax.ShapeDtypeStruct((own, heads * HV), BF16),
            jax.ShapeDtypeStruct((heads, HK, HV), F32),
            jax.ShapeDtypeStruct((heads, own, 1), F32),
        ],
        cost_estimate=pl.CostEstimate(
            flops=heads * 2 * own * HK * HV, bytes_accessed=16 * own * heads * HV, transcendentals=own * heads * HV
        ),
        name="gate_backward",
    )(log_gamma, q, grad, gate, ret)


def backward_kernel(parts, per, lg_ref, q_ref, k_ref, v_ref, state_in_ref, state_grad_ref, cos_ref, sin_ref, *refs):
    g_refs, (g_q_ref, g_k_ref, g_v_ref, inner_ref, acc_k, acc_v) = refs[:parts], refs[parts:]
    log_gamma = lg_ref[pl.program_id(0)]
    down, across = decay_vectors(log_gamma)
    state_in, state_grad = state_in_ref[0], state_grad_ref[0]
    key_scale = 1.0 / math.sqrt(HK)
    total = parts * per

    def put(ref, r, x, factor):
        turned = x * cos_ref[cut(r), :] - pair_swap(x) * sin_ref[cut(r), :]
        ref[cut(r), :] = (turned * factor).astype(BF16)

    for r in range(total):
        g = g_refs[r // per][cut(r % per), :]
        q, k, v = q_ref[cut(r), :], k_ref[cut(r), :], v_ref[cut(r), :]
        tail = down_tail(log_gamma, total * BLOCK - r * BLOCK)
        acc_v[cut(r), :] = nn((k.astype(F32) * tail).astype(BF16), state_grad)
        acc_k[cut(r), :] = nt(v, state_grad) * tail
        g_q = nt(g, state_in) * (down * jnp.exp(log_gamma * (BLOCK * r)))
        for j in range(r + 1):
            kj, vj = k_ref[cut(j), :], v_ref[cut(j), :]
            weights = block_decay(nt(q, kj), r, j, log_gamma, down, across)
            g_scores = block_decay(nt(g, vj), r, j, log_gamma, down, across)
            acc_v[cut(j), :] += tn(weights, g)
            acc_k[cut(j), :] += tn(g_scores, q)
            g_q = g_q + nn(g_scores, kj)
        inner_ref[0, cut(r), :] = jnp.sum(g_q * q.astype(F32), axis=1, keepdims=True)
        put(g_q_ref, r, g_q, 1.0)
    for r in range(total):
        g_k = acc_k[cut(r), :]
        g_v = acc_v[cut(r), :].astype(BF16)
        g_v_ref[cut(r), :] = g_v
        inner_ref[0, cut(r), :] += jnp.sum(g_k * k_ref[cut(r), :].astype(F32), axis=1, keepdims=True) + jnp.sum(
            g_v.astype(F32) * v_ref[cut(r), :].astype(F32), axis=1, keepdims=True
        )
        put(g_k_ref, r, g_k, key_scale)


def down_tail(log_gamma, start):
    m = lax.broadcasted_iota(jnp.int32, (BLOCK, 1), 0).astype(F32)
    return jnp.exp((start - m) * log_gamma)


def retention_backward(log_gamma, q, k, v, state_in, state_grad, cosine, sine, g_ret):
    rows = q.shape[0]
    heads = q.shape[1] // HK
    parts = len(g_ret)
    own = rows // parts
    blocks = rows // BLOCK
    pairs = blocks * (blocks + 1) // 2
    flops = heads * 2 * (pairs * BLOCK * BLOCK * (3 * HK + 2 * HV) + 3 * rows * HK * HV)
    head_keys = pl.BlockSpec((rows, HK), lambda h: (0, h))
    head_values = pl.BlockSpec((rows, HV), lambda h: (0, h))
    head_state = pl.BlockSpec((1, HK, HV), lambda h: (h, 0, 0))
    table = pl.BlockSpec((rows, HK), lambda h: (0, 0))
    return pl.pallas_call(
        lambda *refs: backward_kernel(parts, own // BLOCK, *refs),
        grid=(heads,),
        in_specs=[
            pl.BlockSpec(memory_space=pltpu.SMEM),
            head_keys,
            head_keys,
            head_values,
            head_state,
            head_state,
            table,
            table,
            *[pl.BlockSpec((own, HV), lambda h: (0, h))] * parts,
        ],
        out_specs=[head_keys, head_keys, head_values, pl.BlockSpec((1, rows, 1), lambda h: (h, 0, 0))],
        out_shape=[
            jax.ShapeDtypeStruct((rows, heads * HK), BF16),
            jax.ShapeDtypeStruct((rows, heads * HK), BF16),
            jax.ShapeDtypeStruct((rows, heads * HV), BF16),
            jax.ShapeDtypeStruct((heads, rows, 1), F32),
        ],
        scratch_shapes=[pltpu.VMEM((rows, HK), F32), pltpu.VMEM((rows, HV), F32)],
        cost_estimate=pl.CostEstimate(flops=flops, bytes_accessed=16 * rows * heads * HK, transcendentals=0),
        name="retention_backward",
    )(log_gamma, q, k, v, state_in, state_grad, cosine, sine, *g_ret)


def after(x, *before):
    return lax.optimization_barrier((x, *before))[0]


def on_device(
    layer_input,
    gain_attn,
    w_query,
    w_key,
    w_value,
    w_retgate,
    w_out,
    gain_mlp,
    w_gate,
    w_up,
    w_down,
    cotangent,
):
    data = ("dp", "ctx")
    rows, width = layer_input.shape
    n_tp, at_tp = lax.axis_size("tp"), lax.axis_index("tp")
    features = width * n_tp
    heads = w_query.shape[1] // HK
    units = w_gate.shape[1]

    parts = 2
    own = rows // parts
    cuts = [slice(c * own, (c + 1) * own) for c in range(parts)]

    qk = heads * HK
    vw = heads * HV
    attn_shard = jnp.concatenate([w_query, w_key, w_value, w_retgate, w_out], axis=1)
    attn_full = lax.all_gather(attn_shard, data, axis=0, tiled=True)
    in_full, out_full = attn_full[:, : 2 * qk + 2 * vw], attn_full[:, 2 * qk + 2 * vw :]

    gains = small_gather(jnp.stack([gain_attn, gain_mlp]), "tp")

    def normed_full(blocks, gain_all):
        squares = sum(jnp.sum(jnp.square(b.astype(F32)), axis=1, keepdims=True) for b in blocks)
        scale = lax.rsqrt(squares / features + EPSILON)
        done = []
        for k, b in enumerate(blocks):
            gain = lax.dynamic_slice(gain_all, (0, ((at_tp - k) % n_tp) * width), (1, width))
            done.append((b.astype(F32) * scale * gain).astype(BF16))
        return place(done, "tp", BF16), scale

    log_gamma = jnp.log1p(-jnp.exp2(-5.0 - (at_tp * heads + jnp.arange(heads)).astype(F32)))
    log_block = rows * log_gamma
    positions = lax.axis_index("ctx") * rows + jnp.arange(rows)
    frequencies = jnp.exp(-math.log(10000.0) * jnp.linspace(0.0, 1.0, HK // 2, dtype=F32))
    angles = positions.astype(F32)[:, None] * frequencies[None, :]
    cosine = jnp.repeat(jnp.cos(angles), 2, axis=1)
    sine = jnp.stack([-jnp.sin(angles), jnp.sin(angles)], axis=2).reshape(rows, HK)
    steps = jnp.arange(rows).astype(F32)
    tail_decay = [jnp.exp((rows - steps) * log_gamma[h])[:, None] for h in range(heads)]

    x_blocks = line_gather(layer_input, "tp")
    normed, scale_attn = normed_full(x_blocks, gains[0:1])
    grad_full = lax.all_gather(after(cotangent, x_blocks[1]), "tp", axis=1, tiled=True)
    mlp_shard = jnp.concatenate([after(w_gate, normed), w_up, w_down], axis=1)
    mlp_full = lax.all_gather(mlp_shard, data, axis=0, tiled=True)
    gate_up_full, down_full = mlp_full[:, : 2 * units], mlp_full[:, 2 * units :]
    q, k = project(normed, attn_full, heads, cosine, sine)
    v = nn(normed, in_full[:, 2 * qk : 2 * qk + vw]).astype(BF16)
    keyed = [
        (k[:, h * HK : (h + 1) * HK].astype(F32) * tail_decay[h]).astype(BF16) for h in range(heads)
    ]
    local_state = jnp.stack([tn(keyed[h], v[:, h * HV : (h + 1) * HV]) for h in range(heads)])
    gate_pre = nn(after(normed, local_state), in_full[:, 2 * qk + vw :])
    state_in = states_before(local_state, log_block, "ctx").astype(BF16)
    gated, retained = [], []
    for c in range(parts):
        one, other = retention_forward(c, parts, log_gamma, q, k, v, gate_pre, state_in)
        gated.append(one)
        retained.append(other)

    x_own = layer_input.astype(F32)
    middle, normed_mlp, scale_mlp, hidden, grad_acts, inner_mlp, grad_middle, grad_attn = ([] for _ in range(8))
    gain_mlp_sum = 0.0

    def norm_back(own_rows, scale, gain, inner, partial):
        grad_normed, _ = line_scatter(partial, "tp")
        hat = own_rows * scale
        grad = scale * (grad_normed * gain[None, :] - hat * (inner[:, None] / features))
        return grad, jnp.sum(grad_normed * hat, axis=0)

    def row_total(inner):
        lanes = 128
        return swap_sum(inner.reshape(-1, lanes), "tp").reshape(-1)

    branch = [line_scatter(nt(gated[c], out_full).astype(BF16), "tp")[0] for c in range(parts)]
    for c in range(parts):
        middle.append(x_own[cuts[c]] + branch[c])
        blocks = line_gather(middle[c].astype(BF16), "tp")
        one, other = normed_full(blocks, gains[1:2])
        normed_mlp.append(one)
        scale_mlp.append(other)
    for c in range(parts):
        gate_up = nn(normed_mlp[c], gate_up_full)
        gate_act, up_act = gate_up[:, :units], gate_up[:, units:]
        grad_hidden = nn(grad_full[cuts[c]], down_full)
        cdf = 0.5 * (1.0 + lax.erf(gate_act * math.sqrt(0.5)))
        gelu = gate_act * cdf
        density = jnp.exp(-0.5 * gate_act * gate_act) * (1.0 / math.sqrt(2.0 * math.pi))
        hidden.append((gelu * up_act).astype(BF16))
        grad_gate_act = (grad_hidden * up_act * (cdf + gate_act * density)).astype(BF16)
        grad_up_act = (grad_hidden * gelu).astype(BF16)
        inner_mlp.append(
            jnp.sum(grad_gate_act.astype(F32) * gate_act + grad_up_act.astype(F32) * up_act, axis=1)
        )
        grad_acts.append(jnp.concatenate([grad_gate_act, grad_up_act], axis=1))
    for c in range(parts):
        back = nt(grad_acts[c], gate_up_full).astype(BF16)
        grad_mid, gain_sum = norm_back(middle[c], scale_mlp[c], gain_mlp, row_total(inner_mlp[c]), back)
        gain_mlp_sum = gain_mlp_sum + gain_sum
        grad_middle.append(cotangent[cuts[c]].astype(F32) + grad_mid)
    for c in range(parts):
        grad_attn.append(place(line_gather(grad_middle[c].astype(BF16), "tp"), "tp", BF16))
    hidden_all = jnp.concatenate(hidden)
    mlp_parts = nt(hidden_all, down_full).astype(BF16)
    grad_down = tn(grad_full, hidden_all).astype(BF16)
    grad_gate_up = tn(jnp.concatenate(normed_mlp), jnp.concatenate(grad_acts)).astype(BF16)

    grad_attn[0] = after(grad_attn[0], grad_gate_up, grad_down, mlp_parts)
    mlp_parts = after(mlp_parts, grad_attn[0])
    mlp_out, mlp_early = line_scatter(mlp_parts, "tp")
    layer_output = (jnp.concatenate(middle) + mlp_out).astype(BF16)
    g_gate, g_ret = [], []
    partial_state = 0.0
    inner_attn = []
    for c in range(parts):
        grad_gated = nn(grad_attn[c], out_full)
        gg, gr, ps, inner = gate_backward(c, parts, log_gamma, q, grad_gated, gate_pre, retained[c])
        g_gate.append(gg)
        g_ret.append(gr)
        partial_state = partial_state + ps
        inner_attn.append(jnp.sum(inner[:, :, 0], axis=0))
    state_grad, got = states_after(partial_state, log_block, "ctx")
    state_grad = state_grad.astype(BF16)
    g_gate = jnp.concatenate(g_gate)
    grad_out = tn(after(jnp.concatenate(grad_attn), got, mlp_early[0]), jnp.concatenate(gated)).astype(BF16)
    grad_retgate = tn(normed, after(g_gate, got, mlp_early[0])).astype(BF16)
    g_q, g_k, g_v, inner = retention_backward(
        log_gamma, q, k, v, state_in, after(state_grad, grad_out, grad_retgate, mlp_early[-1]), cosine, sine, g_ret
    )
    inner_attn = jnp.concatenate(inner_attn) + jnp.sum(inner[:, :, 0], axis=0)
    grads_attn = jnp.concatenate([g_q, g_k, g_v, g_gate], axis=1)
    back = []
    for c in range(parts):
        back.append(nt(after(grads_attn[cuts[c]], *back), in_full).astype(BF16))
    grad_qkv_w = tn(normed, after(grads_attn[:, : 2 * qk + vw], *back, mlp_out)).astype(BF16)
    inner_attn = row_total(inner_attn)
    grad_input, gain_attn_sum = [], 0.0
    for c in range(parts):
        grad_in, gain_sum = norm_back(x_own[cuts[c]], scale_attn[cuts[c]], gain_attn, inner_attn[cuts[c]], back[c])
        grad_input.append((grad_middle[c] + grad_in).astype(BF16))
        gain_attn_sum = gain_attn_sum + gain_sum
    grad_input = jnp.concatenate(grad_input)

    def shard(grad):
        return lax.psum_scatter(grad, data, scatter_dimension=0, tiled=True).astype(F32)

    s_down = shard(grad_down)
    s_gate_up = shard(grad_gate_up)
    s_out = shard(grad_out)
    s_retgate = shard(grad_retgate)
    s_qkv = shard(grad_qkv_w)
    s_query, s_key, s_value = s_qkv[:, :qk], s_qkv[:, qk : 2 * qk], s_qkv[:, 2 * qk :]
    gain_sums = swap_sum(swap_sum(jnp.stack([gain_attn_sum, gain_mlp_sum]), "ctx"), "dp")
    return (
        layer_output,
        grad_input,
        gain_sums[0],
        s_query,
        s_key,
        s_value,
        s_retgate,
        s_out,
        gain_sums[1],
        s_gate_up[:, :units],
        s_gate_up[:, units:],
        s_down,
    )


def solution(mesh):
    tokens = P(("dp", "ctx"), "tp")
    gain = P("tp")
    weight = P(("dp", "ctx"), "tp")

    return jax.shard_map(
        on_device,
        mesh=mesh,
        in_specs=(tokens, gain, weight, weight, weight, weight, weight, gain, weight, weight, weight, tokens),
        out_specs=(tokens, tokens, gain, weight, weight, weight, weight, weight, gain, weight, weight, weight),
        check_vma=False,
    )
```

```python
import math

import jax
import jax.numpy as jnp
from jax import lax
from jax.experimental import pallas as pl
from jax.experimental.pallas import tpu as pltpu
from jax.sharding import PartitionSpec as P


HK = 256
HV = 512
EPSILON = 1e-06
BLOCK = 256
F32 = jnp.float32
BF16 = jnp.bfloat16


def nn(a, b):
    return lax.dot_general(a, b, (((1,), (0,)), ((), ())), preferred_element_type=F32)


def tn(a, b):
    return lax.dot_general(a, b, (((0,), (0,)), ((), ())), preferred_element_type=F32)


def nt(a, b):
    return lax.dot_general(a, b, (((1,), (1,)), ((), ())), preferred_element_type=F32)


def after(x, *before):
    return lax.optimization_barrier((x, *before))[0]


def right(lo, hi):
    return [(i, i + 1) for i in range(lo, hi)]


def left(lo, hi):
    return [(i, i - 1) for i in range(hi, lo, -1)]


def line_gather(x, axis, before=()):
    n, i = lax.axis_size(axis), lax.axis_index(axis)
    rights, lefts = [x], [x]
    for k in range(1, n):
        r_pairs = right(k - 1, n - 1)
        l_pairs = left(0, n - k)
        if k == 2 and before:
            rights[-1] = after(rights[-1], *before)
        if 2 * k > n + 1:
            both = lax.ppermute(jnp.where(i >= k - 1, rights[-1], lefts[-1]), axis, r_pairs + l_pairs)
            rights.append(both)
            lefts.append(both)
        else:
            rights.append(lax.ppermute(rights[-1], axis, r_pairs))
            lefts.append(lax.ppermute(lefts[-1], axis, l_pairs))
    return [(rights[k], lefts[n - k]) for k in range(1, n)]


def place(blocks, axis, dtype):
    n, i = lax.axis_size(axis), lax.axis_index(axis)
    rows, width = blocks[0].shape
    full = jnp.zeros((rows, n * width), dtype)
    for k, block in enumerate(blocks):
        at = ((i - k) % n) * width
        full = lax.dynamic_update_slice(full, block.astype(dtype), (0, at))
    return full


def line_scatter(parts, axis):
    n, i = lax.axis_size(axis), lax.axis_index(axis)
    width = parts.shape[1] // n

    def block(j):
        return lax.dynamic_slice(parts, (0, jnp.clip(j, 0, n - 1) * width), (parts.shape[0], width))

    from_left = from_right = None
    early = []
    for k in range(1, n):
        r_pairs = right(0, k)
        l_pairs = left(n - 1 - k, n - 1)
        if 2 * k < n - 1:
            data = block(jnp.where(i < k, i + n - k, i - n + k))
            if from_left is not None:
                data = (data.astype(F32) + jnp.where(i < k, from_left, from_right).astype(F32)).astype(BF16)
            from_left = from_right = lax.ppermute(data, axis, r_pairs + l_pairs)
            from_left = jnp.where(i <= k, from_left, jnp.zeros_like(from_left))
            from_right = jnp.where(i >= n - 1 - k, from_right, jnp.zeros_like(from_right))
        else:
            r_data, l_data = block(i + n - k), block(i - n + k)
            if from_left is not None:
                r_data = (r_data.astype(F32) + from_left.astype(F32)).astype(BF16)
                l_data = (l_data.astype(F32) + from_right.astype(F32)).astype(BF16)
            from_left = lax.ppermute(r_data, axis, r_pairs)
            from_right = lax.ppermute(l_data, axis, l_pairs)
        if k < n - 1:
            early.append((from_left, from_right))
    return block(i).astype(F32) + from_left.astype(F32) + from_right.astype(F32), early


def small_gather(x, axis):
    n = lax.axis_size(axis)
    blocks = [x] + [lax.ppermute(x, axis, [(j, (j + s) % n) for j in range(n)]) for s in range(1, n)]
    return place(blocks, axis, x.dtype)


def swap_sum(x, axis):
    n = lax.axis_size(axis)
    g = 1
    while g < n:
        x = x + lax.ppermute(x, axis, [(j, j ^ g) for j in range(n)])
        g *= 2
    return x


def states_before(local, log_block, axis):
    n, b = lax.axis_size(axis), lax.axis_index(axis)
    total, prefix, g = local, jnp.zeros_like(local), 1
    while g < n:
        got = lax.ppermute(total.astype(BF16), axis, [(j, j ^ g) for j in range(n)]).astype(F32)
        upper = (b // g) % 2 == 1
        mine = jnp.exp((b % g).astype(F32) * log_block)[:, None, None]
        whole = jnp.exp(g * log_block)[:, None, None]
        prefix = jnp.where(upper, prefix + mine * got, prefix)
        total = jnp.where(upper, whole * got + total, whole * total + got)
        g *= 2
    return prefix


def states_after(local, log_block, axis):
    first = None
    n, b = lax.axis_size(axis), lax.axis_index(axis)
    total, suffix, g = local, jnp.zeros_like(local), 1
    while g < n:
        got = lax.ppermute(total.astype(BF16), axis, [(j, j ^ g) for j in range(n)]).astype(F32)
        first = got if first is None else first
        upper = (b // g) % 2 == 1
        mine = jnp.exp((g - 1 - b % g).astype(F32) * log_block)[:, None, None]
        whole = jnp.exp(g * log_block)[:, None, None]
        suffix = jnp.where(upper, suffix, suffix + mine * got)
        total = jnp.where(upper, got + whole * total, total + whole * got)
        g *= 2
    return suffix, first


def pair_swap(x):
    lane = lax.broadcasted_iota(jnp.int32, x.shape, 1)
    width = x.shape[1]
    return jnp.where(lane % 2 == 0, pltpu.roll(x, width - 1, 1), pltpu.roll(x, 1, 1))


def side_by_side(*arrays):
    rows = arrays[0].shape[0]
    widths = [a.shape[1] for a in arrays]

    def kernel(*refs):
        parts, out, sems = refs[:-2], refs[-2], refs[-1]
        copies, column = [], 0
        for i, width in enumerate(widths):
            copies.append(pltpu.make_async_copy(parts[i], out.at[:, column : column + width], sems.at[i]))
            column += width
        for copy in copies:
            copy.start()
        for copy in copies:
            copy.wait()

    return pl.pallas_call(
        kernel,
        in_specs=[pl.BlockSpec(memory_space=pl.ANY)] * len(arrays),
        out_specs=pl.BlockSpec(memory_space=pl.ANY),
        out_shape=jax.ShapeDtypeStruct((rows, sum(widths)), arrays[0].dtype),
        scratch_shapes=[pltpu.SemaphoreType.DMA((len(arrays),))],
        cost_estimate=pl.CostEstimate(flops=0, bytes_accessed=4 * rows * sum(widths), transcendentals=0),
        name="side_by_side",
    )(*arrays)


def fill_normed(at, refs, gain_ref, full_ref):
    n = len(refs) // 2 + 1
    width = refs[0].shape[1]
    blocks = [refs[0][...].astype(F32)]
    for k in range(1, n):
        blocks.append(jnp.where(at >= k, refs[2 * k - 1][...], refs[2 * k][...]).astype(F32))
    squares = sum(jnp.sum(b * b, axis=1, keepdims=True) for b in blocks)
    scale = lax.rsqrt(squares / (n * width) + EPSILON)
    for k, b in enumerate(blocks):
        where = pl.ds(pl.multiple_of(((at + n - k) % n) * width, width), width)
        full_ref[:, where] = (b * scale * gain_ref[:, where]).astype(BF16)
    return scale


def flat(x, pairs):
    return [x] + [p for pair in pairs for p in pair]


def project_kernel(heads, count, at_ref, lg_ref, gain_ref, w_ref, cos_ref, sin_ref, *refs):
    blocks, (full_ref, scale_ref, q_ref, k_ref, v_ref, state_ref) = refs[:count], refs[count:]
    step = pl.program_id(0)
    rows = pl.num_programs(0) * BLOCK
    scale_ref[...] = fill_normed(at_ref[0], blocks, gain_ref, full_ref)
    x = full_ref[...]
    qk = heads * HK
    c, s = cos_ref[...], sin_ref[...]
    k_out = nn(x, w_ref[:, qk : 2 * qk])
    v_out = nn(x, w_ref[:, 2 * qk :]).astype(BF16)
    q_out = nn(x, w_ref[:, :qk])
    v_ref[...] = v_out
    m = lax.broadcasted_iota(jnp.int32, (BLOCK, 1), 0) + step * BLOCK
    for h in range(heads):
        at = slice(h * HK, (h + 1) * HK)
        one = k_out[:, at]
        key = ((one * c + pair_swap(one) * s) * (1.0 / math.sqrt(HK))).astype(BF16)
        k_ref[:, at] = key
        tail = jnp.exp((rows - m).astype(F32) * lg_ref[h])
        add = tn((key.astype(F32) * tail).astype(BF16), v_out[:, h * HV : (h + 1) * HV])

        @pl.when(step == 0)
        def _(h=h, add=add):
            state_ref[h] = add

        @pl.when(step > 0)
        def _(h=h, add=add):
            state_ref[h] += add

        one = q_out[:, at]
        q_ref[:, at] = (one * c + pair_swap(one) * s).astype(BF16)


def project(at, log_gamma, gain, w, x, pairs, heads, cosine, sine):
    rows, width = x.shape
    features = w.shape[0]
    outs = 2 * heads * HK + heads * HV
    blocks = flat(x, pairs)

    def by_rows(columns):
        return pl.BlockSpec((BLOCK, columns), lambda r: (r, 0))

    return pl.pallas_call(
        lambda *refs: project_kernel(heads, len(blocks), *refs),
        grid=(rows // BLOCK,),
        in_specs=[
            pl.BlockSpec(memory_space=pltpu.SMEM),
            pl.BlockSpec(memory_space=pltpu.SMEM),
            pl.BlockSpec((1, features), lambda r: (0, 0)),
            pl.BlockSpec((features, outs), lambda r: (0, 0)),
            by_rows(HK),
            by_rows(HK),
            *[by_rows(width)] * len(blocks),
        ],
        out_specs=[
            by_rows(features),
            by_rows(1),
            by_rows(heads * HK),
            by_rows(heads * HK),
            by_rows(heads * HV),
            pl.BlockSpec((heads, HK, HV), lambda r: (0, 0, 0)),
        ],
        out_shape=[
            jax.ShapeDtypeStruct((rows, features), BF16),
            jax.ShapeDtypeStruct((rows, 1), F32),
            jax.ShapeDtypeStruct((rows, heads * HK), BF16),
            jax.ShapeDtypeStruct((rows, heads * HK), BF16),
            jax.ShapeDtypeStruct((rows, heads * HV), BF16),
            jax.ShapeDtypeStruct((heads, HK, HV), F32),
        ],
        cost_estimate=pl.CostEstimate(
            flops=2 * rows * features * outs, bytes_accessed=2 * features * outs + 12 * rows * features, transcendentals=0
        ),
        name="project",
    )(at, log_gamma, gain, w, cosine, sine, *blocks)


def product_kernel(x_ref, w_ref, out_ref):
    out_ref[...] = nn(x_ref[...], w_ref[...])


def product(x, w, at, columns):
    rows, inner = x.shape
    return pl.pallas_call(
        product_kernel,
        grid=(rows // BLOCK,),
        in_specs=[
            pl.BlockSpec((BLOCK, inner), lambda r: (r, 0)),
            pl.BlockSpec((inner, columns), lambda r: (0, at)),
        ],
        out_specs=pl.BlockSpec((BLOCK, columns), lambda r: (r, 0)),
        out_shape=jax.ShapeDtypeStruct((rows, columns), F32),
        cost_estimate=pl.CostEstimate(
            flops=2 * rows * inner * columns, bytes_accessed=2 * inner * columns + 8 * rows * columns, transcendentals=0
        ),
        name="product",
    )(x, w)


def mlp_kernel(units, count, at_ref, gain_ref, w_ref, grad_ref, *refs):
    blocks, (full_ref, hidden_ref, acts_ref, scale_ref, inner_ref, back_ref) = refs[:count], refs[-6:]
    scale_ref[...] = fill_normed(at_ref[0], blocks, gain_ref, full_ref)
    x = full_ref[...]
    gate = nn(x, w_ref[:, :units])
    up = nn(x, w_ref[:, units : 2 * units])
    grad = nn(grad_ref[...], w_ref[:, 2 * units :])
    cdf = 0.5 * (1.0 + lax.erf(gate * math.sqrt(0.5)))
    gelu = gate * cdf
    density = jnp.exp(-0.5 * gate * gate) * (1.0 / math.sqrt(2.0 * math.pi))
    hidden_ref[...] = (gelu * up).astype(BF16)
    g_gate = (grad * up * (cdf + gate * density)).astype(BF16)
    g_up = (grad * gelu).astype(BF16)
    acts_ref[:, :units] = g_gate
    acts_ref[:, units:] = g_up
    inner_ref[...] = jnp.sum(g_gate.astype(F32) * gate + g_up.astype(F32) * up, axis=1, keepdims=True)
    back_ref[...] = (nt(g_gate, w_ref[:, :units]) + nt(g_up, w_ref[:, units : 2 * units])).astype(BF16)


def mlp(at, gain, w, part, grad, x, pairs, shared):
    rows, width = x.shape
    features = w.shape[0]
    units = w.shape[1] // 3
    blocks = flat(x, pairs)
    steps = rows // BLOCK
    total = grad.shape[0]

    def by_rows(columns):
        return pl.BlockSpec((BLOCK, columns), lambda r: (r, 0))

    def own_rows(columns):
        return pl.BlockSpec((BLOCK, columns), lambda r: (part * steps + r, 0))

    return pl.pallas_call(
        lambda *refs: mlp_kernel(units, len(blocks), *refs),
        grid=(steps,),
        in_specs=[
            pl.BlockSpec(memory_space=pltpu.SMEM),
            pl.BlockSpec((1, features), lambda r: (0, 0)),
            pl.BlockSpec((features, 3 * units), lambda r: (0, 0)),
            own_rows(features),
            *[by_rows(width)] * len(blocks),
            *[pl.BlockSpec(memory_space=pl.ANY)] * len(shared),
        ],
        out_specs=[own_rows(features), own_rows(units), own_rows(2 * units), by_rows(1), by_rows(1), by_rows(features)],
        out_shape=[
            jax.ShapeDtypeStruct((total, features), BF16),
            jax.ShapeDtypeStruct((total, units), BF16),
            jax.ShapeDtypeStruct((total, 2 * units), BF16),
            jax.ShapeDtypeStruct((rows, 1), F32),
            jax.ShapeDtypeStruct((rows, 1), F32),
            jax.ShapeDtypeStruct((rows, features), BF16),
        ],
        input_output_aliases={4 + len(blocks) + i: i for i in range(len(shared))},
        cost_estimate=pl.CostEstimate(
            flops=10 * rows * features * units,
            bytes_accessed=6 * features * units + 14 * rows * features,
            transcendentals=2 * rows * units,
        ),
        name="mlp",
    )(at, gain, w, grad, *blocks, *shared)


def decay_vectors(log_gamma):
    down = lax.broadcasted_iota(jnp.int32, (BLOCK, 1), 0).astype(F32)
    across = lax.broadcasted_iota(jnp.int32, (1, BLOCK), 1).astype(F32)
    return jnp.exp(down * log_gamma), jnp.exp(-across * log_gamma)


def block_decay(scores, r, j, log_gamma, down, across):
    out = scores * (down * jnp.exp(log_gamma * (BLOCK * (r - j)))) * across
    if r == j:
        n = lax.broadcasted_iota(jnp.int32, scores.shape, 0)
        m = lax.broadcasted_iota(jnp.int32, scores.shape, 1)
        out = jnp.where(n >= m, out, 0.0)
    return out.astype(BF16)


def cut(r):
    return slice(r * BLOCK, (r + 1) * BLOCK)


def forward_kernel(first, count, lg_ref, q_ref, k_ref, v_ref, gate_ref, state_ref, w_ref, *refs):
    gated_ref, ret_ref, out_ref, acc_ref = refs[-4:]
    head = pl.program_id(0)
    log_gamma = lg_ref[head]
    down, across = decay_vectors(log_gamma)
    state = state_ref[0]
    for at in range(count):
        r = first + at
        q = q_ref[cut(at), :]
        ret = nn(q, state) * (down * jnp.exp(log_gamma * (BLOCK * r)))
        for j in range(r + 1):
            weights = block_decay(nt(q, k_ref[cut(j), :]), r, j, log_gamma, down, across)
            ret = ret + nn(weights, v_ref[cut(j), :])
        ret_ref[cut(at), :] = ret
        scale = lax.rsqrt(jnp.mean(ret * ret, axis=1, keepdims=True) + EPSILON)
        gate = gate_ref[cut(at), :]
        gated = (gate / (1.0 + jnp.exp(-gate)) * (ret * scale)).astype(BF16)
        gated_ref[cut(at), :] = gated
        out = nt(gated, w_ref[...])

        @pl.when(head == 0)
        def _(at=at, out=out):
            acc_ref[cut(at), :] = out

        @pl.when(head > 0)
        def _(at=at, out=out):
            acc_ref[cut(at), :] += out

        @pl.when(head == pl.num_programs(0) - 1)
        def _(at=at):
            out_ref[cut(at), :] = acc_ref[cut(at), :].astype(BF16)


def retention_forward(part, parts, log_gamma, q, k, v, gate, state, w, first_column, shared):
    rows = q.shape[0]
    heads = q.shape[1] // HK
    features = w.shape[0]
    own = rows // parts
    seen = own * (part + 1)
    count = own // BLOCK
    pairs = sum(part * count + at + 1 for at in range(count))
    flops = heads * (pairs * 2 * BLOCK * BLOCK * (HK + HV) + 2 * own * HK * HV + 2 * own * HV * features)
    head_out = pl.BlockSpec((own, HV), lambda h: (part, h))
    return pl.pallas_call(
        lambda *refs: forward_kernel(part * count, count, *refs),
        grid=(heads,),
        in_specs=[
            pl.BlockSpec(memory_space=pltpu.SMEM),
            pl.BlockSpec((own, HK), lambda h: (part, h)),
            pl.BlockSpec((seen, HK), lambda h: (0, h)),
            pl.BlockSpec((seen, HV), lambda h: (0, h)),
            pl.BlockSpec((own, HV), lambda h: (part, h)),
            pl.BlockSpec((1, HK, HV), lambda h: (h, 0, 0)),
            pl.BlockSpec((features, HV), lambda h: (0, first_column // HV + h)),
            *[pl.BlockSpec(memory_space=pl.ANY)] * len(shared),
        ],
        out_specs=[head_out, head_out, pl.BlockSpec((own, features), lambda h: (0, 0))],
        input_output_aliases={7 + i: i for i in range(len(shared))},
        out_shape=[
            jax.ShapeDtypeStruct((rows, heads * HV), BF16),
            jax.ShapeDtypeStruct((rows, heads * HV), F32),
            jax.ShapeDtypeStruct((own, features), BF16),
        ],
        scratch_shapes=[pltpu.VMEM((own, features), F32)],
        cost_estimate=pl.CostEstimate(flops=flops, bytes_accessed=20 * own * heads * HV, transcendentals=own * heads * HV),
        name="retention_forward",
    )(log_gamma, q, k, v, gate, state, w, *shared)


def gate_backward_kernel(first, count, n_blocks, at_ref, lg_ref, q_ref, w_ref, gate_ref, ret_ref, *refs):
    blocks, (g_gate_ref, g_ret_ref, full_ref, state_ref, inner_ref) = refs[:n_blocks], refs[-5:]
    head = pl.program_id(0)
    log_gamma = lg_ref[head]
    down, _ = decay_vectors(log_gamma)
    n = n_blocks // 2 + 1
    width = blocks[0].shape[1]
    here = at_ref[0]
    state = None
    for at in range(count):
        r = first + at

        @pl.when(head == 0)
        def _(at=at):
            for k in range(n):
                block = blocks[0][cut(at), :]
                if k:
                    block = jnp.where(here >= k, blocks[2 * k - 1][cut(at), :], blocks[2 * k][cut(at), :])
                where = pl.ds(pl.multiple_of(((here + n - k) % n) * width, width), width)
                full_ref[cut(at), where] = block

        grad = nn(full_ref[cut(at), :], w_ref[...])
        ret = ret_ref[cut(at), :]
        gate = gate_ref[cut(at), :]
        scale = lax.rsqrt(jnp.mean(ret * ret, axis=1, keepdims=True) + EPSILON)
        grouped = ret * scale
        sig = 1.0 / (1.0 + jnp.exp(-gate))
        g_gate = (grad * grouped * (sig * (1.0 + gate * (1.0 - sig)))).astype(BF16)
        g = grad * (gate * sig)
        g_ret = (scale * (g - grouped * jnp.mean(g * grouped, axis=1, keepdims=True))).astype(BF16)
        g_gate_ref[cut(at), :] = g_gate
        g_ret_ref[cut(at), :] = g_ret
        inner_ref[0, cut(at), :] = jnp.sum(g_gate.astype(F32) * gate, axis=1, keepdims=True)
        q = (q_ref[cut(at), :].astype(F32) * (down * jnp.exp(log_gamma * (BLOCK * r)))).astype(BF16)
        add = tn(q, g_ret)
        state = add if state is None else state + add
    state_ref[0] = state


def gate_backward(part, parts, here, log_gamma, q, w, first_column, gate, ret, x, pairs, shared):
    rows = q.shape[0]
    heads = q.shape[1] // HK
    features = w.shape[0]
    own = rows // parts
    count = own // BLOCK
    blocks = flat(x, pairs)
    head_out = pl.BlockSpec((own, HV), lambda h: (part, h))
    return pl.pallas_call(
        lambda *refs: gate_backward_kernel(part * count, count, len(blocks), *refs),
        grid=(heads,),
        in_specs=[
            pl.BlockSpec(memory_space=pltpu.SMEM),
            pl.BlockSpec(memory_space=pltpu.SMEM),
            pl.BlockSpec((own, HK), lambda h: (part, h)),
            pl.BlockSpec((features, HV), lambda h: (0, first_column // HV + h)),
            head_out,
            head_out,
            *[pl.BlockSpec((own, x.shape[1]), lambda h: (0, 0))] * len(blocks),
            *[pl.BlockSpec(memory_space=pl.ANY)] * len(shared),
        ],
        out_specs=[
            head_out,
            head_out,
            pl.BlockSpec((own, features), lambda h: (part, 0)),
            pl.BlockSpec((1, HK, HV), lambda h: (h, 0, 0)),
            pl.BlockSpec((1, own, 1), lambda h: (h, 0, 0)),
        ],
        input_output_aliases={6 + len(blocks) + i: i for i in range(len(shared))},
        out_shape=[
            jax.ShapeDtypeStruct((rows, heads * HV), BF16),
            jax.ShapeDtypeStruct((rows, heads * HV), BF16),
            jax.ShapeDtypeStruct((rows, features), BF16),
            jax.ShapeDtypeStruct((heads, HK, HV), F32),
            jax.ShapeDtypeStruct((heads, own, 1), F32),
        ],
        cost_estimate=pl.CostEstimate(
            flops=heads * 2 * own * HV * (HK + features),
            bytes_accessed=16 * own * heads * HV,
            transcendentals=own * heads * HV,
        ),
        name="gate_backward",
    )(here, log_gamma, q, w, gate, ret, *blocks, *shared)


def backward_kernel(total, lg_ref, q_ref, k_ref, v_ref, state_in_ref, state_grad_ref, cos_ref, sin_ref, *refs):
    g_ref, gate_ref, all_ref, inner_ref, acc_k, acc_v, g_q_ref, g_k_ref, g_v_ref, sems = refs
    head, heads = pl.program_id(0), pl.num_programs(0)
    log_gamma = lg_ref[head]
    down, across = decay_vectors(log_gamma)
    state_in, state_grad = state_in_ref[0], state_grad_ref[0]
    key_scale = 1.0 / math.sqrt(HK)

    def send(ref, column, width, i):
        target = all_ref.at[:, pl.ds(pl.multiple_of(column, HK), width)]
        return pltpu.make_async_copy(ref, target, sems.at[i])

    gates = send(gate_ref, heads * (2 * HK + HV) + head * HV, HV, 0)
    gates.start()

    def put(ref, r, x, factor):
        turned = x * cos_ref[cut(r), :] - pair_swap(x) * sin_ref[cut(r), :]
        ref[cut(r), :] = (turned * factor).astype(BF16)

    for r in range(total):
        g = g_ref[cut(r), :]
        q, k, v = q_ref[cut(r), :], k_ref[cut(r), :], v_ref[cut(r), :]
        tail = down_tail(log_gamma, total * BLOCK - r * BLOCK)
        acc_v[cut(r), :] = nn((k.astype(F32) * tail).astype(BF16), state_grad)
        acc_k[cut(r), :] = nt(v, state_grad) * tail
        g_q = nt(g, state_in) * (down * jnp.exp(log_gamma * (BLOCK * r)))
        for j in range(r + 1):
            kj, vj = k_ref[cut(j), :], v_ref[cut(j), :]
            weights = block_decay(nt(q, kj), r, j, log_gamma, down, across)
            g_scores = block_decay(nt(g, vj), r, j, log_gamma, down, across)
            acc_v[cut(j), :] += tn(weights, g)
            acc_k[cut(j), :] += tn(g_scores, q)
            g_q = g_q + nn(g_scores, kj)
        inner_ref[0, cut(r), :] = jnp.sum(g_q * q.astype(F32), axis=1, keepdims=True)
        put(g_q_ref, r, g_q, 1.0)
    for r in range(total):
        g_k = acc_k[cut(r), :]
        g_v = acc_v[cut(r), :].astype(BF16)
        g_v_ref[cut(r), :] = g_v
        inner_ref[0, cut(r), :] += jnp.sum(g_k * k_ref[cut(r), :].astype(F32), axis=1, keepdims=True) + jnp.sum(
            g_v.astype(F32) * v_ref[cut(r), :].astype(F32), axis=1, keepdims=True
        )
        put(g_k_ref, r, g_k, key_scale)
    copies = [
        send(g_q_ref, head * HK, HK, 1),
        send(g_k_ref, (heads + head) * HK, HK, 2),
        send(g_v_ref, 2 * heads * HK + head * HV, HV, 3),
    ]
    for copy in copies:
        copy.start()
    for copy in [gates] + copies:
        copy.wait()


def down_tail(log_gamma, start):
    m = lax.broadcasted_iota(jnp.int32, (BLOCK, 1), 0).astype(F32)
    return jnp.exp((start - m) * log_gamma)


def retention_backward(log_gamma, q, k, v, state_in, state_grad, cosine, sine, g_ret, g_gate):
    rows = q.shape[0]
    heads = q.shape[1] // HK
    blocks = rows // BLOCK
    pairs = blocks * (blocks + 1) // 2
    flops = heads * 2 * (pairs * BLOCK * BLOCK * (3 * HK + 2 * HV) + 3 * rows * HK * HV)
    head_keys = pl.BlockSpec((rows, HK), lambda h: (0, h))
    head_values = pl.BlockSpec((rows, HV), lambda h: (0, h))
    head_state = pl.BlockSpec((1, HK, HV), lambda h: (h, 0, 0))
    table = pl.BlockSpec((rows, HK), lambda h: (0, 0))
    return pl.pallas_call(
        lambda *refs: backward_kernel(blocks, *refs),
        grid=(heads,),
        in_specs=[
            pl.BlockSpec(memory_space=pltpu.SMEM),
            head_keys,
            head_keys,
            head_values,
            head_state,
            head_state,
            table,
            table,
            head_values,
            head_values,
        ],
        out_specs=[pl.BlockSpec(memory_space=pl.ANY), pl.BlockSpec((1, rows, 1), lambda h: (h, 0, 0))],
        out_shape=[
            jax.ShapeDtypeStruct((rows, heads * 2 * (HK + HV)), BF16),
            jax.ShapeDtypeStruct((heads, rows, 1), F32),
        ],
        scratch_shapes=[
            pltpu.VMEM((rows, HK), F32),
            pltpu.VMEM((rows, HV), F32),
            pltpu.VMEM((rows, HK), BF16),
            pltpu.VMEM((rows, HK), BF16),
            pltpu.VMEM((rows, HV), BF16),
            pltpu.SemaphoreType.DMA((4,)),
        ],
        cost_estimate=pl.CostEstimate(flops=flops, bytes_accessed=24 * rows * heads * HK, transcendentals=0),
        name="retention_backward",
    )(log_gamma, q, k, v, state_in, state_grad, cosine, sine, g_ret, g_gate)


def on_device(
    layer_input,
    gain_attn,
    w_query,
    w_key,
    w_value,
    w_retgate,
    w_out,
    gain_mlp,
    w_gate,
    w_up,
    w_down,
    cotangent,
):
    data = ("dp", "ctx")
    rows, width = layer_input.shape
    n_tp, at_tp = lax.axis_size("tp"), lax.axis_index("tp")
    features = width * n_tp
    heads = w_query.shape[1] // HK
    units = w_gate.shape[1]

    parts = 2
    own = rows // parts
    cuts = [slice(c * own, (c + 1) * own) for c in range(parts)]

    qk = heads * HK
    vw = heads * HV
    attn_shard = side_by_side(w_query, w_key, w_value, w_retgate, w_out)
    attn_full = lax.all_gather(attn_shard, data, axis=0, tiled=True)

    gains = small_gather(jnp.stack([gain_attn, gain_mlp]), "tp")

    log_gamma = jnp.log1p(-jnp.exp2(-5.0 - (at_tp * heads + jnp.arange(heads)).astype(F32)))
    log_block = rows * log_gamma
    positions = lax.axis_index("ctx") * rows + jnp.arange(rows)
    frequencies = jnp.exp(-math.log(10000.0) * jnp.linspace(0.0, 1.0, HK // 2, dtype=F32))
    angles = positions.astype(F32)[:, None] * jnp.repeat(frequencies, 2)[None, :]
    cosine = jnp.cos(angles)
    sine = jnp.sin(angles) * jnp.where(jnp.arange(HK) % 2 == 0, -1.0, 1.0)[None, :]
    here = at_tp.reshape(1)
    mlp_shard = side_by_side(w_gate, w_up, w_down)

    pairs = line_gather(layer_input, "tp", (cosine, sine, mlp_shard, log_gamma))
    normed, scale_attn, q, k, v, local_state = project(
        here, log_gamma, gains[0:1], attn_full, layer_input, pairs, heads, cosine, sine
    )
    grad_full = lax.all_gather(after(cotangent, pairs[0][0]), "tp", axis=1, tiled=True)
    mlp_full = lax.all_gather(after(mlp_shard, pairs[0][1]), data, axis=0, tiled=True)
    gate_pre = product(after(normed, local_state), attn_full, (2 * qk + vw) // vw, vw)
    state_in = states_before(local_state, log_block, "ctx").astype(BF16)
    heads_out, branch = [], []
    for c in range(parts):
        *heads_out, out = retention_forward(
            c, parts, log_gamma, q, k, v, gate_pre, state_in, attn_full, 2 * qk + 2 * vw, heads_out
        )
        branch.append(out)
    gated, retained = heads_out

    x_own = layer_input.astype(F32)
    middle, mid_pairs, scale_mlp, inner_mlp, back, grad_middle, grad_own, grad_pairs = ([] for _ in range(8))
    gain_mlp_sum = 0.0

    def norm_back(own_rows, scale, gain, inner, grad_normed):
        hat = own_rows * scale
        grad = scale * (grad_normed * gain[None, :] - hat * (inner[:, None] / features))
        return grad, jnp.sum(grad_normed * hat, axis=0)

    def row_total(inner):
        lanes = 128
        return swap_sum(inner.reshape(-1, lanes), "tp").reshape(-1)

    early = ()
    for c in range(parts):
        total, steps = line_scatter(after(branch[c], *early), "tp")
        early = steps[-1]
        if c:
            total = after(total, mid_pairs[c - 1][0][0])
        middle.append(x_own[cuts[c]] + total)
        mid_pairs.append(line_gather(middle[c].astype(BF16), "tp"))
    shared = []
    for c in range(parts):
        *results, scale, inner, out = mlp(
            here, gains[1:2], mlp_full, c, grad_full, middle[c].astype(BF16), mid_pairs[c], shared
        )
        shared = results
        scale_mlp.append(scale)
        inner_mlp.append(inner[:, 0])
        back.append(out)
    normed_mlp, hidden, grad_acts = shared
    early = ()
    for c in range(parts):
        inner = row_total(inner_mlp[c])
        total, steps = line_scatter(after(back[c], *early), "tp")
        early = steps[-1]
        if c:
            total = after(total, grad_pairs[c - 1][0][0])
        grad_mid, gain_sum = norm_back(middle[c], scale_mlp[c], gain_mlp, inner, total)
        gain_mlp_sum = gain_mlp_sum + gain_sum
        grad_middle.append(cotangent[cuts[c]].astype(F32) + grad_mid)
        grad_own.append(grad_middle[c].astype(BF16))
        grad_pairs.append(line_gather(grad_own[c], "tp"))
    grad_down = tn(grad_full, hidden).astype(BF16)
    grad_gate_up = tn(after(normed_mlp, grad_down), grad_acts).astype(BF16)
    mlp_parts = nt(hidden, mlp_full[:, 2 * units :]).astype(BF16)

    grad_own[0] = after(grad_own[0], grad_gate_up, grad_down, mlp_parts)
    mlp_out, _ = line_scatter(after(mlp_parts, grad_pairs[-1][0][0]), "tp")
    layer_output = (jnp.concatenate(middle) + mlp_out).astype(BF16)
    shared = []
    partial_state = 0.0
    inner_attn = []
    for c in range(parts):
        *shared, ps, inner = gate_backward(
            c,
            parts,
            here,
            log_gamma,
            q,
            attn_full,
            2 * qk + 2 * vw,
            gate_pre,
            retained,
            grad_own[c],
            grad_pairs[c],
            shared,
        )
        partial_state = partial_state + ps
        inner_attn.append(jnp.sum(inner[:, :, 0], axis=0))
    g_gate, g_ret, grad_attn = shared
    state_grad, got = states_after(partial_state, log_block, "ctx")
    state_grad = state_grad.astype(BF16)
    grad_out = tn(after(grad_attn, got), gated).astype(BF16)
    grad_retgate = tn(normed, after(g_gate, got)).astype(BF16)
    grads_attn, inner = retention_backward(
        log_gamma, q, k, v, state_in, after(state_grad, grad_out, grad_retgate), cosine, sine, g_ret, g_gate
    )
    inner_attn = jnp.concatenate(inner_attn) + jnp.sum(inner[:, :, 0], axis=0)
    in_full = attn_full[:, : 2 * qk + 2 * vw]
    back = []
    for c in range(parts):
        back.append(nt(after(grads_attn, *back)[cuts[c]], in_full).astype(BF16))
    grad_qkv_w = tn(normed, after(grads_attn, *back)[:, : 2 * qk + vw]).astype(BF16)
    inner_attn = row_total(inner_attn)
    grad_input, gain_attn_sum = [], 0.0
    early = ()
    for c in range(parts):
        total, steps = line_scatter(after(back[c], *early), "tp")
        early = steps[0]
        grad_in, gain_sum = norm_back(x_own[cuts[c]], scale_attn[cuts[c]], gain_attn, inner_attn[cuts[c]], total)
        grad_input.append((grad_middle[c] + grad_in).astype(BF16))
        gain_attn_sum = gain_attn_sum + gain_sum
    grad_input = jnp.concatenate(grad_input)

    def shard(grad):
        return lax.psum_scatter(grad, data, scatter_dimension=0, tiled=True).astype(F32)

    s_down = shard(grad_down)
    s_gate_up = shard(grad_gate_up)
    s_out = shard(grad_out)
    s_retgate = shard(grad_retgate)
    s_qkv = shard(grad_qkv_w)
    s_query, s_key, s_value = s_qkv[:, :qk], s_qkv[:, qk : 2 * qk], s_qkv[:, 2 * qk :]
    gain_sums = swap_sum(swap_sum(jnp.stack([gain_attn_sum, gain_mlp_sum]), "ctx"), "dp")
    return (
        layer_output,
        grad_input,
        gain_sums[0],
        s_query,
        s_key,
        s_value,
        s_retgate,
        s_out,
        gain_sums[1],
        s_gate_up[:, :units],
        s_gate_up[:, units:],
        s_down,
    )


def solution(mesh):
    tokens = P(("dp", "ctx"), "tp")
    gain = P("tp")
    weight = P(("dp", "ctx"), "tp")

    return jax.shard_map(
        on_device,
        mesh=mesh,
        in_specs=(tokens, gain, weight, weight, weight, weight, weight, gain, weight, weight, weight, tokens),
        out_specs=(tokens, tokens, gain, weight, weight, weight, weight, weight, gain, weight, weight, weight),
        check_vma=False,
    )
```

```python
import math

import jax
import jax.numpy as jnp
from jax import lax
from jax.experimental import pallas as pl
from jax.experimental.pallas import tpu as pltpu
from jax.sharding import PartitionSpec as P


HK = 256
HV = 512
EPSILON = 1e-06
BLOCK = 512
F32 = jnp.float32
BF16 = jnp.bfloat16


def nn(a, b):
    return lax.dot_general(a, b, (((1,), (0,)), ((), ())), preferred_element_type=F32)


def tn(a, b):
    return lax.dot_general(a, b, (((0,), (0,)), ((), ())), preferred_element_type=F32)


def nt(a, b):
    return lax.dot_general(a, b, (((1,), (1,)), ((), ())), preferred_element_type=F32)


def after(x, *before):
    return lax.optimization_barrier((x, *before))[0]


def right(lo, hi):
    return [(i, i + 1) for i in range(lo, hi)]


def left(lo, hi):
    return [(i, i - 1) for i in range(hi, lo, -1)]


def line_gather(x, axis, before=()):
    n, i = lax.axis_size(axis), lax.axis_index(axis)
    rights, lefts = [x], [x]
    for k in range(1, n):
        r_pairs = right(k - 1, n - 1)
        l_pairs = left(0, n - k)
        if k == 2 and before:
            rights[-1] = after(rights[-1], *before)
        if 2 * k > n + 1:
            both = lax.ppermute(jnp.where(i >= k - 1, rights[-1], lefts[-1]), axis, r_pairs + l_pairs)
            rights.append(both)
            lefts.append(both)
        else:
            rights.append(lax.ppermute(rights[-1], axis, r_pairs))
            lefts.append(lax.ppermute(lefts[-1], axis, l_pairs))
    return [(rights[k], lefts[n - k]) for k in range(1, n)]


def place(blocks, axis, dtype):
    n, i = lax.axis_size(axis), lax.axis_index(axis)
    rows, width = blocks[0].shape
    full = jnp.zeros((rows, n * width), dtype)
    for k, block in enumerate(blocks):
        at = ((i - k) % n) * width
        full = lax.dynamic_update_slice(full, block.astype(dtype), (0, at))
    return full


def line_scatter(parts, axis):
    n, i = lax.axis_size(axis), lax.axis_index(axis)
    width = parts.shape[1] // n

    def block(j):
        return lax.dynamic_slice(parts, (0, jnp.clip(j, 0, n - 1) * width), (parts.shape[0], width))

    from_left = from_right = None
    early = []
    for k in range(1, n):
        r_pairs = right(0, k)
        l_pairs = left(n - 1 - k, n - 1)
        if 2 * k < n - 1:
            data = block(jnp.where(i < k, i + n - k, i - n + k))
            if from_left is not None:
                data = (data.astype(F32) + jnp.where(i < k, from_left, from_right).astype(F32)).astype(BF16)
            from_left = from_right = lax.ppermute(data, axis, r_pairs + l_pairs)
            from_left = jnp.where(i <= k, from_left, jnp.zeros_like(from_left))
            from_right = jnp.where(i >= n - 1 - k, from_right, jnp.zeros_like(from_right))
        else:
            r_data, l_data = block(i + n - k), block(i - n + k)
            if from_left is not None:
                r_data = (r_data.astype(F32) + from_left.astype(F32)).astype(BF16)
                l_data = (l_data.astype(F32) + from_right.astype(F32)).astype(BF16)
            from_left = lax.ppermute(r_data, axis, r_pairs)
            from_right = lax.ppermute(l_data, axis, l_pairs)
        if k < n - 1:
            early.append((from_left, from_right))
    return block(i).astype(F32) + from_left.astype(F32) + from_right.astype(F32), early


def small_gather(x, axis):
    n = lax.axis_size(axis)
    blocks = [x] + [lax.ppermute(x, axis, [(j, (j + s) % n) for j in range(n)]) for s in range(1, n)]
    return place(blocks, axis, x.dtype)


def swap_sum(x, axis):
    n = lax.axis_size(axis)
    g = 1
    while g < n:
        x = x + lax.ppermute(x, axis, [(j, j ^ g) for j in range(n)])
        g *= 2
    return x


def states_before(local, log_block, axis):
    n, b = lax.axis_size(axis), lax.axis_index(axis)
    total, prefix, g = local, jnp.zeros_like(local), 1
    while g < n:
        got = lax.ppermute(total.astype(BF16), axis, [(j, j ^ g) for j in range(n)]).astype(F32)
        upper = (b // g) % 2 == 1
        mine = jnp.exp((b % g).astype(F32) * log_block)[:, None, None]
        whole = jnp.exp(g * log_block)[:, None, None]
        prefix = jnp.where(upper, prefix + mine * got, prefix)
        total = jnp.where(upper, whole * got + total, whole * total + got)
        g *= 2
    return prefix


def states_after(local, log_block, axis):
    first = None
    n, b = lax.axis_size(axis), lax.axis_index(axis)
    total, suffix, g = local, jnp.zeros_like(local), 1
    while g < n:
        got = lax.ppermute(total.astype(BF16), axis, [(j, j ^ g) for j in range(n)]).astype(F32)
        first = got if first is None else first
        upper = (b // g) % 2 == 1
        mine = jnp.exp((g - 1 - b % g).astype(F32) * log_block)[:, None, None]
        whole = jnp.exp(g * log_block)[:, None, None]
        suffix = jnp.where(upper, suffix, suffix + mine * got)
        total = jnp.where(upper, got + whole * total, total + whole * got)
        g *= 2
    return suffix, first


def pair_swap(x):
    lane = lax.broadcasted_iota(jnp.int32, x.shape, 1)
    width = x.shape[1]
    return jnp.where(lane % 2 == 0, pltpu.roll(x, width - 1, 1), pltpu.roll(x, 1, 1))


def side_by_side(*arrays):
    rows = arrays[0].shape[0]
    widths = [a.shape[1] for a in arrays]

    def kernel(*refs):
        column = 0
        for ref, width in zip(refs, widths):
            refs[-1][:, column : column + width] = ref[...]
            column += width

    block = min(rows, 64)
    return pl.pallas_call(
        kernel,
        grid=(rows // block,),
        in_specs=[pl.BlockSpec((block, width), lambda r: (r, 0)) for width in widths],
        out_specs=pl.BlockSpec((block, sum(widths)), lambda r: (r, 0)),
        out_shape=jax.ShapeDtypeStruct((rows, sum(widths)), arrays[0].dtype),
        cost_estimate=pl.CostEstimate(flops=0, bytes_accessed=4 * rows * sum(widths), transcendentals=0),
        name="side_by_side",
    )(*arrays)


def gathered(at, refs, k, rows=slice(None)):
    if k == 0:
        return refs[0][rows, :]
    return jnp.where(at >= k, refs[2 * k - 1][rows, :], refs[2 * k][rows, :])


def columns_of(at, n, k, width):
    return pl.ds(pl.multiple_of(((at + n - k) % n) * width, width), width)


def fill_normed(at, refs, gain_ref, full_ref):
    n = len(refs) // 2 + 1
    width = refs[0].shape[1]
    blocks = [gathered(at, refs, k).astype(F32) for k in range(n)]
    squares = sum(jnp.sum(b * b, axis=1, keepdims=True) for b in blocks)
    scale = lax.rsqrt(squares / (n * width) + EPSILON)
    for k, b in enumerate(blocks):
        where = columns_of(at, n, k, width)
        full_ref[:, where] = (b * scale * gain_ref[:, where]).astype(BF16)
    return scale


def flat(x, pairs):
    return [x] + [p for pair in pairs for p in pair]


def project_kernel(heads, count, at_ref, lg_ref, gain_ref, w_ref, cos_ref, sin_ref, *refs):
    blocks, (full_ref, scale_ref, q_ref, k_ref, v_ref, state_ref) = refs[:count], refs[count:]
    step = pl.program_id(0)
    rows = pl.num_programs(0) * BLOCK
    scale_ref[...] = fill_normed(at_ref[0], blocks, gain_ref, full_ref)
    x = full_ref[...]
    qk = heads * HK
    c, s = cos_ref[...], sin_ref[...]
    k_out = nn(x, w_ref[:, qk : 2 * qk])
    v_out = nn(x, w_ref[:, 2 * qk :]).astype(BF16)
    q_out = nn(x, w_ref[:, :qk])
    v_ref[...] = v_out
    m = lax.broadcasted_iota(jnp.int32, (BLOCK, 1), 0) + step * BLOCK
    for h in range(heads):
        at = slice(h * HK, (h + 1) * HK)
        one = k_out[:, at]
        key = ((one * c + pair_swap(one) * s) * (1.0 / math.sqrt(HK))).astype(BF16)
        k_ref[:, at] = key
        tail = jnp.exp((rows - m).astype(F32) * lg_ref[h])
        add = tn((key.astype(F32) * tail).astype(BF16), v_out[:, h * HV : (h + 1) * HV])

        @pl.when(step == 0)
        def _(h=h, add=add):
            state_ref[h] = add

        @pl.when(step > 0)
        def _(h=h, add=add):
            state_ref[h] += add

        one = q_out[:, at]
        q_ref[:, at] = (one * c + pair_swap(one) * s).astype(BF16)


def project(at, log_gamma, gain, w, x, pairs, heads, cosine, sine):
    rows, width = x.shape
    features = w.shape[0]
    outs = 2 * heads * HK + heads * HV
    blocks = flat(x, pairs)

    def by_rows(columns):
        return pl.BlockSpec((BLOCK, columns), lambda r: (r, 0))

    return pl.pallas_call(
        lambda *refs: project_kernel(heads, len(blocks), *refs),
        grid=(rows // BLOCK,),
        in_specs=[
            pl.BlockSpec(memory_space=pltpu.SMEM),
            pl.BlockSpec(memory_space=pltpu.SMEM),
            pl.BlockSpec((1, features), lambda r: (0, 0)),
            pl.BlockSpec((features, outs), lambda r: (0, 0)),
            by_rows(HK),
            by_rows(HK),
            *[by_rows(width)] * len(blocks),
        ],
        out_specs=[
            by_rows(features),
            by_rows(1),
            by_rows(heads * HK),
            by_rows(heads * HK),
            by_rows(heads * HV),
            pl.BlockSpec((heads, HK, HV), lambda r: (0, 0, 0)),
        ],
        out_shape=[
            jax.ShapeDtypeStruct((rows, features), BF16),
            jax.ShapeDtypeStruct((rows, 1), F32),
            jax.ShapeDtypeStruct((rows, heads * HK), BF16),
            jax.ShapeDtypeStruct((rows, heads * HK), BF16),
            jax.ShapeDtypeStruct((rows, heads * HV), BF16),
            jax.ShapeDtypeStruct((heads, HK, HV), F32),
        ],
        cost_estimate=pl.CostEstimate(
            flops=2 * rows * features * outs, bytes_accessed=2 * features * outs + 12 * rows * features, transcendentals=0
        ),
        name="project",
    )(at, log_gamma, gain, w, cosine, sine, *blocks)


def product_kernel(x_ref, w_ref, out_ref):
    out_ref[...] = nn(x_ref[...], w_ref[...])


def product(x, w, at, columns):
    rows, inner = x.shape
    return pl.pallas_call(
        product_kernel,
        grid=(rows // BLOCK,),
        in_specs=[
            pl.BlockSpec((BLOCK, inner), lambda r: (r, 0)),
            pl.BlockSpec((inner, columns), lambda r: (0, at)),
        ],
        out_specs=pl.BlockSpec((BLOCK, columns), lambda r: (r, 0)),
        out_shape=jax.ShapeDtypeStruct((rows, columns), F32),
        cost_estimate=pl.CostEstimate(
            flops=2 * rows * inner * columns, bytes_accessed=2 * inner * columns + 8 * rows * columns, transcendentals=0
        ),
        name="product",
    )(x, w)


def mlp_kernel(units, count, at_ref, gain_ref, w_ref, *refs):
    blocks, grads = refs[:count], refs[count : 2 * count]
    full_ref, hidden_ref, acts_ref, grad_ref, scale_ref, inner_ref, back_ref = refs[-7:]
    at, n = at_ref[0], count // 2 + 1
    scale_ref[...] = fill_normed(at, blocks, gain_ref, full_ref)
    for k in range(n):
        grad_ref[:, columns_of(at, n, k, grads[0].shape[1])] = gathered(at, grads, k)
    x = full_ref[...]
    gate = nn(x, w_ref[:, :units])
    up = nn(x, w_ref[:, units : 2 * units])
    grad = nn(grad_ref[...], w_ref[:, 2 * units :])
    cdf = 0.5 * (1.0 + lax.erf(gate * math.sqrt(0.5)))
    gelu = gate * cdf
    density = jnp.exp(-0.5 * gate * gate) * (1.0 / math.sqrt(2.0 * math.pi))
    hidden_ref[...] = (gelu * up).astype(BF16)
    g_gate = (grad * up * (cdf + gate * density)).astype(BF16)
    g_up = (grad * gelu).astype(BF16)
    acts_ref[:, :units] = g_gate
    acts_ref[:, units:] = g_up
    inner_ref[...] = jnp.sum(g_gate.astype(F32) * gate + g_up.astype(F32) * up, axis=1, keepdims=True)
    back_ref[...] = (nt(g_gate, w_ref[:, :units]) + nt(g_up, w_ref[:, units : 2 * units])).astype(BF16)


def mlp(at, gain, w, part, grads, x, pairs, shared):
    rows, width = x.shape
    features = w.shape[0]
    units = w.shape[1] // 3
    blocks = flat(x, pairs)
    steps = rows // BLOCK
    total = grads[0].shape[0]

    def by_rows(columns):
        return pl.BlockSpec((BLOCK, columns), lambda r: (r, 0))

    def own_rows(columns):
        return pl.BlockSpec((BLOCK, columns), lambda r: (part * steps + r, 0))

    return pl.pallas_call(
        lambda *refs: mlp_kernel(units, len(blocks), *refs),
        grid=(steps,),
        in_specs=[
            pl.BlockSpec(memory_space=pltpu.SMEM),
            pl.BlockSpec((1, features), lambda r: (0, 0)),
            pl.BlockSpec((features, 3 * units), lambda r: (0, 0)),
            *[by_rows(width)] * len(blocks),
            *[own_rows(width)] * len(grads),
            *[pl.BlockSpec(memory_space=pl.ANY)] * len(shared),
        ],
        out_specs=[
            own_rows(features),
            own_rows(units),
            own_rows(2 * units),
            own_rows(features),
            by_rows(1),
            by_rows(1),
            by_rows(features),
        ],
        out_shape=[
            jax.ShapeDtypeStruct((total, features), BF16),
            jax.ShapeDtypeStruct((total, units), BF16),
            jax.ShapeDtypeStruct((total, 2 * units), BF16),
            jax.ShapeDtypeStruct((total, features), BF16),
            jax.ShapeDtypeStruct((rows, 1), F32),
            jax.ShapeDtypeStruct((rows, 1), F32),
            jax.ShapeDtypeStruct((rows, features), BF16),
        ],
        input_output_aliases={3 + 2 * len(blocks) + i: i for i in range(len(shared))},
        cost_estimate=pl.CostEstimate(
            flops=10 * rows * features * units,
            bytes_accessed=6 * features * units + 14 * rows * features,
            transcendentals=2 * rows * units,
        ),
        name="mlp",
    )(at, gain, w, *blocks, *grads, *shared)


def decay_vectors(log_gamma):
    down = lax.broadcasted_iota(jnp.int32, (BLOCK, 1), 0).astype(F32)
    across = lax.broadcasted_iota(jnp.int32, (1, BLOCK), 1).astype(F32)
    return jnp.exp(down * log_gamma), jnp.exp(-across * log_gamma)


def block_decay(scores, r, j, log_gamma, down, across):
    out = scores * (down * jnp.exp(log_gamma * (BLOCK * (r - j)))) * across
    if r == j:
        n = lax.broadcasted_iota(jnp.int32, scores.shape, 0)
        m = lax.broadcasted_iota(jnp.int32, scores.shape, 1)
        out = jnp.where(n >= m, out, 0.0)
    return out.astype(BF16)


def cut(r):
    return slice(r * BLOCK, (r + 1) * BLOCK)


def forward_kernel(first, count, lg_ref, q_ref, k_ref, v_ref, gate_ref, state_ref, w_ref, *refs):
    gated_ref, ret_ref, out_ref, acc_ref = refs[-4:]
    head = pl.program_id(0)
    log_gamma = lg_ref[head]
    down, across = decay_vectors(log_gamma)
    state = state_ref[0]
    for at in range(count):
        r = first + at
        q = q_ref[cut(at), :]
        ret = nn(q, state) * (down * jnp.exp(log_gamma * (BLOCK * r)))
        for j in range(r + 1):
            weights = block_decay(nt(q, k_ref[cut(j), :]), r, j, log_gamma, down, across)
            ret = ret + nn(weights, v_ref[cut(j), :])
        ret_ref[cut(at), :] = ret
        scale = lax.rsqrt(jnp.mean(ret * ret, axis=1, keepdims=True) + EPSILON)
        gate = gate_ref[cut(at), :]
        gated = (gate / (1.0 + jnp.exp(-gate)) * (ret * scale)).astype(BF16)
        gated_ref[cut(at), :] = gated
        out = nt(gated, w_ref[...])

        @pl.when(head == 0)
        def _(at=at, out=out):
            acc_ref[cut(at), :] = out

        @pl.when(head > 0)
        def _(at=at, out=out):
            acc_ref[cut(at), :] += out

        @pl.when(head == pl.num_programs(0) - 1)
        def _(at=at):
            out_ref[cut(at), :] = acc_ref[cut(at), :].astype(BF16)


def retention_forward(part, parts, log_gamma, q, k, v, gate, state, w, first_column, shared):
    rows = q.shape[0]
    heads = q.shape[1] // HK
    features = w.shape[0]
    own = rows // parts
    seen = own * (part + 1)
    count = own // BLOCK
    pairs = sum(part * count + at + 1 for at in range(count))
    flops = heads * (pairs * 2 * BLOCK * BLOCK * (HK + HV) + 2 * own * HK * HV + 2 * own * HV * features)
    head_out = pl.BlockSpec((own, HV), lambda h: (part, h))
    return pl.pallas_call(
        lambda *refs: forward_kernel(part * count, count, *refs),
        grid=(heads,),
        in_specs=[
            pl.BlockSpec(memory_space=pltpu.SMEM),
            pl.BlockSpec((own, HK), lambda h: (part, h)),
            pl.BlockSpec((seen, HK), lambda h: (0, h)),
            pl.BlockSpec((seen, HV), lambda h: (0, h)),
            pl.BlockSpec((own, HV), lambda h: (part, h)),
            pl.BlockSpec((1, HK, HV), lambda h: (h, 0, 0)),
            pl.BlockSpec((features, HV), lambda h: (0, first_column // HV + h)),
            *[pl.BlockSpec(memory_space=pl.ANY)] * len(shared),
        ],
        out_specs=[head_out, head_out, pl.BlockSpec((own, features), lambda h: (0, 0))],
        input_output_aliases={7 + i: i for i in range(len(shared))},
        out_shape=[
            jax.ShapeDtypeStruct((rows, heads * HV), BF16),
            jax.ShapeDtypeStruct((rows, heads * HV), F32),
            jax.ShapeDtypeStruct((own, features), BF16),
        ],
        scratch_shapes=[pltpu.VMEM((own, features), F32)],
        cost_estimate=pl.CostEstimate(flops=flops, bytes_accessed=20 * own * heads * HV, transcendentals=own * heads * HV),
        name="retention_forward",
    )(log_gamma, q, k, v, gate, state, w, *shared)


def gate_backward_kernel(first, count, n_blocks, at_ref, lg_ref, q_ref, w_ref, gate_ref, ret_ref, *refs):
    blocks, (g_gate_ref, g_ret_ref, full_ref, state_ref, inner_ref) = refs[:n_blocks], refs[-5:]
    head = pl.program_id(0)
    log_gamma = lg_ref[head]
    down, _ = decay_vectors(log_gamma)
    n = n_blocks // 2 + 1
    width = blocks[0].shape[1]
    here = at_ref[0]
    state = None
    for at in range(count):
        r = first + at

        @pl.when(head == 0)
        def _(at=at):
            for k in range(n):
                full_ref[cut(at), columns_of(here, n, k, width)] = gathered(here, blocks, k, cut(at))

        grad = nn(full_ref[cut(at), :], w_ref[...])
        ret = ret_ref[cut(at), :]
        gate = gate_ref[cut(at), :]
        scale = lax.rsqrt(jnp.mean(ret * ret, axis=1, keepdims=True) + EPSILON)
        grouped = ret * scale
        sig = 1.0 / (1.0 + jnp.exp(-gate))
        g_gate = (grad * grouped * (sig * (1.0 + gate * (1.0 - sig)))).astype(BF16)
        g = grad * (gate * sig)
        g_ret = (scale * (g - grouped * jnp.mean(g * grouped, axis=1, keepdims=True))).astype(BF16)
        g_gate_ref[cut(at), :] = g_gate
        g_ret_ref[cut(at), :] = g_ret
        inner_ref[0, cut(at), :] = jnp.sum(g_gate.astype(F32) * gate, axis=1, keepdims=True)
        q = (q_ref[cut(at), :].astype(F32) * (down * jnp.exp(log_gamma * (BLOCK * r)))).astype(BF16)
        add = tn(q, g_ret)
        state = add if state is None else state + add
    state_ref[0] = state


def gate_backward(part, parts, here, log_gamma, q, w, first_column, gate, ret, x, pairs, shared):
    rows = q.shape[0]
    heads = q.shape[1] // HK
    features = w.shape[0]
    own = rows // parts
    count = own // BLOCK
    blocks = flat(x, pairs)
    head_out = pl.BlockSpec((own, HV), lambda h: (part, h))
    return pl.pallas_call(
        lambda *refs: gate_backward_kernel(part * count, count, len(blocks), *refs),
        grid=(heads,),
        in_specs=[
            pl.BlockSpec(memory_space=pltpu.SMEM),
            pl.BlockSpec(memory_space=pltpu.SMEM),
            pl.BlockSpec((own, HK), lambda h: (part, h)),
            pl.BlockSpec((features, HV), lambda h: (0, first_column // HV + h)),
            head_out,
            head_out,
            *[pl.BlockSpec((own, x.shape[1]), lambda h: (0, 0))] * len(blocks),
            *[pl.BlockSpec(memory_space=pl.ANY)] * len(shared),
        ],
        out_specs=[
            head_out,
            head_out,
            pl.BlockSpec((own, features), lambda h: (part, 0)),
            pl.BlockSpec((1, HK, HV), lambda h: (h, 0, 0)),
            pl.BlockSpec((1, own, 1), lambda h: (h, 0, 0)),
        ],
        input_output_aliases={6 + len(blocks) + i: i for i in range(len(shared))},
        out_shape=[
            jax.ShapeDtypeStruct((rows, heads * HV), BF16),
            jax.ShapeDtypeStruct((rows, heads * HV), BF16),
            jax.ShapeDtypeStruct((rows, features), BF16),
            jax.ShapeDtypeStruct((heads, HK, HV), F32),
            jax.ShapeDtypeStruct((heads, own, 1), F32),
        ],
        cost_estimate=pl.CostEstimate(
            flops=heads * 2 * own * HV * (HK + features),
            bytes_accessed=16 * own * heads * HV,
            transcendentals=own * heads * HV,
        ),
        name="gate_backward",
    )(here, log_gamma, q, w, gate, ret, *blocks, *shared)


def backward_kernel(total, lg_ref, q_ref, k_ref, v_ref, state_in_ref, state_grad_ref, cos_ref, sin_ref, *refs):
    g_ref, gate_ref, all_ref, inner_ref, acc_k, acc_v, g_q_ref, g_k_ref, g_v_ref, sems = refs
    head, heads = pl.program_id(0), pl.num_programs(0)
    log_gamma = lg_ref[head]
    down, across = decay_vectors(log_gamma)
    state_in, state_grad = state_in_ref[0], state_grad_ref[0]
    key_scale = 1.0 / math.sqrt(HK)

    def send(ref, column, width, i):
        target = all_ref.at[:, pl.ds(pl.multiple_of(column, HK), width)]
        return pltpu.make_async_copy(ref, target, sems.at[i])

    gates = send(gate_ref, heads * (2 * HK + HV) + head * HV, HV, 0)
    gates.start()

    def put(ref, r, x, factor):
        turned = x * cos_ref[cut(r), :] - pair_swap(x) * sin_ref[cut(r), :]
        ref[cut(r), :] = (turned * factor).astype(BF16)

    for r in range(total):
        g = g_ref[cut(r), :]
        q, k, v = q_ref[cut(r), :], k_ref[cut(r), :], v_ref[cut(r), :]
        tail = down_tail(log_gamma, total * BLOCK - r * BLOCK)
        acc_v[cut(r), :] = nn((k.astype(F32) * tail).astype(BF16), state_grad)
        acc_k[cut(r), :] = nt(v, state_grad) * tail
        g_q = nt(g, state_in) * (down * jnp.exp(log_gamma * (BLOCK * r)))
        for j in range(r + 1):
            kj, vj = k_ref[cut(j), :], v_ref[cut(j), :]
            weights = block_decay(nt(q, kj), r, j, log_gamma, down, across)
            g_scores = block_decay(nt(g, vj), r, j, log_gamma, down, across)
            acc_v[cut(j), :] += tn(weights, g)
            acc_k[cut(j), :] += tn(g_scores, q)
            g_q = g_q + nn(g_scores, kj)
        inner_ref[0, cut(r), :] = jnp.sum(g_q * q.astype(F32), axis=1, keepdims=True)
        put(g_q_ref, r, g_q, 1.0)
    for r in range(total):
        g_k = acc_k[cut(r), :]
        g_v = acc_v[cut(r), :].astype(BF16)
        g_v_ref[cut(r), :] = g_v
        inner_ref[0, cut(r), :] += jnp.sum(g_k * k_ref[cut(r), :].astype(F32), axis=1, keepdims=True) + jnp.sum(
            g_v.astype(F32) * v_ref[cut(r), :].astype(F32), axis=1, keepdims=True
        )
        put(g_k_ref, r, g_k, key_scale)
    copies = [
        send(g_q_ref, head * HK, HK, 1),
        send(g_k_ref, (heads + head) * HK, HK, 2),
        send(g_v_ref, 2 * heads * HK + head * HV, HV, 3),
    ]
    for copy in copies:
        copy.start()
    for copy in [gates] + copies:
        copy.wait()


def down_tail(log_gamma, start):
    m = lax.broadcasted_iota(jnp.int32, (BLOCK, 1), 0).astype(F32)
    return jnp.exp((start - m) * log_gamma)


def retention_backward(log_gamma, q, k, v, state_in, state_grad, cosine, sine, g_ret, g_gate):
    rows = q.shape[0]
    heads = q.shape[1] // HK
    blocks = rows // BLOCK
    pairs = blocks * (blocks + 1) // 2
    flops = heads * 2 * (pairs * BLOCK * BLOCK * (3 * HK + 2 * HV) + 3 * rows * HK * HV)
    head_keys = pl.BlockSpec((rows, HK), lambda h: (0, h))
    head_values = pl.BlockSpec((rows, HV), lambda h: (0, h))
    head_state = pl.BlockSpec((1, HK, HV), lambda h: (h, 0, 0))
    table = pl.BlockSpec((rows, HK), lambda h: (0, 0))
    return pl.pallas_call(
        lambda *refs: backward_kernel(blocks, *refs),
        grid=(heads,),
        in_specs=[
            pl.BlockSpec(memory_space=pltpu.SMEM),
            head_keys,
            head_keys,
            head_values,
            head_state,
            head_state,
            table,
            table,
            head_values,
            head_values,
        ],
        out_specs=[pl.BlockSpec(memory_space=pl.ANY), pl.BlockSpec((1, rows, 1), lambda h: (h, 0, 0))],
        out_shape=[
            jax.ShapeDtypeStruct((rows, heads * 2 * (HK + HV)), BF16),
            jax.ShapeDtypeStruct((heads, rows, 1), F32),
        ],
        scratch_shapes=[
            pltpu.VMEM((rows, HK), F32),
            pltpu.VMEM((rows, HV), F32),
            pltpu.VMEM((rows, HK), BF16),
            pltpu.VMEM((rows, HK), BF16),
            pltpu.VMEM((rows, HV), BF16),
            pltpu.SemaphoreType.DMA((4,)),
        ],
        cost_estimate=pl.CostEstimate(flops=flops, bytes_accessed=24 * rows * heads * HK, transcendentals=0),
        name="retention_backward",
    )(log_gamma, q, k, v, state_in, state_grad, cosine, sine, g_ret, g_gate)


def on_device(
    layer_input,
    gain_attn,
    w_query,
    w_key,
    w_value,
    w_retgate,
    w_out,
    gain_mlp,
    w_gate,
    w_up,
    w_down,
    cotangent,
):
    data = ("dp", "ctx")
    rows, width = layer_input.shape
    n_tp, at_tp = lax.axis_size("tp"), lax.axis_index("tp")
    features = width * n_tp
    heads = w_query.shape[1] // HK
    units = w_gate.shape[1]

    parts = 2
    own = rows // parts
    cuts = [slice(c * own, (c + 1) * own) for c in range(parts)]

    qk = heads * HK
    vw = heads * HV
    attn_shard = side_by_side(w_query, w_key, w_value, w_retgate, w_out)
    attn_full = lax.all_gather(attn_shard, data, axis=0, tiled=True)

    gains = small_gather(jnp.stack([gain_attn, gain_mlp]), "tp")

    log_gamma = jnp.log1p(-jnp.exp2(-5.0 - (at_tp * heads + jnp.arange(heads)).astype(F32)))
    log_block = rows * log_gamma
    positions = lax.axis_index("ctx") * rows + jnp.arange(rows)
    frequencies = jnp.exp(-math.log(10000.0) * jnp.linspace(0.0, 1.0, HK // 2, dtype=F32))
    angles = positions.astype(F32)[:, None] * jnp.repeat(frequencies, 2)[None, :]
    cosine = jnp.cos(angles)
    sine = jnp.sin(angles) * jnp.where(jnp.arange(HK) % 2 == 0, -1.0, 1.0)[None, :]
    here = at_tp.reshape(1)
    mlp_shard = side_by_side(w_gate, w_up, w_down)

    pairs = line_gather(layer_input, "tp", (cosine, sine, mlp_shard, log_gamma))
    normed, scale_attn, q, k, v, local_state = project(
        here, log_gamma, gains[0:1], attn_full, layer_input, pairs, heads, cosine, sine
    )
    cot = after(cotangent, pairs[-1][0])
    cot_blocks = flat(cot, line_gather(cot, "tp"))
    mlp_full = lax.all_gather(after(mlp_shard, pairs[0][1]), data, axis=0, tiled=True)
    gate_pre = product(after(normed, local_state), attn_full, (2 * qk + vw) // vw, vw)
    state_in = states_before(local_state, log_block, "ctx").astype(BF16)
    heads_out, branch = [], []
    for c in range(parts):
        *heads_out, out = retention_forward(
            c, parts, log_gamma, q, k, v, gate_pre, state_in, attn_full, 2 * qk + 2 * vw, heads_out
        )
        branch.append(out)
    gated, retained = heads_out

    def stacked(*grads):
        devices = math.prod(lax.axis_size(axis) for axis in data)
        return jnp.concatenate([g.reshape(devices, -1, g.shape[1]) for g in grads], axis=1)

    x_own = layer_input.astype(F32)
    middle, mid_pairs, scale_mlp, inner_mlp, back, grad_middle, grad_own, grad_pairs = ([] for _ in range(8))
    gain_mlp_sum = 0.0

    def norm_back(own_rows, scale, gain, inner, grad_normed):
        hat = own_rows * scale
        grad = scale * (grad_normed * gain[None, :] - hat * (inner[:, None] / features))
        return grad, jnp.sum(grad_normed * hat, axis=0)

    def row_total(inner):
        lanes = 128
        return swap_sum(inner.reshape(-1, lanes), "tp").reshape(-1)

    for c in range(parts):
        total = lax.psum_scatter(branch[c], "tp", scatter_dimension=1, tiled=True).astype(F32)
        if c:
            total = after(total, mid_pairs[c - 1][0][0])
        middle.append(x_own[cuts[c]] + total)
        mid_pairs.append(line_gather(middle[c].astype(BF16), "tp"))
    shared = []
    for c in range(parts):
        *results, scale, inner, out = mlp(
            here, gains[1:2], mlp_full, c, cot_blocks, middle[c].astype(BF16), mid_pairs[c], shared
        )
        shared = results
        scale_mlp.append(scale)
        inner_mlp.append(inner[:, 0])
        back.append(out)
    normed_mlp, hidden, grad_acts, grad_full = shared
    for c in range(parts):
        inner = row_total(inner_mlp[c])
        total = lax.psum_scatter(back[c], "tp", scatter_dimension=1, tiled=True).astype(F32)
        if c:
            total = after(total, grad_pairs[c - 1][0][0])
        grad_mid, gain_sum = norm_back(middle[c], scale_mlp[c], gain_mlp, inner, total)
        gain_mlp_sum = gain_mlp_sum + gain_sum
        grad_middle.append(cotangent[cuts[c]].astype(F32) + grad_mid)
        grad_own.append(grad_middle[c].astype(BF16))
        grad_pairs.append(line_gather(grad_own[c], "tp"))
    grad_down = tn(grad_full, hidden).astype(BF16)
    grad_gate_up = tn(after(normed_mlp, grad_down), grad_acts).astype(BF16)
    grad_mlp = stacked(grad_gate_up[:, :units], grad_gate_up[:, units:], grad_down)
    mlp_parts = nt(hidden, mlp_full[:, 2 * units :]).astype(BF16)

    grad_own[0] = after(grad_own[0], grad_mlp, mlp_parts)
    mlp_out, _ = line_scatter(after(mlp_parts, grad_pairs[-1][0][0]), "tp")
    layer_output = (jnp.concatenate(middle) + mlp_out).astype(BF16)
    shared = []
    partial_state = 0.0
    inner_attn = []
    for c in range(parts):
        *shared, ps, inner = gate_backward(
            c,
            parts,
            here,
            log_gamma,
            q,
            attn_full,
            2 * qk + 2 * vw,
            gate_pre,
            retained,
            grad_own[c],
            grad_pairs[c],
            shared,
        )
        partial_state = partial_state + ps
        inner_attn.append(jnp.sum(inner[:, :, 0], axis=0))
    g_gate, g_ret, grad_attn = shared
    state_grad, got = states_after(partial_state, log_block, "ctx")
    state_grad = state_grad.astype(BF16)
    grad_out = tn(after(grad_attn, got), gated).astype(BF16)
    grad_retgate = tn(normed, after(g_gate, got)).astype(BF16)
    grad_heads = stacked(grad_retgate, grad_out)
    grads_attn, inner = retention_backward(
        log_gamma, q, k, v, state_in, after(state_grad, grad_heads), cosine, sine, g_ret, g_gate
    )
    inner_attn = jnp.concatenate(inner_attn) + jnp.sum(inner[:, :, 0], axis=0)
    in_full = attn_full[:, : 2 * qk + 2 * vw]
    back = []
    for c in range(parts):
        back.append(nt(after(grads_attn, *back)[cuts[c]], in_full).astype(BF16))
    grad_qkv_w = tn(normed, after(grads_attn, *back)[:, : 2 * qk + vw]).astype(BF16)
    inner_attn = row_total(inner_attn)
    grad_input, gain_attn_sum = [], 0.0
    early = ()
    for c in range(parts):
        total, steps = line_scatter(after(back[c], *early), "tp")
        early = steps[0]
        grad_in, gain_sum = norm_back(x_own[cuts[c]], scale_attn[cuts[c]], gain_attn, inner_attn[cuts[c]], total)
        grad_input.append((grad_middle[c] + grad_in).astype(BF16))
        gain_attn_sum = gain_attn_sum + gain_sum
    grad_input = jnp.concatenate(grad_input)

    def shard(grad):
        return lax.psum_scatter(grad, data, scatter_dimension=0, tiled=True).astype(F32)

    s_gate, s_up, s_down = jnp.split(shard(grad_mlp)[0], 3)
    s_retgate, s_out = jnp.split(shard(grad_heads)[0], 2)
    s_qkv = shard(grad_qkv_w)
    s_query, s_key, s_value = s_qkv[:, :qk], s_qkv[:, qk : 2 * qk], s_qkv[:, 2 * qk :]
    gain_sums = swap_sum(swap_sum(jnp.stack([gain_attn_sum, gain_mlp_sum]), "ctx"), "dp")
    return (
        layer_output,
        grad_input,
        gain_sums[0],
        s_query,
        s_key,
        s_value,
        s_retgate,
        s_out,
        gain_sums[1],
        s_gate,
        s_up,
        s_down,
    )


def solution(mesh):
    tokens = P(("dp", "ctx"), "tp")
    gain = P("tp")
    weight = P(("dp", "ctx"), "tp")

    return jax.shard_map(
        on_device,
        mesh=mesh,
        in_specs=(tokens, gain, weight, weight, weight, weight, weight, gain, weight, weight, weight, tokens),
        out_specs=(tokens, tokens, gain, weight, weight, weight, weight, weight, gain, weight, weight, weight),
        check_vma=False,
    )
```

```python
import math

import jax
import jax.numpy as jnp
from jax import lax
from jax.experimental import pallas as pl
from jax.experimental.pallas import tpu as pltpu
from jax.sharding import PartitionSpec as P


HK = 256
HV = 512
EPSILON = 1e-06
BLOCK = 512
COLUMNS = 1024
TP, CTX, DP = "tp", "ctx", "dp"
F32 = jnp.float32
BF16 = jnp.bfloat16


def nn(a, b):
    return lax.dot_general(a, b, (((1,), (0,)), ((), ())), preferred_element_type=F32)


def tn(a, b):
    return lax.dot_general(a, b, (((0,), (0,)), ((), ())), preferred_element_type=F32)


def nt(a, b):
    return lax.dot_general(a, b, (((1,), (1,)), ((), ())), preferred_element_type=F32)


def after(x, *before):
    return lax.optimization_barrier((x, *before))[0]


def right(lo, hi):
    return [(i, i + 1) for i in range(lo, hi)]


def left(lo, hi):
    return [(i, i - 1) for i in range(hi, lo, -1)]


def line_gather(x, axis, before=()):
    n, i = lax.axis_size(axis), lax.axis_index(axis)
    rights, lefts = [x], [x]
    for k in range(1, n):
        r_pairs = right(k - 1, n - 1)
        l_pairs = left(0, n - k)
        if k == 2 and before:
            rights[-1] = after(rights[-1], *before)
        if 2 * k > n + 1:
            both = lax.ppermute(jnp.where(i >= k - 1, rights[-1], lefts[-1]), axis, r_pairs + l_pairs)
            rights.append(both)
            lefts.append(both)
        else:
            rights.append(lax.ppermute(rights[-1], axis, r_pairs))
            lefts.append(lax.ppermute(lefts[-1], axis, l_pairs))
    return [(rights[k], lefts[n - k]) for k in range(1, n)]


def place(blocks, axis, dtype):
    n, i = lax.axis_size(axis), lax.axis_index(axis)
    rows, width = blocks[0].shape
    full = jnp.zeros((rows, n * width), dtype)
    for k, block in enumerate(blocks):
        at = ((i - k) % n) * width
        full = lax.dynamic_update_slice(full, block.astype(dtype), (0, at))
    return full


def line_scatter(parts, axis):
    n, i = lax.axis_size(axis), lax.axis_index(axis)
    width = parts.shape[1] // n

    def block(j):
        return lax.dynamic_slice(parts, (0, jnp.clip(j, 0, n - 1) * width), (parts.shape[0], width))

    from_left = from_right = None
    early = []
    for k in range(1, n):
        r_pairs = right(0, k)
        l_pairs = left(n - 1 - k, n - 1)
        if 2 * k < n - 1:
            data = block(jnp.where(i < k, i + n - k, i - n + k))
            if from_left is not None:
                data = (data.astype(F32) + jnp.where(i < k, from_left, from_right).astype(F32)).astype(BF16)
            from_left = from_right = lax.ppermute(data, axis, r_pairs + l_pairs)
            from_left = jnp.where(i <= k, from_left, jnp.zeros_like(from_left))
            from_right = jnp.where(i >= n - 1 - k, from_right, jnp.zeros_like(from_right))
        else:
            r_data, l_data = block(i + n - k), block(i - n + k)
            if from_left is not None:
                r_data = (r_data.astype(F32) + from_left.astype(F32)).astype(BF16)
                l_data = (l_data.astype(F32) + from_right.astype(F32)).astype(BF16)
            from_left = lax.ppermute(r_data, axis, r_pairs)
            from_right = lax.ppermute(l_data, axis, l_pairs)
        if k < n - 1:
            early.append((from_left, from_right))
    return block(i).astype(F32) + from_left.astype(F32) + from_right.astype(F32), early


def small_gather(x, axis):
    n = lax.axis_size(axis)
    blocks = [x] + [lax.ppermute(x, axis, [(j, (j + s) % n) for j in range(n)]) for s in range(1, n)]
    return place(blocks, axis, x.dtype)


def swap_sum(x, axis):
    n = lax.axis_size(axis)
    g = 1
    while g < n:
        x = x + lax.ppermute(x, axis, [(j, j ^ g) for j in range(n)])
        g *= 2
    return x


def states_before(local, log_block, axis):
    n, b = lax.axis_size(axis), lax.axis_index(axis)
    total, prefix, g = local, jnp.zeros_like(local), 1
    while g < n:
        got = lax.ppermute(total.astype(BF16), axis, [(j, j ^ g) for j in range(n)]).astype(F32)
        upper = (b // g) % 2 == 1
        mine = jnp.exp((b % g).astype(F32) * log_block)[:, None, None]
        whole = jnp.exp(g * log_block)[:, None, None]
        prefix = jnp.where(upper, prefix + mine * got, prefix)
        total = jnp.where(upper, whole * got + total, whole * total + got)
        g *= 2
    return prefix


def states_after(local, log_block, axis):
    first = None
    n, b = lax.axis_size(axis), lax.axis_index(axis)
    total, suffix, g = local, jnp.zeros_like(local), 1
    while g < n:
        got = lax.ppermute(total.astype(BF16), axis, [(j, j ^ g) for j in range(n)]).astype(F32)
        first = got if first is None else first
        upper = (b // g) % 2 == 1
        mine = jnp.exp((g - 1 - b % g).astype(F32) * log_block)[:, None, None]
        whole = jnp.exp(g * log_block)[:, None, None]
        suffix = jnp.where(upper, suffix, suffix + mine * got)
        total = jnp.where(upper, got + whole * total, total + whole * got)
        g *= 2
    return suffix, first


def pair_swap(x):
    lane = lax.broadcasted_iota(jnp.int32, x.shape, 1)
    width = x.shape[1]
    return jnp.where(lane % 2 == 0, pltpu.roll(x, width - 1, 1), pltpu.roll(x, 1, 1))


def side_by_side(*arrays):
    rows = arrays[0].shape[0]
    widths = [a.shape[1] for a in arrays]

    def kernel(*refs):
        column = 0
        for ref, width in zip(refs, widths):
            refs[-1][:, column : column + width] = ref[...]
            column += width

    block = min(rows, 64)
    return pl.pallas_call(
        kernel,
        grid=(rows // block,),
        in_specs=[pl.BlockSpec((block, width), lambda r: (r, 0)) for width in widths],
        out_specs=pl.BlockSpec((block, sum(widths)), lambda r: (r, 0)),
        out_shape=jax.ShapeDtypeStruct((rows, sum(widths)), arrays[0].dtype),
        cost_estimate=pl.CostEstimate(flops=0, bytes_accessed=4 * rows * sum(widths), transcendentals=0),
        name="join",
    )(*arrays)


def stacked(devices, *grads):
    rows = grads[0].shape[0] // devices
    counts = [g.shape[1] // COLUMNS for g in grads]
    firsts = [sum(counts[:i]) for i in range(len(counts))]

    def kernel(*refs):
        t = pl.program_id(1)
        for ref, first, count in zip(refs, firsts, counts):

            @pl.when((t >= first) & (t < first + count))
            def _(ref=ref):
                refs[-1][0] = ref[...]

    def spec(first, count):
        return pl.BlockSpec((rows, COLUMNS), lambda d, t: (d, jnp.clip(t - first, 0, count - 1)))

    total = sum(counts)
    return pl.pallas_call(
        kernel,
        grid=(devices, total),
        in_specs=[spec(first, count) for first, count in zip(firsts, counts)],
        out_specs=pl.BlockSpec((1, rows, COLUMNS), lambda d, t: (d, t, 0)),
        out_shape=jax.ShapeDtypeStruct((devices, total * rows, COLUMNS), grads[0].dtype),
        cost_estimate=pl.CostEstimate(flops=0, bytes_accessed=4 * devices * total * rows * COLUMNS, transcendentals=0),
        name="stack",
    )(*grads)


def gathered(at, refs, k, rows=slice(None)):
    if k == 0:
        return refs[0][rows, :]
    return jnp.where(at >= k, refs[2 * k - 1][rows, :], refs[2 * k][rows, :])


def columns_of(at, n, k, width):
    return pl.ds(pl.multiple_of(((at + n - k) % n) * width, width), width)


def fill_normed(at, refs, gain_ref, full_ref):
    n = len(refs) // 2 + 1
    width = refs[0].shape[1]
    blocks = [gathered(at, refs, k).astype(F32) for k in range(n)]
    squares = sum(jnp.sum(b * b, axis=1, keepdims=True) for b in blocks)
    scale = lax.rsqrt(squares / (n * width) + EPSILON)
    for k, b in enumerate(blocks):
        where = columns_of(at, n, k, width)
        full_ref[:, where] = (b * scale * gain_ref[:, where]).astype(BF16)
    return scale


def flat(x, pairs):
    return [x] + [p for pair in pairs for p in pair]


def project_kernel(heads, count, at_ref, lg_ref, gain_ref, w_ref, cos_ref, sin_ref, *refs):
    blocks, (full_ref, scale_ref, q_ref, k_ref, v_ref, state_ref) = refs[:count], refs[count:]
    step = pl.program_id(0)
    rows = pl.num_programs(0) * BLOCK
    scale_ref[...] = fill_normed(at_ref[0], blocks, gain_ref, full_ref)
    x = full_ref[...]
    qk = heads * HK
    c, s = cos_ref[...], sin_ref[...]
    k_out = nn(x, w_ref[:, qk : 2 * qk])
    v_out = nn(x, w_ref[:, 2 * qk :]).astype(BF16)
    q_out = nn(x, w_ref[:, :qk])
    v_ref[...] = v_out
    m = lax.broadcasted_iota(jnp.int32, (BLOCK, 1), 0) + step * BLOCK
    for h in range(heads):
        at = slice(h * HK, (h + 1) * HK)
        one = k_out[:, at]
        key = ((one * c + pair_swap(one) * s) * (1.0 / math.sqrt(HK))).astype(BF16)
        k_ref[:, at] = key
        tail = jnp.exp((rows - m).astype(F32) * lg_ref[h])
        add = tn((key.astype(F32) * tail).astype(BF16), v_out[:, h * HV : (h + 1) * HV])

        @pl.when(step == 0)
        def _(h=h, add=add):
            state_ref[h] = add

        @pl.when(step > 0)
        def _(h=h, add=add):
            state_ref[h] += add

        one = q_out[:, at]
        q_ref[:, at] = (one * c + pair_swap(one) * s).astype(BF16)


def project(at, log_gamma, gain, w, x, pairs, heads, cosine, sine):
    rows, width = x.shape
    features = w.shape[0]
    outs = 2 * heads * HK + heads * HV
    blocks = flat(x, pairs)

    def by_rows(columns):
        return pl.BlockSpec((BLOCK, columns), lambda r: (r, 0))

    return pl.pallas_call(
        lambda *refs: project_kernel(heads, len(blocks), *refs),
        grid=(rows // BLOCK,),
        in_specs=[
            pl.BlockSpec(memory_space=pltpu.SMEM),
            pl.BlockSpec(memory_space=pltpu.SMEM),
            pl.BlockSpec((1, features), lambda r: (0, 0)),
            pl.BlockSpec((features, outs), lambda r: (0, 0)),
            by_rows(HK),
            by_rows(HK),
            *[by_rows(width)] * len(blocks),
        ],
        out_specs=[
            by_rows(features),
            by_rows(1),
            by_rows(heads * HK),
            by_rows(heads * HK),
            by_rows(heads * HV),
            pl.BlockSpec((heads, HK, HV), lambda r: (0, 0, 0)),
        ],
        out_shape=[
            jax.ShapeDtypeStruct((rows, features), BF16),
            jax.ShapeDtypeStruct((rows, 1), F32),
            jax.ShapeDtypeStruct((rows, heads * HK), BF16),
            jax.ShapeDtypeStruct((rows, heads * HK), BF16),
            jax.ShapeDtypeStruct((rows, heads * HV), BF16),
            jax.ShapeDtypeStruct((heads, HK, HV), F32),
        ],
        cost_estimate=pl.CostEstimate(
            flops=2 * rows * features * outs, bytes_accessed=2 * features * outs + 12 * rows * features, transcendentals=0
        ),
        name="proj",
    )(at, log_gamma, gain, w, cosine, sine, *blocks)


def product_kernel(x_ref, w_ref, out_ref):
    out_ref[...] = nn(x_ref[...], w_ref[...])


def product(x, w, at, columns):
    rows, inner = x.shape
    return pl.pallas_call(
        product_kernel,
        grid=(rows // BLOCK,),
        in_specs=[
            pl.BlockSpec((BLOCK, inner), lambda r: (r, 0)),
            pl.BlockSpec((inner, columns), lambda r: (0, at)),
        ],
        out_specs=pl.BlockSpec((BLOCK, columns), lambda r: (r, 0)),
        out_shape=jax.ShapeDtypeStruct((rows, columns), F32),
        cost_estimate=pl.CostEstimate(
            flops=2 * rows * inner * columns, bytes_accessed=2 * inner * columns + 8 * rows * columns, transcendentals=0
        ),
        name="prod",
    )(x, w)


def mlp_kernel(units, count, at_ref, gain_ref, w_ref, grad_ref, *refs):
    blocks, (full_ref, hidden_ref, acts_ref, scale_ref, inner_ref, back_ref) = refs[:count], refs[-6:]
    scale_ref[...] = fill_normed(at_ref[0], blocks, gain_ref, full_ref)
    x = full_ref[...]
    gate = nn(x, w_ref[:, :units])
    up = nn(x, w_ref[:, units : 2 * units])
    grad = nn(grad_ref[...], w_ref[:, 2 * units :])
    cdf = 0.5 * (1.0 + lax.erf(gate * math.sqrt(0.5)))
    gelu = gate * cdf
    density = jnp.exp(-0.5 * gate * gate) * (1.0 / math.sqrt(2.0 * math.pi))
    hidden_ref[...] = (gelu * up).astype(BF16)
    g_gate = (grad * up * (cdf + gate * density)).astype(BF16)
    g_up = (grad * gelu).astype(BF16)
    acts_ref[:, :units] = g_gate
    acts_ref[:, units:] = g_up
    inner_ref[...] = jnp.sum(g_gate.astype(F32) * gate + g_up.astype(F32) * up, axis=1, keepdims=True)
    back_ref[...] = (nt(g_gate, w_ref[:, :units]) + nt(g_up, w_ref[:, units : 2 * units])).astype(BF16)


def mlp(at, gain, w, part, grad, x, pairs, shared):
    rows, width = x.shape
    features = w.shape[0]
    units = w.shape[1] // 3
    blocks = flat(x, pairs)
    steps = rows // BLOCK
    total = grad.shape[0]

    def by_rows(columns):
        return pl.BlockSpec((BLOCK, columns), lambda r: (r, 0))

    def own_rows(columns):
        return pl.BlockSpec((BLOCK, columns), lambda r: (part * steps + r, 0))

    return pl.pallas_call(
        lambda *refs: mlp_kernel(units, len(blocks), *refs),
        grid=(steps,),
        in_specs=[
            pl.BlockSpec(memory_space=pltpu.SMEM),
            pl.BlockSpec((1, features), lambda r: (0, 0)),
            pl.BlockSpec((features, 3 * units), lambda r: (0, 0)),
            own_rows(features),
            *[by_rows(width)] * len(blocks),
            *[pl.BlockSpec(memory_space=pl.ANY)] * len(shared),
        ],
        out_specs=[
            own_rows(features),
            own_rows(units),
            own_rows(2 * units),
            by_rows(1),
            by_rows(1),
            by_rows(features),
        ],
        out_shape=[
            jax.ShapeDtypeStruct((total, features), BF16),
            jax.ShapeDtypeStruct((total, units), BF16),
            jax.ShapeDtypeStruct((total, 2 * units), BF16),
            jax.ShapeDtypeStruct((rows, 1), F32),
            jax.ShapeDtypeStruct((rows, 1), F32),
            jax.ShapeDtypeStruct((rows, features), BF16),
        ],
        input_output_aliases={4 + len(blocks) + i: i for i in range(len(shared))},
        cost_estimate=pl.CostEstimate(
            flops=10 * rows * features * units,
            bytes_accessed=6 * features * units + 14 * rows * features,
            transcendentals=2 * rows * units,
        ),
        name="mlp",
    )(at, gain, w, grad, *blocks, *shared)


def decay_vectors(log_gamma):
    down = lax.broadcasted_iota(jnp.int32, (BLOCK, 1), 0).astype(F32)
    across = lax.broadcasted_iota(jnp.int32, (1, BLOCK), 1).astype(F32)
    return jnp.exp(down * log_gamma), jnp.exp(-across * log_gamma)


def block_decay(scores, r, j, log_gamma, down, across):
    out = scores * (down * jnp.exp(log_gamma * (BLOCK * (r - j)))) * across
    if r == j:
        n = lax.broadcasted_iota(jnp.int32, scores.shape, 0)
        m = lax.broadcasted_iota(jnp.int32, scores.shape, 1)
        out = jnp.where(n >= m, out, 0.0)
    return out.astype(BF16)


def cut(r):
    return slice(r * BLOCK, (r + 1) * BLOCK)


def forward_kernel(first, count, lg_ref, q_ref, k_ref, v_ref, gate_ref, state_ref, w_ref, *refs):
    gated_ref, ret_ref, out_ref, acc_ref = refs[-4:]
    head = pl.program_id(0)
    log_gamma = lg_ref[head]
    down, across = decay_vectors(log_gamma)
    state = state_ref[0]
    for at in range(count):
        r = first + at
        q = q_ref[cut(at), :]
        ret = nn(q, state) * (down * jnp.exp(log_gamma * (BLOCK * r)))
        for j in range(r + 1):
            weights = block_decay(nt(q, k_ref[cut(j), :]), r, j, log_gamma, down, across)
            ret = ret + nn(weights, v_ref[cut(j), :])
        ret_ref[cut(at), :] = ret
        scale = lax.rsqrt(jnp.mean(ret * ret, axis=1, keepdims=True) + EPSILON)
        gate = gate_ref[cut(at), :]
        gated = (gate / (1.0 + jnp.exp(-gate)) * (ret * scale)).astype(BF16)
        gated_ref[cut(at), :] = gated
        out = nt(gated, w_ref[...])

        @pl.when(head == 0)
        def _(at=at, out=out):
            acc_ref[cut(at), :] = out

        @pl.when(head > 0)
        def _(at=at, out=out):
            acc_ref[cut(at), :] += out

        @pl.when(head == pl.num_programs(0) - 1)
        def _(at=at):
            out_ref[cut(at), :] = acc_ref[cut(at), :].astype(BF16)


def retention_forward(part, parts, log_gamma, q, k, v, gate, state, w, first_column, shared):
    rows = q.shape[0]
    heads = q.shape[1] // HK
    features = w.shape[0]
    own = rows // parts
    seen = own * (part + 1)
    count = own // BLOCK
    pairs = sum(part * count + at + 1 for at in range(count))
    flops = heads * (pairs * 2 * BLOCK * BLOCK * (HK + HV) + 2 * own * HK * HV + 2 * own * HV * features)
    head_out = pl.BlockSpec((own, HV), lambda h: (part, h))
    return pl.pallas_call(
        lambda *refs: forward_kernel(part * count, count, *refs),
        grid=(heads,),
        in_specs=[
            pl.BlockSpec(memory_space=pltpu.SMEM),
            pl.BlockSpec((own, HK), lambda h: (part, h)),
            pl.BlockSpec((seen, HK), lambda h: (0, h)),
            pl.BlockSpec((seen, HV), lambda h: (0, h)),
            pl.BlockSpec((own, HV), lambda h: (part, h)),
            pl.BlockSpec((1, HK, HV), lambda h: (h, 0, 0)),
            pl.BlockSpec((features, HV), lambda h: (0, first_column // HV + h)),
            *[pl.BlockSpec(memory_space=pl.ANY)] * len(shared),
        ],
        out_specs=[head_out, head_out, pl.BlockSpec((own, features), lambda h: (0, 0))],
        input_output_aliases={7 + i: i for i in range(len(shared))},
        out_shape=[
            jax.ShapeDtypeStruct((rows, heads * HV), BF16),
            jax.ShapeDtypeStruct((rows, heads * HV), F32),
            jax.ShapeDtypeStruct((own, features), BF16),
        ],
        scratch_shapes=[pltpu.VMEM((own, features), F32)],
        cost_estimate=pl.CostEstimate(flops=flops, bytes_accessed=20 * own * heads * HV, transcendentals=own * heads * HV),
        name="fwd",
    )(log_gamma, q, k, v, gate, state, w, *shared)


def gate_backward_kernel(first, count, n_blocks, at_ref, lg_ref, q_ref, w_ref, gate_ref, ret_ref, *refs):
    blocks, (g_gate_ref, g_ret_ref, full_ref, state_ref, inner_ref) = refs[:n_blocks], refs[-5:]
    head = pl.program_id(0)
    log_gamma = lg_ref[head]
    down, _ = decay_vectors(log_gamma)
    n = n_blocks // 2 + 1
    width = blocks[0].shape[1]
    here = at_ref[0]
    state = None
    for at in range(count):
        r = first + at

        @pl.when(head == 0)
        def _(at=at):
            for k in range(n):
                full_ref[cut(at), columns_of(here, n, k, width)] = gathered(here, blocks, k, cut(at))

        grad = nn(full_ref[cut(at), :], w_ref[...])
        ret = ret_ref[cut(at), :]
        gate = gate_ref[cut(at), :]
        scale = lax.rsqrt(jnp.mean(ret * ret, axis=1, keepdims=True) + EPSILON)
        grouped = ret * scale
        sig = 1.0 / (1.0 + jnp.exp(-gate))
        g_gate = (grad * grouped * (sig * (1.0 + gate * (1.0 - sig)))).astype(BF16)
        g = grad * (gate * sig)
        g_ret = (scale * (g - grouped * jnp.mean(g * grouped, axis=1, keepdims=True))).astype(BF16)
        g_gate_ref[cut(at), :] = g_gate
        g_ret_ref[cut(at), :] = g_ret
        inner_ref[0, cut(at), :] = jnp.sum(g_gate.astype(F32) * gate, axis=1, keepdims=True)
        q = (q_ref[cut(at), :].astype(F32) * (down * jnp.exp(log_gamma * (BLOCK * r)))).astype(BF16)
        add = tn(q, g_ret)
        state = add if state is None else state + add
    state_ref[0] = state


def gate_backward(part, parts, here, log_gamma, q, w, first_column, gate, ret, x, pairs, shared):
    rows = q.shape[0]
    heads = q.shape[1] // HK
    features = w.shape[0]
    own = rows // parts
    count = own // BLOCK
    blocks = flat(x, pairs)
    head_out = pl.BlockSpec((own, HV), lambda h: (part, h))
    return pl.pallas_call(
        lambda *refs: gate_backward_kernel(part * count, count, len(blocks), *refs),
        grid=(heads,),
        in_specs=[
            pl.BlockSpec(memory_space=pltpu.SMEM),
            pl.BlockSpec(memory_space=pltpu.SMEM),
            pl.BlockSpec((own, HK), lambda h: (part, h)),
            pl.BlockSpec((features, HV), lambda h: (0, first_column // HV + h)),
            head_out,
            head_out,
            *[pl.BlockSpec((own, x.shape[1]), lambda h: (0, 0))] * len(blocks),
            *[pl.BlockSpec(memory_space=pl.ANY)] * len(shared),
        ],
        out_specs=[
            head_out,
            head_out,
            pl.BlockSpec((own, features), lambda h: (part, 0)),
            pl.BlockSpec((1, HK, HV), lambda h: (h, 0, 0)),
            pl.BlockSpec((1, own, 1), lambda h: (h, 0, 0)),
        ],
        input_output_aliases={6 + len(blocks) + i: i for i in range(len(shared))},
        out_shape=[
            jax.ShapeDtypeStruct((rows, heads * HV), BF16),
            jax.ShapeDtypeStruct((rows, heads * HV), BF16),
            jax.ShapeDtypeStruct((rows, features), BF16),
            jax.ShapeDtypeStruct((heads, HK, HV), F32),
            jax.ShapeDtypeStruct((heads, own, 1), F32),
        ],
        cost_estimate=pl.CostEstimate(
            flops=heads * 2 * own * HV * (HK + features),
            bytes_accessed=16 * own * heads * HV,
            transcendentals=own * heads * HV,
        ),
        name="gate",
    )(here, log_gamma, q, w, gate, ret, *blocks, *shared)


def backward_kernel(total, lg_ref, q_ref, k_ref, v_ref, state_in_ref, state_grad_ref, cos_ref, sin_ref, *refs):
    g_ref, gate_ref, all_ref, inner_ref, acc_k, acc_v, g_q_ref, g_k_ref, g_v_ref, sems = refs
    head, heads = pl.program_id(0), pl.num_programs(0)
    log_gamma = lg_ref[head]
    down, across = decay_vectors(log_gamma)
    state_in, state_grad = state_in_ref[0], state_grad_ref[0]
    key_scale = 1.0 / math.sqrt(HK)

    def send(ref, column, width, i):
        target = all_ref.at[:, pl.ds(pl.multiple_of(column, HK), width)]
        return pltpu.make_async_copy(ref, target, sems.at[i])

    gates = send(gate_ref, heads * (2 * HK + HV) + head * HV, HV, 0)
    gates.start()

    def put(ref, r, x, factor):
        turned = x * cos_ref[cut(r), :] - pair_swap(x) * sin_ref[cut(r), :]
        ref[cut(r), :] = (turned * factor).astype(BF16)

    for r in range(total):
        g = g_ref[cut(r), :]
        q, k, v = q_ref[cut(r), :], k_ref[cut(r), :], v_ref[cut(r), :]
        tail = down_tail(log_gamma, total * BLOCK - r * BLOCK)
        acc_v[cut(r), :] = nn((k.astype(F32) * tail).astype(BF16), state_grad)
        acc_k[cut(r), :] = nt(v, state_grad) * tail
        g_q = nt(g, state_in) * (down * jnp.exp(log_gamma * (BLOCK * r)))
        for j in range(r + 1):
            kj, vj = k_ref[cut(j), :], v_ref[cut(j), :]
            weights = block_decay(nt(q, kj), r, j, log_gamma, down, across)
            g_scores = block_decay(nt(g, vj), r, j, log_gamma, down, across)
            acc_v[cut(j), :] += tn(weights, g)
            acc_k[cut(j), :] += tn(g_scores, q)
            g_q = g_q + nn(g_scores, kj)
        inner_ref[0, cut(r), :] = jnp.sum(g_q * q.astype(F32), axis=1, keepdims=True)
        put(g_q_ref, r, g_q, 1.0)
    for r in range(total):
        g_k = acc_k[cut(r), :]
        g_v = acc_v[cut(r), :].astype(BF16)
        g_v_ref[cut(r), :] = g_v
        inner_ref[0, cut(r), :] += jnp.sum(g_k * k_ref[cut(r), :].astype(F32), axis=1, keepdims=True) + jnp.sum(
            g_v.astype(F32) * v_ref[cut(r), :].astype(F32), axis=1, keepdims=True
        )
        put(g_k_ref, r, g_k, key_scale)
    copies = [
        send(g_q_ref, head * HK, HK, 1),
        send(g_k_ref, (heads + head) * HK, HK, 2),
        send(g_v_ref, 2 * heads * HK + head * HV, HV, 3),
    ]
    for copy in copies:
        copy.start()
    for copy in [gates] + copies:
        copy.wait()


def down_tail(log_gamma, start):
    m = lax.broadcasted_iota(jnp.int32, (BLOCK, 1), 0).astype(F32)
    return jnp.exp((start - m) * log_gamma)


def retention_backward(log_gamma, q, k, v, state_in, state_grad, cosine, sine, g_ret, g_gate):
    rows = q.shape[0]
    heads = q.shape[1] // HK
    blocks = rows // BLOCK
    pairs = blocks * (blocks + 1) // 2
    flops = heads * 2 * (pairs * BLOCK * BLOCK * (3 * HK + 2 * HV) + 3 * rows * HK * HV)
    head_keys = pl.BlockSpec((rows, HK), lambda h: (0, h))
    head_values = pl.BlockSpec((rows, HV), lambda h: (0, h))
    head_state = pl.BlockSpec((1, HK, HV), lambda h: (h, 0, 0))
    table = pl.BlockSpec((rows, HK), lambda h: (0, 0))
    return pl.pallas_call(
        lambda *refs: backward_kernel(blocks, *refs),
        grid=(heads,),
        in_specs=[
            pl.BlockSpec(memory_space=pltpu.SMEM),
            head_keys,
            head_keys,
            head_values,
            head_state,
            head_state,
            table,
            table,
            head_values,
            head_values,
        ],
        out_specs=[pl.BlockSpec(memory_space=pl.ANY), pl.BlockSpec((1, rows, 1), lambda h: (h, 0, 0))],
        out_shape=[
            jax.ShapeDtypeStruct((rows, heads * 2 * (HK + HV)), BF16),
            jax.ShapeDtypeStruct((heads, rows, 1), F32),
        ],
        scratch_shapes=[
            pltpu.VMEM((rows, HK), F32),
            pltpu.VMEM((rows, HV), F32),
            pltpu.VMEM((rows, HK), BF16),
            pltpu.VMEM((rows, HK), BF16),
            pltpu.VMEM((rows, HV), BF16),
            pltpu.SemaphoreType.DMA((4,)),
        ],
        cost_estimate=pl.CostEstimate(flops=flops, bytes_accessed=24 * rows * heads * HK, transcendentals=0),
        name="bwd",
    )(log_gamma, q, k, v, state_in, state_grad, cosine, sine, g_ret, g_gate)


def on_device(
    layer_input,
    gain_attn,
    w_query,
    w_key,
    w_value,
    w_retgate,
    w_out,
    gain_mlp,
    w_gate,
    w_up,
    w_down,
    cotangent,
):
    data = (DP, CTX)
    rows, width = layer_input.shape
    n_tp, at_tp = lax.axis_size(TP), lax.axis_index(TP)
    features = width * n_tp
    heads = w_query.shape[1] // HK
    units = w_gate.shape[1]

    parts = 2
    own = rows // parts
    cuts = [slice(c * own, (c + 1) * own) for c in range(parts)]

    qk = heads * HK
    vw = heads * HV
    attn_shard = side_by_side(w_query, w_key, w_value, w_retgate, w_out)
    attn_full = lax.all_gather(attn_shard, data, axis=0, tiled=True)

    gains = small_gather(jnp.stack([gain_attn, gain_mlp]), TP)

    log_gamma = jnp.log1p(-jnp.exp2(-5.0 - (at_tp * heads + jnp.arange(heads)).astype(F32)))
    log_block = rows * log_gamma
    positions = lax.axis_index(CTX) * rows + jnp.arange(rows)
    frequencies = jnp.exp(-math.log(10000.0) * jnp.linspace(0.0, 1.0, HK // 2, dtype=F32))
    angles = positions.astype(F32)[:, None] * jnp.repeat(frequencies, 2)[None, :]
    cosine = jnp.cos(angles)
    sine = jnp.sin(angles) * jnp.where(jnp.arange(HK) % 2 == 0, -1.0, 1.0)[None, :]
    here = at_tp.reshape(1)
    mlp_shard = side_by_side(w_gate, w_up, w_down)

    pairs = line_gather(layer_input, TP, (cosine, sine, mlp_shard, log_gamma, gains))
    normed, scale_attn, q, k, v, local_state = project(
        here, log_gamma, gains[0:1], attn_full, layer_input, pairs, heads, cosine, sine
    )
    grad_full = lax.all_gather(after(cotangent, pairs[0][0]), TP, axis=1, tiled=True)
    mlp_full = lax.all_gather(after(mlp_shard, pairs[0][1]), data, axis=0, tiled=True)
    gate_pre = product(after(normed, local_state), attn_full, (2 * qk + vw) // vw, vw)
    state_in = states_before(local_state, log_block, CTX).astype(BF16)
    heads_out, branch = [], []
    for c in range(parts):
        *heads_out, out = retention_forward(
            c, parts, log_gamma, q, k, v, gate_pre, state_in, attn_full, 2 * qk + 2 * vw, heads_out
        )
        branch.append(out)
    gated, retained = heads_out

    devices = math.prod(lax.axis_size(axis) for axis in data)

    x_own = layer_input.astype(F32)
    middle, mid_pairs, scale_mlp, inner_mlp, back, grad_middle, grad_own, grad_pairs = ([] for _ in range(8))
    gain_mlp_sum = 0.0

    def norm_back(own_rows, scale, gain, inner, grad_normed):
        hat = own_rows * scale
        grad = scale * (grad_normed * gain[None, :] - hat * (inner[:, None] / features))
        return grad, jnp.sum(grad_normed * hat, axis=0)

    def row_total(inner):
        lanes = 128
        return swap_sum(inner.reshape(-1, lanes), TP).reshape(-1)

    early = ()
    for c in range(parts):
        total, steps = line_scatter(after(branch[c], *early), TP)
        early = steps[-1]
        if c:
            total = after(total, mid_pairs[c - 1][0][0])
        middle.append(x_own[cuts[c]] + total)
        mid_pairs.append(line_gather(middle[c].astype(BF16), TP))
    shared = []
    for c in range(parts):
        *results, scale, inner, out = mlp(
            here, gains[1:2], mlp_full, c, grad_full, middle[c].astype(BF16), mid_pairs[c], shared
        )
        shared = results
        scale_mlp.append(scale)
        inner_mlp.append(inner[:, 0])
        back.append(out)
    normed_mlp, hidden, grad_acts = shared
    early = ()
    for c in range(parts):
        inner = row_total(inner_mlp[c])
        total, steps = line_scatter(after(back[c], *early), TP)
        early = steps[-1]
        if c:
            total = after(total, grad_pairs[c - 1][0][0])
        grad_mid, gain_sum = norm_back(middle[c], scale_mlp[c], gain_mlp, inner, total)
        gain_mlp_sum = gain_mlp_sum + gain_sum
        grad_middle.append(cotangent[cuts[c]].astype(F32) + grad_mid)
        grad_own.append(grad_middle[c].astype(BF16))
        grad_pairs.append(line_gather(grad_own[c], TP))
    grad_down = tn(grad_full, hidden).astype(BF16)
    grad_gate_up = tn(after(normed_mlp, grad_down), grad_acts).astype(BF16)
    grad_mlp = stacked(devices, grad_gate_up, grad_down)
    mlp_parts = nt(hidden, mlp_full[:, 2 * units :]).astype(BF16)

    grad_own[0] = after(grad_own[0], grad_mlp)
    mlp_out = lax.psum_scatter(after(mlp_parts, grad_pairs[-1][0][0]), TP, scatter_dimension=1, tiled=True)
    layer_output = (jnp.concatenate(middle) + mlp_out.astype(F32)).astype(BF16)
    shared = []
    partial_state = 0.0
    inner_attn = []
    for c in range(parts):
        *shared, ps, inner = gate_backward(
            c,
            parts,
            here,
            log_gamma,
            q,
            attn_full,
            2 * qk + 2 * vw,
            gate_pre,
            retained,
            grad_own[c],
            grad_pairs[c],
            shared,
        )
        partial_state = partial_state + ps
        inner_attn.append(jnp.sum(inner[:, :, 0], axis=0))
    g_gate, g_ret, grad_attn = shared
    state_grad, got = states_after(partial_state, log_block, CTX)
    state_grad = state_grad.astype(BF16)
    grad_out = tn(after(grad_attn, got), gated).astype(BF16)
    grad_retgate = tn(normed, after(g_gate, got)).astype(BF16)
    grad_heads = stacked(devices, grad_retgate, grad_out)
    grads_attn, inner = retention_backward(
        log_gamma, q, k, v, state_in, after(state_grad, grad_heads), cosine, sine, g_ret, g_gate
    )
    inner_attn = jnp.concatenate(inner_attn) + jnp.sum(inner[:, :, 0], axis=0)
    in_full = attn_full[:, : 2 * qk + 2 * vw]
    back = []
    for c in range(parts):
        rows_grads = after(grads_attn, *back, *([grad_qkv_w] if c else []))
        back.append(nt(rows_grads[cuts[c]], in_full).astype(BF16))
        if c == 0:
            grad_qkv_w = tn(normed, after(grads_attn, *back)[:, : 2 * qk + vw]).astype(BF16)
    inner_attn = row_total(inner_attn)
    grad_input, gain_attn_sum = [], 0.0
    early = ()
    for c in range(parts):
        total, steps = line_scatter(after(back[c], *early), TP)
        early = steps[0]
        grad_in, gain_sum = norm_back(x_own[cuts[c]], scale_attn[cuts[c]], gain_attn, inner_attn[cuts[c]], total)
        grad_input.append((grad_middle[c] + grad_in).astype(BF16))
        gain_attn_sum = gain_attn_sum + gain_sum
    grad_input = jnp.concatenate(grad_input)

    def shard(grad):
        return lax.psum_scatter(grad, data, scatter_dimension=0, tiled=True).astype(F32)

    s_gate, s_up, s_down = jnp.split(shard(grad_mlp)[0], 3)
    s_retgate, s_out = jnp.split(shard(grad_heads)[0], 2)
    s_qkv = shard(grad_qkv_w)
    s_query, s_key, s_value = s_qkv[:, :qk], s_qkv[:, qk : 2 * qk], s_qkv[:, 2 * qk :]
    gain_sums = swap_sum(swap_sum(jnp.stack([gain_attn_sum, gain_mlp_sum]), CTX), DP)
    return (
        layer_output,
        grad_input,
        gain_sums[0],
        s_query,
        s_key,
        s_value,
        s_retgate,
        s_out,
        gain_sums[1],
        s_gate,
        s_up,
        s_down,
    )


def solution(mesh):
    tokens = P((DP, CTX), TP)
    gain = P(TP)
    weight = P((DP, CTX), TP)

    return jax.shard_map(
        on_device,
        mesh=mesh,
        in_specs=(tokens, gain, weight, weight, weight, weight, weight, gain, weight, weight, weight, tokens),
        out_specs=(tokens, tokens, gain, weight, weight, weight, weight, weight, gain, weight, weight, weight),
        check_vma=False,
    )
```

```python
import math

import jax
import jax.numpy as jnp
from jax import lax
from jax.experimental import pallas as pl
from jax.experimental.pallas import tpu as pltpu
from jax.sharding import PartitionSpec as P


HK = 256
HV = 512
EPSILON = 1e-06
BLOCK = 512
TP, CTX, DP = "tp", "ctx", "dp"
F32 = jnp.float32
BF16 = jnp.bfloat16


def nn(a, b):
    return lax.dot_general(a, b, (((1,), (0,)), ((), ())), preferred_element_type=F32)


def tn(a, b):
    return lax.dot_general(a, b, (((0,), (0,)), ((), ())), preferred_element_type=F32)


def nt(a, b):
    return lax.dot_general(a, b, (((1,), (1,)), ((), ())), preferred_element_type=F32)


def after(x, *before):
    return lax.optimization_barrier((x, *before))[0]


def right(lo, hi):
    return [(i, i + 1) for i in range(lo, hi)]


def left(lo, hi):
    return [(i, i - 1) for i in range(hi, lo, -1)]


def line_gather(x, axis, before=()):
    n, i = lax.axis_size(axis), lax.axis_index(axis)
    rights, lefts = [x], [x]
    for k in range(1, n):
        r_pairs = right(k - 1, n - 1)
        l_pairs = left(0, n - k)
        if k == 2 and before:
            rights[-1] = after(rights[-1], *before)
        if 2 * k > n + 1:
            both = lax.ppermute(jnp.where(i >= k - 1, rights[-1], lefts[-1]), axis, r_pairs + l_pairs)
            rights.append(both)
            lefts.append(both)
        else:
            rights.append(lax.ppermute(rights[-1], axis, r_pairs))
            lefts.append(lax.ppermute(lefts[-1], axis, l_pairs))
    return [(rights[k], lefts[n - k]) for k in range(1, n)]


def place(blocks, axis, dtype):
    n, i = lax.axis_size(axis), lax.axis_index(axis)
    rows, width = blocks[0].shape
    full = jnp.zeros((rows, n * width), dtype)
    for k, block in enumerate(blocks):
        at = ((i - k) % n) * width
        full = lax.dynamic_update_slice(full, block.astype(dtype), (0, at))
    return full


def line_scatter(parts, axis):
    n, i = lax.axis_size(axis), lax.axis_index(axis)
    width = parts.shape[1] // n

    def block(j):
        return lax.dynamic_slice(parts, (0, jnp.clip(j, 0, n - 1) * width), (parts.shape[0], width))

    from_left = from_right = None
    early = []
    for k in range(1, n):
        r_pairs = right(0, k)
        l_pairs = left(n - 1 - k, n - 1)
        if 2 * k < n - 1:
            data = block(jnp.where(i < k, i + n - k, i - n + k))
            if from_left is not None:
                data = (data.astype(F32) + jnp.where(i < k, from_left, from_right).astype(F32)).astype(BF16)
            from_left = from_right = lax.ppermute(data, axis, r_pairs + l_pairs)
            from_left = jnp.where(i <= k, from_left, jnp.zeros_like(from_left))
            from_right = jnp.where(i >= n - 1 - k, from_right, jnp.zeros_like(from_right))
        else:
            r_data, l_data = block(i + n - k), block(i - n + k)
            if from_left is not None:
                r_data = (r_data.astype(F32) + from_left.astype(F32)).astype(BF16)
                l_data = (l_data.astype(F32) + from_right.astype(F32)).astype(BF16)
            from_left = lax.ppermute(r_data, axis, r_pairs)
            from_right = lax.ppermute(l_data, axis, l_pairs)
        if k < n - 1:
            early.append((from_left, from_right))
    return block(i).astype(F32) + from_left.astype(F32) + from_right.astype(F32), early


def routed_scatter(parts, axis):
    n, i = lax.axis_size(axis), lax.axis_index(axis)
    width = parts.shape[1] // n

    def block(j):
        return lax.dynamic_slice(parts, (0, (j % n) * width), (parts.shape[0], width))

    total = block(i).astype(F32)
    for k in range(1, n):
        total = total + lax.ppermute(block(i + k), axis, [(j, (j + k) % n) for j in range(n)]).astype(F32)
    return total


def small_gather(x, axis):
    n = lax.axis_size(axis)
    blocks = [x] + [lax.ppermute(x, axis, [(j, (j + s) % n) for j in range(n)]) for s in range(1, n)]
    return place(blocks, axis, x.dtype)


def swap_sum(x, axis):
    n = lax.axis_size(axis)
    g = 1
    while g < n:
        x = x + lax.ppermute(x, axis, [(j, j ^ g) for j in range(n)])
        g *= 2
    return x


def states_before(local, log_block, axis):
    n, b = lax.axis_size(axis), lax.axis_index(axis)
    total, prefix, g = local, jnp.zeros_like(local), 1
    while g < n:
        got = lax.ppermute(total.astype(BF16), axis, [(j, j ^ g) for j in range(n)]).astype(F32)
        upper = (b // g) % 2 == 1
        mine = jnp.exp((b % g).astype(F32) * log_block)[:, None, None]
        whole = jnp.exp(g * log_block)[:, None, None]
        prefix = jnp.where(upper, prefix + mine * got, prefix)
        total = jnp.where(upper, whole * got + total, whole * total + got)
        g *= 2
    return prefix


def states_after(local, log_block, axis):
    first = None
    n, b = lax.axis_size(axis), lax.axis_index(axis)
    total, suffix, g = local, jnp.zeros_like(local), 1
    while g < n:
        got = lax.ppermute(total.astype(BF16), axis, [(j, j ^ g) for j in range(n)]).astype(F32)
        first = got if first is None else first
        upper = (b // g) % 2 == 1
        mine = jnp.exp((g - 1 - b % g).astype(F32) * log_block)[:, None, None]
        whole = jnp.exp(g * log_block)[:, None, None]
        suffix = jnp.where(upper, suffix, suffix + mine * got)
        total = jnp.where(upper, got + whole * total, total + whole * got)
        g *= 2
    return suffix, first


def pair_swap(x):
    lane = lax.broadcasted_iota(jnp.int32, x.shape, 1)
    width = x.shape[1]
    return jnp.where(lane % 2 == 0, pltpu.roll(x, width - 1, 1), pltpu.roll(x, 1, 1))


def side_by_side(*arrays):
    rows = arrays[0].shape[0]
    widths = [a.shape[1] for a in arrays]

    def kernel(*refs):
        column = 0
        for ref, width in zip(refs, widths):
            refs[-1][:, column : column + width] = ref[...]
            column += width

    block = min(rows, 64)
    return pl.pallas_call(
        kernel,
        grid=(rows // block,),
        in_specs=[pl.BlockSpec((block, width), lambda r: (r, 0)) for width in widths],
        out_specs=pl.BlockSpec((block, sum(widths)), lambda r: (r, 0)),
        out_shape=jax.ShapeDtypeStruct((rows, sum(widths)), arrays[0].dtype),
        cost_estimate=pl.CostEstimate(flops=0, bytes_accessed=4 * rows * sum(widths), transcendentals=0),
        name="join",
    )(*arrays)


def gathered(at, refs, k, rows=slice(None)):
    if k == 0:
        return refs[0][rows, :]
    return jnp.where(at >= k, refs[2 * k - 1][rows, :], refs[2 * k][rows, :])


def columns_of(at, n, k, width):
    return pl.ds(pl.multiple_of(((at + n - k) % n) * width, width), width)


def fill_normed(at, refs, gain_ref, full_ref):
    n = len(refs) // 2 + 1
    width = refs[0].shape[1]
    blocks = [gathered(at, refs, k).astype(F32) for k in range(n)]
    squares = sum(jnp.sum(b * b, axis=1, keepdims=True) for b in blocks)
    scale = lax.rsqrt(squares / (n * width) + EPSILON)
    for k, b in enumerate(blocks):
        where = columns_of(at, n, k, width)
        full_ref[:, where] = (b * scale * gain_ref[:, where]).astype(BF16)
    return scale


def flat(x, pairs):
    return [x] + [p for pair in pairs for p in pair]


def project_kernel(heads, count, at_ref, lg_ref, gain_ref, w_ref, cos_ref, sin_ref, *refs):
    blocks, (full_ref, scale_ref, q_ref, k_ref, v_ref, state_ref) = refs[:count], refs[count:]
    step = pl.program_id(0)
    rows = pl.num_programs(0) * BLOCK
    scale_ref[...] = fill_normed(at_ref[0], blocks, gain_ref, full_ref)
    x = full_ref[...]
    qk = heads * HK
    c, s = cos_ref[...], sin_ref[...]
    k_out = nn(x, w_ref[:, qk : 2 * qk])
    v_out = nn(x, w_ref[:, 2 * qk :]).astype(BF16)
    q_out = nn(x, w_ref[:, :qk])
    v_ref[...] = v_out
    m = lax.broadcasted_iota(jnp.int32, (BLOCK, 1), 0) + step * BLOCK
    for h in range(heads):
        at = slice(h * HK, (h + 1) * HK)
        one = k_out[:, at]
        key = ((one * c + pair_swap(one) * s) * (1.0 / math.sqrt(HK))).astype(BF16)
        k_ref[:, at] = key
        tail = jnp.exp((rows - m).astype(F32) * lg_ref[h])
        add = tn((key.astype(F32) * tail).astype(BF16), v_out[:, h * HV : (h + 1) * HV])

        @pl.when(step == 0)
        def _(h=h, add=add):
            state_ref[h] = add

        @pl.when(step > 0)
        def _(h=h, add=add):
            state_ref[h] += add

        one = q_out[:, at]
        q_ref[:, at] = (one * c + pair_swap(one) * s).astype(BF16)


def project(at, log_gamma, gain, w, x, pairs, heads, cosine, sine):
    rows, width = x.shape
    features = w.shape[0]
    outs = 2 * heads * HK + heads * HV
    blocks = flat(x, pairs)

    def by_rows(columns):
        return pl.BlockSpec((BLOCK, columns), lambda r: (r, 0))

    return pl.pallas_call(
        lambda *refs: project_kernel(heads, len(blocks), *refs),
        grid=(rows // BLOCK,),
        in_specs=[
            pl.BlockSpec(memory_space=pltpu.SMEM),
            pl.BlockSpec(memory_space=pltpu.SMEM),
            pl.BlockSpec((1, features), lambda r: (0, 0)),
            pl.BlockSpec((features, outs), lambda r: (0, 0)),
            by_rows(HK),
            by_rows(HK),
            *[by_rows(width)] * len(blocks),
        ],
        out_specs=[
            by_rows(features),
            by_rows(1),
            by_rows(heads * HK),
            by_rows(heads * HK),
            by_rows(heads * HV),
            pl.BlockSpec((heads, HK, HV), lambda r: (0, 0, 0)),
        ],
        out_shape=[
            jax.ShapeDtypeStruct((rows, features), BF16),
            jax.ShapeDtypeStruct((rows, 1), F32),
            jax.ShapeDtypeStruct((rows, heads * HK), BF16),
            jax.ShapeDtypeStruct((rows, heads * HK), BF16),
            jax.ShapeDtypeStruct((rows, heads * HV), BF16),
            jax.ShapeDtypeStruct((heads, HK, HV), F32),
        ],
        cost_estimate=pl.CostEstimate(
            flops=2 * rows * features * outs, bytes_accessed=2 * features * outs + 12 * rows * features, transcendentals=0
        ),
        name="proj",
    )(at, log_gamma, gain, w, cosine, sine, *blocks)


def product_kernel(x_ref, w_ref, out_ref):
    out_ref[...] = nn(x_ref[...], w_ref[...])


def product(x, w, at, columns):
    rows, inner = x.shape
    return pl.pallas_call(
        product_kernel,
        grid=(rows // BLOCK,),
        in_specs=[
            pl.BlockSpec((BLOCK, inner), lambda r: (r, 0)),
            pl.BlockSpec((inner, columns), lambda r: (0, at)),
        ],
        out_specs=pl.BlockSpec((BLOCK, columns), lambda r: (r, 0)),
        out_shape=jax.ShapeDtypeStruct((rows, columns), F32),
        cost_estimate=pl.CostEstimate(
            flops=2 * rows * inner * columns, bytes_accessed=2 * inner * columns + 8 * rows * columns, transcendentals=0
        ),
        name="prod",
    )(x, w)


def mlp_kernel(units, count, at_ref, gain_ref, w_ref, *refs):
    blocks, grads = refs[:count], refs[count : 2 * count]
    full_ref, hidden_ref, acts_ref, grad_ref, scale_ref, inner_ref, back_ref = refs[-7:]
    at, n = at_ref[0], count // 2 + 1
    scale_ref[...] = fill_normed(at, blocks, gain_ref, full_ref)
    for k in range(n):
        grad_ref[:, columns_of(at, n, k, grads[0].shape[1])] = gathered(at, grads, k)
    x = full_ref[...]
    gate = nn(x, w_ref[:, :units])
    up = nn(x, w_ref[:, units : 2 * units])
    grad = nn(grad_ref[...], w_ref[:, 2 * units :])
    cdf = 0.5 * (1.0 + lax.erf(gate * math.sqrt(0.5)))
    gelu = gate * cdf
    density = jnp.exp(-0.5 * gate * gate) * (1.0 / math.sqrt(2.0 * math.pi))
    hidden_ref[...] = (gelu * up).astype(BF16)
    g_gate = (grad * up * (cdf + gate * density)).astype(BF16)
    g_up = (grad * gelu).astype(BF16)
    acts_ref[:, :units] = g_gate
    acts_ref[:, units:] = g_up
    inner_ref[...] = jnp.sum(g_gate.astype(F32) * gate + g_up.astype(F32) * up, axis=1, keepdims=True)
    back_ref[...] = (nt(g_gate, w_ref[:, :units]) + nt(g_up, w_ref[:, units : 2 * units])).astype(BF16)


def mlp(at, gain, w, part, grads, x, pairs, shared):
    rows, width = x.shape
    features = w.shape[0]
    units = w.shape[1] // 3
    blocks = flat(x, pairs)
    steps = rows // BLOCK
    total = grads[0].shape[0]

    def by_rows(columns):
        return pl.BlockSpec((BLOCK, columns), lambda r: (r, 0))

    def own_rows(columns):
        return pl.BlockSpec((BLOCK, columns), lambda r: (part * steps + r, 0))

    return pl.pallas_call(
        lambda *refs: mlp_kernel(units, len(blocks), *refs),
        grid=(steps,),
        in_specs=[
            pl.BlockSpec(memory_space=pltpu.SMEM),
            pl.BlockSpec((1, features), lambda r: (0, 0)),
            pl.BlockSpec((features, 3 * units), lambda r: (0, 0)),
            *[by_rows(width)] * len(blocks),
            *[own_rows(width)] * len(grads),
            *[pl.BlockSpec(memory_space=pl.ANY)] * len(shared),
        ],
        out_specs=[
            own_rows(features),
            own_rows(units),
            own_rows(2 * units),
            own_rows(features),
            by_rows(1),
            by_rows(1),
            by_rows(features),
        ],
        out_shape=[
            jax.ShapeDtypeStruct((total, features), BF16),
            jax.ShapeDtypeStruct((total, units), BF16),
            jax.ShapeDtypeStruct((total, 2 * units), BF16),
            jax.ShapeDtypeStruct((total, features), BF16),
            jax.ShapeDtypeStruct((rows, 1), F32),
            jax.ShapeDtypeStruct((rows, 1), F32),
            jax.ShapeDtypeStruct((rows, features), BF16),
        ],
        input_output_aliases={3 + 2 * len(blocks) + i: i for i in range(len(shared))},
        cost_estimate=pl.CostEstimate(
            flops=10 * rows * features * units,
            bytes_accessed=6 * features * units + 14 * rows * features,
            transcendentals=2 * rows * units,
        ),
        name="mlp",
    )(at, gain, w, *blocks, *grads, *shared)


def decay_vectors(log_gamma):
    down = lax.broadcasted_iota(jnp.int32, (BLOCK, 1), 0).astype(F32)
    across = lax.broadcasted_iota(jnp.int32, (1, BLOCK), 1).astype(F32)
    return jnp.exp(down * log_gamma), jnp.exp(-across * log_gamma)


def block_decay(scores, r, j, log_gamma, down, across):
    out = scores * (down * jnp.exp(log_gamma * (BLOCK * (r - j)))) * across
    if r == j:
        n = lax.broadcasted_iota(jnp.int32, scores.shape, 0)
        m = lax.broadcasted_iota(jnp.int32, scores.shape, 1)
        out = jnp.where(n >= m, out, 0.0)
    return out.astype(BF16)


def cut(r):
    return slice(r * BLOCK, (r + 1) * BLOCK)


def forward_kernel(first, count, lg_ref, q_ref, k_ref, v_ref, gate_ref, state_ref, w_ref, *refs):
    gated_ref, ret_ref, out_ref, acc_ref = refs[-4:]
    head = pl.program_id(0)
    log_gamma = lg_ref[head]
    down, across = decay_vectors(log_gamma)
    state = state_ref[0]
    for at in range(count):
        r = first + at
        q = q_ref[cut(at), :]
        ret = nn(q, state) * (down * jnp.exp(log_gamma * (BLOCK * r)))
        for j in range(r + 1):
            weights = block_decay(nt(q, k_ref[cut(j), :]), r, j, log_gamma, down, across)
            ret = ret + nn(weights, v_ref[cut(j), :])
        ret_ref[cut(at), :] = ret
        scale = lax.rsqrt(jnp.mean(ret * ret, axis=1, keepdims=True) + EPSILON)
        gate = gate_ref[cut(at), :]
        gated = (gate / (1.0 + jnp.exp(-gate)) * (ret * scale)).astype(BF16)
        gated_ref[cut(at), :] = gated
        out = nt(gated, w_ref[...])

        @pl.when(head == 0)
        def _(at=at, out=out):
            acc_ref[cut(at), :] = out

        @pl.when(head > 0)
        def _(at=at, out=out):
            acc_ref[cut(at), :] += out

        @pl.when(head == pl.num_programs(0) - 1)
        def _(at=at):
            out_ref[cut(at), :] = acc_ref[cut(at), :].astype(BF16)


def retention_forward(part, parts, log_gamma, q, k, v, gate, state, w, first_column, shared):
    rows = q.shape[0]
    heads = q.shape[1] // HK
    features = w.shape[0]
    own = rows // parts
    seen = own * (part + 1)
    count = own // BLOCK
    pairs = sum(part * count + at + 1 for at in range(count))
    flops = heads * (pairs * 2 * BLOCK * BLOCK * (HK + HV) + 2 * own * HK * HV + 2 * own * HV * features)
    head_out = pl.BlockSpec((own, HV), lambda h: (part, h))
    return pl.pallas_call(
        lambda *refs: forward_kernel(part * count, count, *refs),
        grid=(heads,),
        in_specs=[
            pl.BlockSpec(memory_space=pltpu.SMEM),
            pl.BlockSpec((own, HK), lambda h: (part, h)),
            pl.BlockSpec((seen, HK), lambda h: (0, h)),
            pl.BlockSpec((seen, HV), lambda h: (0, h)),
            pl.BlockSpec((own, HV), lambda h: (part, h)),
            pl.BlockSpec((1, HK, HV), lambda h: (h, 0, 0)),
            pl.BlockSpec((features, HV), lambda h: (0, first_column // HV + h)),
            *[pl.BlockSpec(memory_space=pl.ANY)] * len(shared),
        ],
        out_specs=[head_out, head_out, pl.BlockSpec((own, features), lambda h: (0, 0))],
        input_output_aliases={7 + i: i for i in range(len(shared))},
        out_shape=[
            jax.ShapeDtypeStruct((rows, heads * HV), BF16),
            jax.ShapeDtypeStruct((rows, heads * HV), F32),
            jax.ShapeDtypeStruct((own, features), BF16),
        ],
        scratch_shapes=[pltpu.VMEM((own, features), F32)],
        cost_estimate=pl.CostEstimate(flops=flops, bytes_accessed=20 * own * heads * HV, transcendentals=own * heads * HV),
        name="fwd",
    )(log_gamma, q, k, v, gate, state, w, *shared)


def gate_backward_kernel(first, count, n_blocks, at_ref, lg_ref, q_ref, w_ref, gate_ref, ret_ref, *refs):
    blocks, (g_gate_ref, g_ret_ref, full_ref, state_ref, inner_ref) = refs[:n_blocks], refs[-5:]
    head = pl.program_id(0)
    log_gamma = lg_ref[head]
    down, _ = decay_vectors(log_gamma)
    n = n_blocks // 2 + 1
    width = blocks[0].shape[1]
    here = at_ref[0]
    state = None
    for at in range(count):
        r = first + at

        @pl.when(head == 0)
        def _(at=at):
            for k in range(n):
                full_ref[cut(at), columns_of(here, n, k, width)] = gathered(here, blocks, k, cut(at))

        grad = nn(full_ref[cut(at), :], w_ref[...])
        ret = ret_ref[cut(at), :]
        gate = gate_ref[cut(at), :]
        scale = lax.rsqrt(jnp.mean(ret * ret, axis=1, keepdims=True) + EPSILON)
        grouped = ret * scale
        sig = 1.0 / (1.0 + jnp.exp(-gate))
        g_gate = (grad * grouped * (sig * (1.0 + gate * (1.0 - sig)))).astype(BF16)
        g = grad * (gate * sig)
        g_ret = (scale * (g - grouped * jnp.mean(g * grouped, axis=1, keepdims=True))).astype(BF16)
        g_gate_ref[cut(at), :] = g_gate
        g_ret_ref[cut(at), :] = g_ret
        inner_ref[0, cut(at), :] = jnp.sum(g_gate.astype(F32) * gate, axis=1, keepdims=True)
        q = (q_ref[cut(at), :].astype(F32) * (down * jnp.exp(log_gamma * (BLOCK * r)))).astype(BF16)
        add = tn(q, g_ret)
        state = add if state is None else state + add
    state_ref[0] = state


def gate_backward(part, parts, here, log_gamma, q, w, first_column, gate, ret, x, pairs, shared):
    rows = q.shape[0]
    heads = q.shape[1] // HK
    features = w.shape[0]
    own = rows // parts
    count = own // BLOCK
    blocks = flat(x, pairs)
    head_out = pl.BlockSpec((own, HV), lambda h: (part, h))
    return pl.pallas_call(
        lambda *refs: gate_backward_kernel(part * count, count, len(blocks), *refs),
        grid=(heads,),
        in_specs=[
            pl.BlockSpec(memory_space=pltpu.SMEM),
            pl.BlockSpec(memory_space=pltpu.SMEM),
            pl.BlockSpec((own, HK), lambda h: (part, h)),
            pl.BlockSpec((features, HV), lambda h: (0, first_column // HV + h)),
            head_out,
            head_out,
            *[pl.BlockSpec((own, x.shape[1]), lambda h: (0, 0))] * len(blocks),
            *[pl.BlockSpec(memory_space=pl.ANY)] * len(shared),
        ],
        out_specs=[
            head_out,
            head_out,
            pl.BlockSpec((own, features), lambda h: (part, 0)),
            pl.BlockSpec((1, HK, HV), lambda h: (h, 0, 0)),
            pl.BlockSpec((1, own, 1), lambda h: (h, 0, 0)),
        ],
        input_output_aliases={6 + len(blocks) + i: i for i in range(len(shared))},
        out_shape=[
            jax.ShapeDtypeStruct((rows, heads * HV), BF16),
            jax.ShapeDtypeStruct((rows, heads * HV), BF16),
            jax.ShapeDtypeStruct((rows, features), BF16),
            jax.ShapeDtypeStruct((heads, HK, HV), F32),
            jax.ShapeDtypeStruct((heads, own, 1), F32),
        ],
        cost_estimate=pl.CostEstimate(
            flops=heads * 2 * own * HV * (HK + features),
            bytes_accessed=16 * own * heads * HV,
            transcendentals=own * heads * HV,
        ),
        name="gate",
    )(here, log_gamma, q, w, gate, ret, *blocks, *shared)


def backward_kernel(total, lg_ref, q_ref, k_ref, v_ref, state_in_ref, state_grad_ref, cos_ref, sin_ref, *refs):
    g_ref, gate_ref, all_ref, inner_ref, acc_k, acc_v, g_q_ref, g_k_ref, g_v_ref, sems = refs
    head, heads = pl.program_id(0), pl.num_programs(0)
    log_gamma = lg_ref[head]
    down, across = decay_vectors(log_gamma)
    state_in, state_grad = state_in_ref[0], state_grad_ref[0]
    key_scale = 1.0 / math.sqrt(HK)

    def send(ref, column, width, i):
        target = all_ref.at[:, pl.ds(pl.multiple_of(column, HK), width)]
        return pltpu.make_async_copy(ref, target, sems.at[i])

    gates = send(gate_ref, heads * (2 * HK + HV) + head * HV, HV, 0)
    gates.start()

    def put(ref, r, x, factor):
        turned = x * cos_ref[cut(r), :] - pair_swap(x) * sin_ref[cut(r), :]
        ref[cut(r), :] = (turned * factor).astype(BF16)

    for r in range(total):
        g = g_ref[cut(r), :]
        q, k, v = q_ref[cut(r), :], k_ref[cut(r), :], v_ref[cut(r), :]
        tail = down_tail(log_gamma, total * BLOCK - r * BLOCK)
        acc_v[cut(r), :] = nn((k.astype(F32) * tail).astype(BF16), state_grad)
        acc_k[cut(r), :] = nt(v, state_grad) * tail
        g_q = nt(g, state_in) * (down * jnp.exp(log_gamma * (BLOCK * r)))
        for j in range(r + 1):
            kj, vj = k_ref[cut(j), :], v_ref[cut(j), :]
            weights = block_decay(nt(q, kj), r, j, log_gamma, down, across)
            g_scores = block_decay(nt(g, vj), r, j, log_gamma, down, across)
            acc_v[cut(j), :] += tn(weights, g)
            acc_k[cut(j), :] += tn(g_scores, q)
            g_q = g_q + nn(g_scores, kj)
        inner_ref[0, cut(r), :] = jnp.sum(g_q * q.astype(F32), axis=1, keepdims=True)
        put(g_q_ref, r, g_q, 1.0)
    for r in range(total):
        g_k = acc_k[cut(r), :]
        g_v = acc_v[cut(r), :].astype(BF16)
        g_v_ref[cut(r), :] = g_v
        inner_ref[0, cut(r), :] += jnp.sum(g_k * k_ref[cut(r), :].astype(F32), axis=1, keepdims=True) + jnp.sum(
            g_v.astype(F32) * v_ref[cut(r), :].astype(F32), axis=1, keepdims=True
        )
        put(g_k_ref, r, g_k, key_scale)
    copies = [
        send(g_q_ref, head * HK, HK, 1),
        send(g_k_ref, (heads + head) * HK, HK, 2),
        send(g_v_ref, 2 * heads * HK + head * HV, HV, 3),
    ]
    for copy in copies:
        copy.start()
    for copy in [gates] + copies:
        copy.wait()


def down_tail(log_gamma, start):
    m = lax.broadcasted_iota(jnp.int32, (BLOCK, 1), 0).astype(F32)
    return jnp.exp((start - m) * log_gamma)


def retention_backward(log_gamma, q, k, v, state_in, state_grad, cosine, sine, g_ret, g_gate):
    rows = q.shape[0]
    heads = q.shape[1] // HK
    blocks = rows // BLOCK
    pairs = blocks * (blocks + 1) // 2
    flops = heads * 2 * (pairs * BLOCK * BLOCK * (3 * HK + 2 * HV) + 3 * rows * HK * HV)
    head_keys = pl.BlockSpec((rows, HK), lambda h: (0, h))
    head_values = pl.BlockSpec((rows, HV), lambda h: (0, h))
    head_state = pl.BlockSpec((1, HK, HV), lambda h: (h, 0, 0))
    table = pl.BlockSpec((rows, HK), lambda h: (0, 0))
    return pl.pallas_call(
        lambda *refs: backward_kernel(blocks, *refs),
        grid=(heads,),
        in_specs=[
            pl.BlockSpec(memory_space=pltpu.SMEM),
            head_keys,
            head_keys,
            head_values,
            head_state,
            head_state,
            table,
            table,
            head_values,
            head_values,
        ],
        out_specs=[pl.BlockSpec(memory_space=pl.ANY), pl.BlockSpec((1, rows, 1), lambda h: (h, 0, 0))],
        out_shape=[
            jax.ShapeDtypeStruct((rows, heads * 2 * (HK + HV)), BF16),
            jax.ShapeDtypeStruct((heads, rows, 1), F32),
        ],
        scratch_shapes=[
            pltpu.VMEM((rows, HK), F32),
            pltpu.VMEM((rows, HV), F32),
            pltpu.VMEM((rows, HK), BF16),
            pltpu.VMEM((rows, HK), BF16),
            pltpu.VMEM((rows, HV), BF16),
            pltpu.SemaphoreType.DMA((4,)),
        ],
        cost_estimate=pl.CostEstimate(flops=flops, bytes_accessed=24 * rows * heads * HK, transcendentals=0),
        name="bwd",
    )(log_gamma, q, k, v, state_in, state_grad, cosine, sine, g_ret, g_gate)


def on_device(
    layer_input,
    gain_attn,
    w_query,
    w_key,
    w_value,
    w_retgate,
    w_out,
    gain_mlp,
    w_gate,
    w_up,
    w_down,
    cotangent,
):
    data = (DP, CTX)
    rows, width = layer_input.shape
    n_tp, at_tp = lax.axis_size(TP), lax.axis_index(TP)
    features = width * n_tp
    heads = w_query.shape[1] // HK
    units = w_gate.shape[1]

    parts = 2
    own = rows // parts
    cuts = [slice(c * own, (c + 1) * own) for c in range(parts)]

    qk = heads * HK
    vw = heads * HV
    attn_shard = side_by_side(w_query, w_key, w_value, w_retgate, w_out)
    attn_full = lax.all_gather(attn_shard, data, axis=0, tiled=True)

    gains = small_gather(jnp.stack([gain_attn, gain_mlp]), TP)

    log_gamma = jnp.log1p(-jnp.exp2(-5.0 - (at_tp * heads + jnp.arange(heads)).astype(F32)))
    log_block = rows * log_gamma
    positions = lax.axis_index(CTX) * rows + jnp.arange(rows)
    frequencies = jnp.exp(-math.log(10000.0) * jnp.linspace(0.0, 1.0, HK // 2, dtype=F32))
    angles = positions.astype(F32)[:, None] * jnp.repeat(frequencies, 2)[None, :]
    cosine = jnp.cos(angles)
    sine = jnp.sin(angles) * jnp.where(jnp.arange(HK) % 2 == 0, -1.0, 1.0)[None, :]
    here = at_tp.reshape(1)
    mlp_shard = side_by_side(w_gate, w_up, w_down)

    pairs = line_gather(layer_input, TP, (cosine, sine, mlp_shard, log_gamma, gains))
    normed, scale_attn, q, k, v, local_state = project(
        here, log_gamma, gains[0:1], attn_full, layer_input, pairs, heads, cosine, sine
    )
    cot = after(cotangent, pairs[-1][0])
    cot_blocks = flat(cot, line_gather(cot, TP))
    gate_pre = product(after(normed, local_state), attn_full, (2 * qk + vw) // vw, vw)
    state_in = states_before(local_state, log_block, CTX).astype(BF16)
    mlp_full = lax.all_gather(after(mlp_shard, state_in), data, axis=0, tiled=True)
    heads_out, branch = [], []
    for c in range(parts):
        *heads_out, out = retention_forward(
            c, parts, log_gamma, q, k, v, gate_pre, state_in, attn_full, 2 * qk + 2 * vw, heads_out
        )
        branch.append(out)
    gated, retained = heads_out

    devices = math.prod(lax.axis_size(axis) for axis in data)

    x_own = layer_input.astype(F32)
    middle, mid_pairs, scale_mlp, inner_mlp, back, grad_middle, grad_own, grad_pairs = ([] for _ in range(8))
    gain_mlp_sum = 0.0

    def norm_back(own_rows, scale, gain, inner, grad_normed):
        hat = own_rows * scale
        grad = scale * (grad_normed * gain[None, :] - hat * (inner[:, None] / features))
        return grad, jnp.sum(grad_normed * hat, axis=0)

    def row_total(inner):
        lanes = 128
        return swap_sum(inner.reshape(-1, lanes), TP).reshape(-1)

    early = ()
    for c in range(parts):
        total, steps = line_scatter(after(branch[c], *early), TP)
        early = steps[-1]
        if c:
            total = after(total, mid_pairs[c - 1][0][0])
        middle.append(x_own[cuts[c]] + total)
        mid_pairs.append(line_gather(middle[c].astype(BF16), TP))
    shared = []
    for c in range(parts):
        *results, scale, inner, out = mlp(
            here, gains[1:2], mlp_full, c, cot_blocks, middle[c].astype(BF16), mid_pairs[c], shared
        )
        shared = results
        scale_mlp.append(scale)
        inner_mlp.append(inner[:, 0])
        back.append(out)
    normed_mlp, hidden, grad_acts, grad_full = shared
    early = ()
    for c in range(parts):
        inner = row_total(inner_mlp[c])
        total, steps = line_scatter(after(back[c], *early), TP)
        early = steps[-1]
        if c:
            total = after(total, grad_pairs[c - 1][0][0])
        grad_mid, gain_sum = norm_back(middle[c], scale_mlp[c], gain_mlp, inner, total)
        gain_mlp_sum = gain_mlp_sum + gain_sum
        grad_middle.append(cotangent[cuts[c]].astype(F32) + grad_mid)
        grad_own.append(grad_middle[c].astype(BF16))
        grad_pairs.append(line_gather(grad_own[c], TP))
    grad_down = tn(grad_full, hidden).astype(BF16)
    grad_gate_up = tn(after(normed_mlp, grad_down), grad_acts).astype(BF16)
    mlp_parts = nt(hidden, mlp_full[:, 2 * units :]).astype(BF16)

    grad_own[0] = after(grad_own[0], grad_gate_up, grad_down)
    mlp_out = routed_scatter(after(mlp_parts, grad_pairs[-1][-1][0]), TP)
    layer_output = (jnp.concatenate(middle) + mlp_out).astype(BF16)
    shared = []
    partial_state = 0.0
    inner_attn = []
    for c in range(parts):
        *shared, ps, inner = gate_backward(
            c,
            parts,
            here,
            log_gamma,
            q,
            attn_full,
            2 * qk + 2 * vw,
            gate_pre,
            retained,
            grad_own[c],
            grad_pairs[c],
            shared,
        )
        partial_state = partial_state + ps
        inner_attn.append(jnp.sum(inner[:, :, 0], axis=0))
    g_gate, g_ret, grad_attn = shared
    state_grad, got = states_after(partial_state, log_block, CTX)
    state_grad = state_grad.astype(BF16)
    grad_out = tn(after(grad_attn, got), gated).astype(BF16)
    grad_retgate = tn(normed, after(g_gate, got)).astype(BF16)
    grad_heads = jnp.concatenate([g.reshape(devices, -1, vw) for g in (grad_retgate, grad_out)], axis=1)
    grads_attn, inner = retention_backward(
        log_gamma, q, k, v, state_in, after(state_grad, grad_heads), cosine, sine, g_ret, g_gate
    )
    inner_attn = jnp.concatenate(inner_attn) + jnp.sum(inner[:, :, 0], axis=0)
    in_full = attn_full[:, : 2 * qk + 2 * vw]
    back = []
    for c in range(parts):
        rows_grads = after(grads_attn, *back, *([grad_qkv_w] if c else []))
        back.append(nt(rows_grads[cuts[c]], in_full).astype(BF16))
        if c == 0:
            grad_qkv_w = tn(normed, after(grads_attn, *back)[:, : 2 * qk + vw]).astype(BF16)
    inner_attn = row_total(inner_attn)
    grad_input, gain_attn_sum = [], 0.0
    early = ()
    for c in range(parts):
        total, steps = line_scatter(after(back[c], *early), TP)
        early = steps[0]
        grad_in, gain_sum = norm_back(x_own[cuts[c]], scale_attn[cuts[c]], gain_attn, inner_attn[cuts[c]], total)
        grad_input.append((grad_middle[c] + grad_in).astype(BF16))
        gain_attn_sum = gain_attn_sum + gain_sum
    grad_input = jnp.concatenate(grad_input)

    def shard(grad):
        return lax.psum_scatter(grad, data, scatter_dimension=0, tiled=True).astype(F32)

    s_down = shard(grad_down)
    s_gate_up = shard(grad_gate_up)
    s_retgate, s_out = jnp.split(shard(grad_heads)[0], 2)
    s_qkv = shard(grad_qkv_w)
    s_query, s_key, s_value = s_qkv[:, :qk], s_qkv[:, qk : 2 * qk], s_qkv[:, 2 * qk :]
    gain_sums = swap_sum(swap_sum(jnp.stack([gain_attn_sum, gain_mlp_sum]), CTX), DP)
    return (
        layer_output,
        grad_input,
        gain_sums[0],
        s_query,
        s_key,
        s_value,
        s_retgate,
        s_out,
        gain_sums[1],
        s_gate_up[:, :units],
        s_gate_up[:, units:],
        s_down,
    )


def solution(mesh):
    tokens = P((DP, CTX), TP)
    gain = P(TP)
    weight = P((DP, CTX), TP)

    return jax.shard_map(
        on_device,
        mesh=mesh,
        in_specs=(tokens, gain, weight, weight, weight, weight, weight, gain, weight, weight, weight, tokens),
        out_specs=(tokens, tokens, gain, weight, weight, weight, weight, weight, gain, weight, weight, weight),
        check_vma=False,
    )
```

```python
import math

import jax
import jax.numpy as jnp
from jax import lax
from jax.experimental import pallas as pl
from jax.experimental.pallas import tpu as pltpu
from jax.sharding import PartitionSpec as P


HK = 256
HV = 512
EPSILON = 1e-06
BLOCK = 512
TP, CTX, DP = "tp", "ctx", "dp"
F32 = jnp.float32
BF16 = jnp.bfloat16


def nn(a, b):
    return lax.dot_general(a, b, (((1,), (0,)), ((), ())), preferred_element_type=F32)


def tn(a, b):
    return lax.dot_general(a, b, (((0,), (0,)), ((), ())), preferred_element_type=F32)


def nt(a, b):
    return lax.dot_general(a, b, (((1,), (1,)), ((), ())), preferred_element_type=F32)


def after(x, *before):
    return lax.optimization_barrier((x, *before))[0]


def right(lo, hi):
    return [(i, i + 1) for i in range(lo, hi)]


def left(lo, hi):
    return [(i, i - 1) for i in range(hi, lo, -1)]


def line_gather(x, axis, before=()):
    n, i = lax.axis_size(axis), lax.axis_index(axis)
    rights, lefts = [x], [x]
    for k in range(1, n):
        r_pairs = right(k - 1, n - 1)
        l_pairs = left(0, n - k)
        if k == 2 and before:
            rights[-1] = after(rights[-1], *before)
        if 2 * k > n + 1:
            both = lax.ppermute(jnp.where(i >= k - 1, rights[-1], lefts[-1]), axis, r_pairs + l_pairs)
            rights.append(both)
            lefts.append(both)
        else:
            rights.append(lax.ppermute(rights[-1], axis, r_pairs))
            lefts.append(lax.ppermute(lefts[-1], axis, l_pairs))
    return [(rights[k], lefts[n - k]) for k in range(1, n)]


def place(blocks, axis, dtype):
    n, i = lax.axis_size(axis), lax.axis_index(axis)
    rows, width = blocks[0].shape
    full = jnp.zeros((rows, n * width), dtype)
    for k, block in enumerate(blocks):
        at = ((i - k) % n) * width
        full = lax.dynamic_update_slice(full, block.astype(dtype), (0, at))
    return full


def line_scatter(parts, axis):
    n, i = lax.axis_size(axis), lax.axis_index(axis)
    width = parts.shape[1] // n

    def block(j):
        return lax.dynamic_slice(parts, (0, jnp.clip(j, 0, n - 1) * width), (parts.shape[0], width))

    from_left = from_right = None
    early = []
    for k in range(1, n):
        r_pairs = right(0, k)
        l_pairs = left(n - 1 - k, n - 1)
        if 2 * k < n - 1:
            data = block(jnp.where(i < k, i + n - k, i - n + k))
            if from_left is not None:
                data = (data.astype(F32) + jnp.where(i < k, from_left, from_right).astype(F32)).astype(BF16)
            from_left = from_right = lax.ppermute(data, axis, r_pairs + l_pairs)
            from_left = jnp.where(i <= k, from_left, jnp.zeros_like(from_left))
            from_right = jnp.where(i >= n - 1 - k, from_right, jnp.zeros_like(from_right))
        else:
            r_data, l_data = block(i + n - k), block(i - n + k)
            if from_left is not None:
                r_data = (r_data.astype(F32) + from_left.astype(F32)).astype(BF16)
                l_data = (l_data.astype(F32) + from_right.astype(F32)).astype(BF16)
            from_left = lax.ppermute(r_data, axis, r_pairs)
            from_right = lax.ppermute(l_data, axis, l_pairs)
        if k < n - 1:
            early.append((from_left, from_right))
    return block(i).astype(F32) + from_left.astype(F32) + from_right.astype(F32), early


def routed_scatter(parts, axis):
    n, i = lax.axis_size(axis), lax.axis_index(axis)
    width = parts.shape[1] // n

    def block(j):
        return lax.dynamic_slice(parts, (0, (j % n) * width), (parts.shape[0], width))

    total = block(i).astype(F32)
    for k in range(1, n):
        total = total + lax.ppermute(block(i + k), axis, [(j, (j + k) % n) for j in range(n)]).astype(F32)
    return total


def small_gather(x, axis):
    n = lax.axis_size(axis)
    blocks = [x] + [lax.ppermute(x, axis, [(j, (j + s) % n) for j in range(n)]) for s in range(1, n)]
    return place(blocks, axis, x.dtype)


def swap_sum(x, axis):
    n = lax.axis_size(axis)
    g = 1
    while g < n:
        x = x + lax.ppermute(x, axis, [(j, j ^ g) for j in range(n)])
        g *= 2
    return x


def states_before(local, log_block, axis):
    n, b = lax.axis_size(axis), lax.axis_index(axis)
    total, prefix, g = local, jnp.zeros_like(local), 1
    while g < n:
        got = lax.ppermute(total.astype(BF16), axis, [(j, j ^ g) for j in range(n)]).astype(F32)
        upper = (b // g) % 2 == 1
        mine = jnp.exp((b % g).astype(F32) * log_block)[:, None, None]
        whole = jnp.exp(g * log_block)[:, None, None]
        prefix = jnp.where(upper, prefix + mine * got, prefix)
        total = jnp.where(upper, whole * got + total, whole * total + got)
        g *= 2
    return prefix


def states_after(local, log_block, axis):
    first = None
    n, b = lax.axis_size(axis), lax.axis_index(axis)
    total, suffix, g = local, jnp.zeros_like(local), 1
    while g < n:
        got = lax.ppermute(total.astype(BF16), axis, [(j, j ^ g) for j in range(n)]).astype(F32)
        first = got if first is None else first
        upper = (b // g) % 2 == 1
        mine = jnp.exp((g - 1 - b % g).astype(F32) * log_block)[:, None, None]
        whole = jnp.exp(g * log_block)[:, None, None]
        suffix = jnp.where(upper, suffix, suffix + mine * got)
        total = jnp.where(upper, got + whole * total, total + whole * got)
        g *= 2
    return suffix, first


def pair_swap(x):
    lane = lax.broadcasted_iota(jnp.int32, x.shape, 1)
    width = x.shape[1]
    return jnp.where(lane % 2 == 0, pltpu.roll(x, width - 1, 1), pltpu.roll(x, 1, 1))


def side_by_side(*arrays):
    rows = arrays[0].shape[0]
    widths = [a.shape[1] for a in arrays]

    def kernel(*refs):
        column = 0
        for ref, width in zip(refs, widths):
            refs[-1][:, column : column + width] = ref[...]
            column += width

    block = min(rows, 64)
    return pl.pallas_call(
        kernel,
        grid=(rows // block,),
        in_specs=[pl.BlockSpec((block, width), lambda r: (r, 0)) for width in widths],
        out_specs=pl.BlockSpec((block, sum(widths)), lambda r: (r, 0)),
        out_shape=jax.ShapeDtypeStruct((rows, sum(widths)), arrays[0].dtype),
        cost_estimate=pl.CostEstimate(flops=0, bytes_accessed=4 * rows * sum(widths), transcendentals=0),
        name="join",
    )(*arrays)


def gathered(at, refs, k, rows=slice(None)):
    if k == 0:
        return refs[0][rows, :]
    return jnp.where(at >= k, refs[2 * k - 1][rows, :], refs[2 * k][rows, :])


def columns_of(at, n, k, width):
    return pl.ds(pl.multiple_of(((at + n - k) % n) * width, width), width)


def fill_normed(at, refs, gain_ref, full_ref):
    n = len(refs) // 2 + 1
    width = refs[0].shape[1]
    blocks = [gathered(at, refs, k).astype(F32) for k in range(n)]
    squares = sum(jnp.sum(b * b, axis=1, keepdims=True) for b in blocks)
    scale = lax.rsqrt(squares / (n * width) + EPSILON)
    for k, b in enumerate(blocks):
        where = columns_of(at, n, k, width)
        full_ref[:, where] = (b * scale * gain_ref[:, where]).astype(BF16)
    return scale


def flat(x, pairs):
    return [x] + [p for pair in pairs for p in pair]


def project_kernel(heads, count, at_ref, lg_ref, gain_ref, w_ref, cos_ref, sin_ref, *refs):
    blocks, (full_ref, scale_ref, q_ref, k_ref, v_ref, state_ref) = refs[:count], refs[count:]
    step = pl.program_id(0)
    rows = pl.num_programs(0) * BLOCK
    scale_ref[...] = fill_normed(at_ref[0], blocks, gain_ref, full_ref)
    x = full_ref[...]
    qk = heads * HK
    c, s = cos_ref[...], sin_ref[...]
    k_out = nn(x, w_ref[:, qk : 2 * qk])
    v_out = nn(x, w_ref[:, 2 * qk :]).astype(BF16)
    q_out = nn(x, w_ref[:, :qk])
    v_ref[...] = v_out
    m = lax.broadcasted_iota(jnp.int32, (BLOCK, 1), 0) + step * BLOCK
    for h in range(heads):
        at = slice(h * HK, (h + 1) * HK)
        one = k_out[:, at]
        key = ((one * c + pair_swap(one) * s) * (1.0 / math.sqrt(HK))).astype(BF16)
        k_ref[:, at] = key
        tail = jnp.exp((rows - m).astype(F32) * lg_ref[h])
        add = tn((key.astype(F32) * tail).astype(BF16), v_out[:, h * HV : (h + 1) * HV])

        @pl.when(step == 0)
        def _(h=h, add=add):
            state_ref[h] = add

        @pl.when(step > 0)
        def _(h=h, add=add):
            state_ref[h] += add

        one = q_out[:, at]
        q_ref[:, at] = (one * c + pair_swap(one) * s).astype(BF16)


def project(at, log_gamma, gain, w, x, pairs, heads, cosine, sine):
    rows, width = x.shape
    features = w.shape[0]
    outs = 2 * heads * HK + heads * HV
    blocks = flat(x, pairs)

    def by_rows(columns):
        return pl.BlockSpec((BLOCK, columns), lambda r: (r, 0))

    return pl.pallas_call(
        lambda *refs: project_kernel(heads, len(blocks), *refs),
        grid=(rows // BLOCK,),
        in_specs=[
            pl.BlockSpec(memory_space=pltpu.SMEM),
            pl.BlockSpec(memory_space=pltpu.SMEM),
            pl.BlockSpec((1, features), lambda r: (0, 0)),
            pl.BlockSpec((features, outs), lambda r: (0, 0)),
            by_rows(HK),
            by_rows(HK),
            *[by_rows(width)] * len(blocks),
        ],
        out_specs=[
            by_rows(features),
            by_rows(1),
            by_rows(heads * HK),
            by_rows(heads * HK),
            by_rows(heads * HV),
            pl.BlockSpec((heads, HK, HV), lambda r: (0, 0, 0)),
        ],
        out_shape=[
            jax.ShapeDtypeStruct((rows, features), BF16),
            jax.ShapeDtypeStruct((rows, 1), F32),
            jax.ShapeDtypeStruct((rows, heads * HK), BF16),
            jax.ShapeDtypeStruct((rows, heads * HK), BF16),
            jax.ShapeDtypeStruct((rows, heads * HV), BF16),
            jax.ShapeDtypeStruct((heads, HK, HV), F32),
        ],
        cost_estimate=pl.CostEstimate(
            flops=2 * rows * features * outs, bytes_accessed=2 * features * outs + 12 * rows * features, transcendentals=0
        ),
        name="proj",
    )(at, log_gamma, gain, w, cosine, sine, *blocks)


def product_kernel(x_ref, w_ref, out_ref):
    out_ref[...] = nn(x_ref[...], w_ref[...])


def product(x, w, at, columns):
    rows, inner = x.shape
    return pl.pallas_call(
        product_kernel,
        grid=(rows // BLOCK,),
        in_specs=[
            pl.BlockSpec((BLOCK, inner), lambda r: (r, 0)),
            pl.BlockSpec((inner, columns), lambda r: (0, at)),
        ],
        out_specs=pl.BlockSpec((BLOCK, columns), lambda r: (r, 0)),
        out_shape=jax.ShapeDtypeStruct((rows, columns), F32),
        cost_estimate=pl.CostEstimate(
            flops=2 * rows * inner * columns, bytes_accessed=2 * inner * columns + 8 * rows * columns, transcendentals=0
        ),
        name="prod",
    )(x, w)


def mlp_kernel(units, count, at_ref, gain_ref, w_ref, *refs):
    blocks, grads = refs[:count], refs[count : 2 * count]
    full_ref, hidden_ref, acts_ref, grad_ref, scale_ref, inner_ref, back_ref = refs[-7:]
    at, n = at_ref[0], count // 2 + 1
    scale_ref[...] = fill_normed(at, blocks, gain_ref, full_ref)
    for k in range(n):
        grad_ref[:, columns_of(at, n, k, grads[0].shape[1])] = gathered(at, grads, k)
    x = full_ref[...]
    gate = nn(x, w_ref[:, :units])
    up = nn(x, w_ref[:, units : 2 * units])
    grad = nn(grad_ref[...], w_ref[:, 2 * units :])
    cdf = 0.5 * (1.0 + lax.erf(gate * math.sqrt(0.5)))
    gelu = gate * cdf
    density = jnp.exp(-0.5 * gate * gate) * (1.0 / math.sqrt(2.0 * math.pi))
    hidden_ref[...] = (gelu * up).astype(BF16)
    g_gate = (grad * up * (cdf + gate * density)).astype(BF16)
    g_up = (grad * gelu).astype(BF16)
    acts_ref[:, :units] = g_gate
    acts_ref[:, units:] = g_up
    inner_ref[...] = jnp.sum(g_gate.astype(F32) * gate + g_up.astype(F32) * up, axis=1, keepdims=True)
    back_ref[...] = (nt(g_gate, w_ref[:, :units]) + nt(g_up, w_ref[:, units : 2 * units])).astype(BF16)


def mlp(at, gain, w, part, grads, x, pairs, shared):
    rows, width = x.shape
    features = w.shape[0]
    units = w.shape[1] // 3
    blocks = flat(x, pairs)
    steps = rows // BLOCK
    total = grads[0].shape[0]

    def by_rows(columns):
        return pl.BlockSpec((BLOCK, columns), lambda r: (r, 0))

    def own_rows(columns):
        return pl.BlockSpec((BLOCK, columns), lambda r: (part * steps + r, 0))

    return pl.pallas_call(
        lambda *refs: mlp_kernel(units, len(blocks), *refs),
        grid=(steps,),
        in_specs=[
            pl.BlockSpec(memory_space=pltpu.SMEM),
            pl.BlockSpec((1, features), lambda r: (0, 0)),
            pl.BlockSpec((features, 3 * units), lambda r: (0, 0)),
            *[by_rows(width)] * len(blocks),
            *[own_rows(width)] * len(grads),
            *[pl.BlockSpec(memory_space=pl.ANY)] * len(shared),
        ],
        out_specs=[
            own_rows(features),
            own_rows(units),
            own_rows(2 * units),
            own_rows(features),
            by_rows(1),
            by_rows(1),
            by_rows(features),
        ],
        out_shape=[
            jax.ShapeDtypeStruct((total, features), BF16),
            jax.ShapeDtypeStruct((total, units), BF16),
            jax.ShapeDtypeStruct((total, 2 * units), BF16),
            jax.ShapeDtypeStruct((total, features), BF16),
            jax.ShapeDtypeStruct((rows, 1), F32),
            jax.ShapeDtypeStruct((rows, 1), F32),
            jax.ShapeDtypeStruct((rows, features), BF16),
        ],
        input_output_aliases={3 + 2 * len(blocks) + i: i for i in range(len(shared))},
        cost_estimate=pl.CostEstimate(
            flops=10 * rows * features * units,
            bytes_accessed=6 * features * units + 14 * rows * features,
            transcendentals=2 * rows * units,
        ),
        name="mlp",
    )(at, gain, w, *blocks, *grads, *shared)


def decay_vectors(log_gamma):
    down = lax.broadcasted_iota(jnp.int32, (BLOCK, 1), 0).astype(F32)
    across = lax.broadcasted_iota(jnp.int32, (1, BLOCK), 1).astype(F32)
    return jnp.exp(down * log_gamma), jnp.exp(-across * log_gamma)


def block_decay(scores, r, j, log_gamma, down, across):
    out = scores * (down * jnp.exp(log_gamma * (BLOCK * (r - j)))) * across
    if r == j:
        n = lax.broadcasted_iota(jnp.int32, scores.shape, 0)
        m = lax.broadcasted_iota(jnp.int32, scores.shape, 1)
        out = jnp.where(n >= m, out, 0.0)
    return out.astype(BF16)


def cut(r):
    return slice(r * BLOCK, (r + 1) * BLOCK)


def forward_kernel(first, count, lg_ref, q_ref, k_ref, v_ref, gate_ref, state_ref, w_ref, *refs):
    gated_ref, ret_ref, out_ref, acc_ref = refs[-4:]
    head = pl.program_id(0)
    log_gamma = lg_ref[head]
    down, across = decay_vectors(log_gamma)
    state = state_ref[0]
    for at in range(count):
        r = first + at
        q = q_ref[cut(at), :]
        ret = nn(q, state) * (down * jnp.exp(log_gamma * (BLOCK * r)))
        for j in range(r + 1):
            weights = block_decay(nt(q, k_ref[cut(j), :]), r, j, log_gamma, down, across)
            ret = ret + nn(weights, v_ref[cut(j), :])
        ret_ref[cut(at), :] = ret
        scale = lax.rsqrt(jnp.mean(ret * ret, axis=1, keepdims=True) + EPSILON)
        gate = gate_ref[cut(at), :]
        gated = (gate / (1.0 + jnp.exp(-gate)) * (ret * scale)).astype(BF16)
        gated_ref[cut(at), :] = gated
        out = nt(gated, w_ref[...])

        @pl.when(head == 0)
        def _(at=at, out=out):
            acc_ref[cut(at), :] = out

        @pl.when(head > 0)
        def _(at=at, out=out):
            acc_ref[cut(at), :] += out

        @pl.when(head == pl.num_programs(0) - 1)
        def _(at=at):
            out_ref[cut(at), :] = acc_ref[cut(at), :].astype(BF16)


def retention_forward(part, parts, log_gamma, q, k, v, gate, state, w, first_column, shared):
    rows = q.shape[0]
    heads = q.shape[1] // HK
    features = w.shape[0]
    own = rows // parts
    seen = own * (part + 1)
    count = own // BLOCK
    pairs = sum(part * count + at + 1 for at in range(count))
    flops = heads * (pairs * 2 * BLOCK * BLOCK * (HK + HV) + 2 * own * HK * HV + 2 * own * HV * features)
    head_out = pl.BlockSpec((own, HV), lambda h: (part, h))
    return pl.pallas_call(
        lambda *refs: forward_kernel(part * count, count, *refs),
        grid=(heads,),
        in_specs=[
            pl.BlockSpec(memory_space=pltpu.SMEM),
            pl.BlockSpec((own, HK), lambda h: (part, h)),
            pl.BlockSpec((seen, HK), lambda h: (0, h)),
            pl.BlockSpec((seen, HV), lambda h: (0, h)),
            pl.BlockSpec((own, HV), lambda h: (part, h)),
            pl.BlockSpec((1, HK, HV), lambda h: (h, 0, 0)),
            pl.BlockSpec((features, HV), lambda h: (0, first_column // HV + h)),
            *[pl.BlockSpec(memory_space=pl.ANY)] * len(shared),
        ],
        out_specs=[head_out, head_out, pl.BlockSpec((own, features), lambda h: (0, 0))],
        input_output_aliases={7 + i: i for i in range(len(shared))},
        out_shape=[
            jax.ShapeDtypeStruct((rows, heads * HV), BF16),
            jax.ShapeDtypeStruct((rows, heads * HV), F32),
            jax.ShapeDtypeStruct((own, features), BF16),
        ],
        scratch_shapes=[pltpu.VMEM((own, features), F32)],
        cost_estimate=pl.CostEstimate(flops=flops, bytes_accessed=20 * own * heads * HV, transcendentals=own * heads * HV),
        name="fwd",
    )(log_gamma, q, k, v, gate, state, w, *shared)


def gate_backward_kernel(first, count, n_blocks, at_ref, lg_ref, q_ref, w_ref, gate_ref, ret_ref, *refs):
    blocks, (g_gate_ref, g_ret_ref, full_ref, state_ref, inner_ref) = refs[:n_blocks], refs[-5:]
    head = pl.program_id(0)
    log_gamma = lg_ref[head]
    down, _ = decay_vectors(log_gamma)
    n = n_blocks // 2 + 1
    width = blocks[0].shape[1]
    here = at_ref[0]
    state = None
    for at in range(count):
        r = first + at

        @pl.when(head == 0)
        def _(at=at):
            for k in range(n):
                full_ref[cut(at), columns_of(here, n, k, width)] = gathered(here, blocks, k, cut(at))

        grad = nn(full_ref[cut(at), :], w_ref[...])
        ret = ret_ref[cut(at), :]
        gate = gate_ref[cut(at), :]
        scale = lax.rsqrt(jnp.mean(ret * ret, axis=1, keepdims=True) + EPSILON)
        grouped = ret * scale
        sig = 1.0 / (1.0 + jnp.exp(-gate))
        g_gate = (grad * grouped * (sig * (1.0 + gate * (1.0 - sig)))).astype(BF16)
        g = grad * (gate * sig)
        g_ret = (scale * (g - grouped * jnp.mean(g * grouped, axis=1, keepdims=True))).astype(BF16)
        g_gate_ref[cut(at), :] = g_gate
        g_ret_ref[cut(at), :] = g_ret
        inner_ref[0, cut(at), :] = jnp.sum(g_gate.astype(F32) * gate, axis=1, keepdims=True)
        q = (q_ref[cut(at), :].astype(F32) * (down * jnp.exp(log_gamma * (BLOCK * r)))).astype(BF16)
        add = tn(q, g_ret)
        state = add if state is None else state + add
    state_ref[0] = state


def gate_backward(part, parts, here, log_gamma, q, w, first_column, gate, ret, x, pairs, shared):
    rows = q.shape[0]
    heads = q.shape[1] // HK
    features = w.shape[0]
    own = rows // parts
    count = own // BLOCK
    blocks = flat(x, pairs)
    head_out = pl.BlockSpec((own, HV), lambda h: (part, h))
    return pl.pallas_call(
        lambda *refs: gate_backward_kernel(part * count, count, len(blocks), *refs),
        grid=(heads,),
        in_specs=[
            pl.BlockSpec(memory_space=pltpu.SMEM),
            pl.BlockSpec(memory_space=pltpu.SMEM),
            pl.BlockSpec((own, HK), lambda h: (part, h)),
            pl.BlockSpec((features, HV), lambda h: (0, first_column // HV + h)),
            head_out,
            head_out,
            *[pl.BlockSpec((own, x.shape[1]), lambda h: (0, 0))] * len(blocks),
            *[pl.BlockSpec(memory_space=pl.ANY)] * len(shared),
        ],
        out_specs=[
            head_out,
            head_out,
            pl.BlockSpec((own, features), lambda h: (part, 0)),
            pl.BlockSpec((1, HK, HV), lambda h: (h, 0, 0)),
            pl.BlockSpec((1, own, 1), lambda h: (h, 0, 0)),
        ],
        input_output_aliases={6 + len(blocks) + i: i for i in range(len(shared))},
        out_shape=[
            jax.ShapeDtypeStruct((rows, heads * HV), BF16),
            jax.ShapeDtypeStruct((rows, heads * HV), BF16),
            jax.ShapeDtypeStruct((rows, features), BF16),
            jax.ShapeDtypeStruct((heads, HK, HV), F32),
            jax.ShapeDtypeStruct((heads, own, 1), F32),
        ],
        cost_estimate=pl.CostEstimate(
            flops=heads * 2 * own * HV * (HK + features),
            bytes_accessed=16 * own * heads * HV,
            transcendentals=own * heads * HV,
        ),
        name="gate",
    )(here, log_gamma, q, w, gate, ret, *blocks, *shared)


def backward_kernel(total, lg_ref, q_ref, k_ref, v_ref, state_in_ref, state_grad_ref, cos_ref, sin_ref, *refs):
    g_ref, gate_ref, all_ref, inner_ref, acc_k, acc_v, g_q_ref, g_k_ref, g_v_ref, sems = refs
    head, heads = pl.program_id(0), pl.num_programs(0)
    log_gamma = lg_ref[head]
    down, across = decay_vectors(log_gamma)
    state_in, state_grad = state_in_ref[0], state_grad_ref[0]
    key_scale = 1.0 / math.sqrt(HK)

    def send(ref, column, width, i):
        target = all_ref.at[:, pl.ds(pl.multiple_of(column, HK), width)]
        return pltpu.make_async_copy(ref, target, sems.at[i])

    gates = send(gate_ref, heads * (2 * HK + HV) + head * HV, HV, 0)
    gates.start()

    def put(ref, r, x, factor):
        turned = x * cos_ref[cut(r), :] - pair_swap(x) * sin_ref[cut(r), :]
        ref[cut(r), :] = (turned * factor).astype(BF16)

    for r in range(total):
        g = g_ref[cut(r), :]
        q, k, v = q_ref[cut(r), :], k_ref[cut(r), :], v_ref[cut(r), :]
        tail = down_tail(log_gamma, total * BLOCK - r * BLOCK)
        acc_v[cut(r), :] = nn((k.astype(F32) * tail).astype(BF16), state_grad)
        acc_k[cut(r), :] = nt(v, state_grad) * tail
        g_q = nt(g, state_in) * (down * jnp.exp(log_gamma * (BLOCK * r)))
        for j in range(r + 1):
            kj, vj = k_ref[cut(j), :], v_ref[cut(j), :]
            weights = block_decay(nt(q, kj), r, j, log_gamma, down, across)
            g_scores = block_decay(nt(g, vj), r, j, log_gamma, down, across)
            acc_v[cut(j), :] += tn(weights, g)
            acc_k[cut(j), :] += tn(g_scores, q)
            g_q = g_q + nn(g_scores, kj)
        inner_ref[0, cut(r), :] = jnp.sum(g_q * q.astype(F32), axis=1, keepdims=True)
        put(g_q_ref, r, g_q, 1.0)
    for r in range(total):
        g_k = acc_k[cut(r), :]
        g_v = acc_v[cut(r), :].astype(BF16)
        g_v_ref[cut(r), :] = g_v
        inner_ref[0, cut(r), :] += jnp.sum(g_k * k_ref[cut(r), :].astype(F32), axis=1, keepdims=True) + jnp.sum(
            g_v.astype(F32) * v_ref[cut(r), :].astype(F32), axis=1, keepdims=True
        )
        put(g_k_ref, r, g_k, key_scale)
    copies = [
        send(g_q_ref, head * HK, HK, 1),
        send(g_k_ref, (heads + head) * HK, HK, 2),
        send(g_v_ref, 2 * heads * HK + head * HV, HV, 3),
    ]
    for copy in copies:
        copy.start()
    for copy in [gates] + copies:
        copy.wait()


def down_tail(log_gamma, start):
    m = lax.broadcasted_iota(jnp.int32, (BLOCK, 1), 0).astype(F32)
    return jnp.exp((start - m) * log_gamma)


def retention_backward(log_gamma, q, k, v, state_in, state_grad, cosine, sine, g_ret, g_gate):
    rows = q.shape[0]
    heads = q.shape[1] // HK
    blocks = rows // BLOCK
    pairs = blocks * (blocks + 1) // 2
    flops = heads * 2 * (pairs * BLOCK * BLOCK * (3 * HK + 2 * HV) + 3 * rows * HK * HV)
    head_keys = pl.BlockSpec((rows, HK), lambda h: (0, h))
    head_values = pl.BlockSpec((rows, HV), lambda h: (0, h))
    head_state = pl.BlockSpec((1, HK, HV), lambda h: (h, 0, 0))
    table = pl.BlockSpec((rows, HK), lambda h: (0, 0))
    return pl.pallas_call(
        lambda *refs: backward_kernel(blocks, *refs),
        grid=(heads,),
        in_specs=[
            pl.BlockSpec(memory_space=pltpu.SMEM),
            head_keys,
            head_keys,
            head_values,
            head_state,
            head_state,
            table,
            table,
            head_values,
            head_values,
        ],
        out_specs=[pl.BlockSpec(memory_space=pl.ANY), pl.BlockSpec((1, rows, 1), lambda h: (h, 0, 0))],
        out_shape=[
            jax.ShapeDtypeStruct((rows, heads * 2 * (HK + HV)), BF16),
            jax.ShapeDtypeStruct((heads, rows, 1), F32),
        ],
        scratch_shapes=[
            pltpu.VMEM((rows, HK), F32),
            pltpu.VMEM((rows, HV), F32),
            pltpu.VMEM((rows, HK), BF16),
            pltpu.VMEM((rows, HK), BF16),
            pltpu.VMEM((rows, HV), BF16),
            pltpu.SemaphoreType.DMA((4,)),
        ],
        cost_estimate=pl.CostEstimate(flops=flops, bytes_accessed=24 * rows * heads * HK, transcendentals=0),
        name="bwd",
    )(log_gamma, q, k, v, state_in, state_grad, cosine, sine, g_ret, g_gate)


def on_device(
    layer_input,
    gain_attn,
    w_query,
    w_key,
    w_value,
    w_retgate,
    w_out,
    gain_mlp,
    w_gate,
    w_up,
    w_down,
    cotangent,
):
    data = (DP, CTX)
    rows, width = layer_input.shape
    n_tp, at_tp = lax.axis_size(TP), lax.axis_index(TP)
    features = width * n_tp
    heads = w_query.shape[1] // HK
    units = w_gate.shape[1]

    parts = 2
    own = rows // parts
    cuts = [slice(c * own, (c + 1) * own) for c in range(parts)]

    qk = heads * HK
    vw = heads * HV
    attn_shard = side_by_side(w_query, w_key, w_value, w_retgate)
    attn_full = lax.all_gather(attn_shard, data, axis=0, tiled=True)
    out_full = lax.all_gather(w_out, data, axis=0, tiled=True)

    gains = small_gather(jnp.stack([gain_attn, gain_mlp]), TP)

    log_gamma = jnp.log1p(-jnp.exp2(-5.0 - (at_tp * heads + jnp.arange(heads)).astype(F32)))
    log_block = rows * log_gamma
    positions = lax.axis_index(CTX) * rows + jnp.arange(rows)
    frequencies = jnp.exp(-math.log(10000.0) * jnp.linspace(0.0, 1.0, HK // 2, dtype=F32))
    angles = positions.astype(F32)[:, None] * jnp.repeat(frequencies, 2)[None, :]
    cosine = jnp.cos(angles)
    sine = jnp.sin(angles) * jnp.where(jnp.arange(HK) % 2 == 0, -1.0, 1.0)[None, :]
    here = at_tp.reshape(1)
    mlp_shard = side_by_side(w_gate, w_up, w_down)

    pairs = line_gather(layer_input, TP, (cosine, sine, mlp_shard, log_gamma, gains))
    normed, scale_attn, q, k, v, local_state = project(
        here, log_gamma, gains[0:1], attn_full, layer_input, pairs, heads, cosine, sine
    )
    cot = after(cotangent, pairs[-1][0])
    cot_blocks = flat(cot, line_gather(cot, TP))
    gate_pre = product(after(normed, local_state), attn_full, (2 * qk + vw) // vw, vw)
    state_in = states_before(local_state, log_block, CTX).astype(BF16)
    mlp_full = lax.all_gather(after(mlp_shard, state_in), data, axis=0, tiled=True)
    heads_out, branch = [], []
    for c in range(parts):
        *heads_out, out = retention_forward(c, parts, log_gamma, q, k, v, gate_pre, state_in, out_full, 0, heads_out)
        branch.append(out)
    gated, retained = heads_out

    x_own = layer_input.astype(F32)
    middle, mid_pairs, scale_mlp, inner_mlp, back, grad_middle, grad_own, grad_pairs = ([] for _ in range(8))
    gain_mlp_sum = 0.0

    def norm_back(own_rows, scale, gain, inner, grad_normed):
        hat = own_rows * scale
        grad = scale * (grad_normed * gain[None, :] - hat * (inner[:, None] / features))
        return grad, jnp.sum(grad_normed * hat, axis=0)

    def row_total(inner):
        lanes = 128
        return swap_sum(inner.reshape(-1, lanes), TP).reshape(-1)

    early = ()
    for c in range(parts):
        total, steps = line_scatter(after(branch[c], *early), TP)
        early = steps[-1]
        if c:
            total = after(total, mid_pairs[c - 1][0][0])
        middle.append(x_own[cuts[c]] + total)
        mid_pairs.append(line_gather(middle[c].astype(BF16), TP))
    shared = []
    for c in range(parts):
        *results, scale, inner, out = mlp(
            here, gains[1:2], mlp_full, c, cot_blocks, middle[c].astype(BF16), mid_pairs[c], shared
        )
        shared = results
        scale_mlp.append(scale)
        inner_mlp.append(inner[:, 0])
        back.append(out)
    normed_mlp, hidden, grad_acts, grad_full = shared
    early = ()
    for c in range(parts):
        inner = row_total(inner_mlp[c])
        total, steps = line_scatter(after(back[c], *early), TP)
        early = steps[-1]
        if c:
            total = after(total, grad_pairs[c - 1][0][0])
        grad_mid, gain_sum = norm_back(middle[c], scale_mlp[c], gain_mlp, inner, total)
        gain_mlp_sum = gain_mlp_sum + gain_sum
        grad_middle.append(cotangent[cuts[c]].astype(F32) + grad_mid)
        grad_own.append(grad_middle[c].astype(BF16))
        grad_pairs.append(line_gather(grad_own[c], TP))
    grad_down = tn(grad_full, hidden).astype(BF16)
    grad_gate_up = tn(after(normed_mlp, grad_down), grad_acts).astype(BF16)
    mlp_parts = nt(hidden, mlp_full[:, 2 * units :]).astype(BF16)

    grad_own[0] = after(grad_own[0], grad_gate_up, grad_down)
    mlp_out = routed_scatter(after(mlp_parts, grad_pairs[-1][-1][0]), TP)
    layer_output = (jnp.concatenate(middle) + mlp_out).astype(BF16)
    shared = []
    partial_state = 0.0
    inner_attn = []
    for c in range(parts):
        *shared, ps, inner = gate_backward(
            c,
            parts,
            here,
            log_gamma,
            q,
            out_full,
            0,
            gate_pre,
            retained,
            grad_own[c],
            grad_pairs[c],
            shared,
        )
        partial_state = partial_state + ps
        inner_attn.append(jnp.sum(inner[:, :, 0], axis=0))
    g_gate, g_ret, grad_attn = shared
    state_grad, got = states_after(partial_state, log_block, CTX)
    state_grad = state_grad.astype(BF16)
    grad_out = tn(after(grad_attn, got), gated).astype(BF16)
    grads_attn, inner = retention_backward(
        log_gamma, q, k, v, state_in, after(state_grad, grad_out), cosine, sine, g_ret, g_gate
    )
    inner_attn = jnp.concatenate(inner_attn) + jnp.sum(inner[:, :, 0], axis=0)
    back = []
    for c in range(parts):
        rows_grads = after(grads_attn, *back, *([grad_in_w] if c else []))
        back.append(nt(rows_grads[cuts[c]], attn_full).astype(BF16))
        if c == 0:
            grad_in_w = tn(normed, after(grads_attn, *back)).astype(BF16)

    def shard(grad):
        return lax.psum_scatter(grad, data, scatter_dimension=0, tiled=True).astype(F32)

    s_down = shard(grad_down)
    s_gate_up = shard(grad_gate_up)
    s_gate, s_up = s_gate_up[:, :units], s_gate_up[:, units:]
    s_out = shard(grad_out)
    s_in = shard(grad_in_w)
    inner_attn, s_down, s_gate, s_up, s_out, layer_output = lax.optimization_barrier(
        (inner_attn, s_down, s_gate, s_up, s_out, layer_output)
    )
    inner_attn = row_total(inner_attn)
    grad_input, gain_attn_sum = [], 0.0
    early = ()
    for c in range(parts):
        total, steps = line_scatter(after(back[c], *early), TP)
        early = steps[0]
        grad_in, gain_sum = norm_back(x_own[cuts[c]], scale_attn[cuts[c]], gain_attn, inner_attn[cuts[c]], total)
        grad_input.append((grad_middle[c] + grad_in).astype(BF16))
        gain_attn_sum = gain_attn_sum + gain_sum
    grad_input = jnp.concatenate(grad_input)

    gain_sums = swap_sum(swap_sum(jnp.stack([gain_attn_sum, gain_mlp_sum]), CTX), DP)
    return (
        layer_output,
        grad_input,
        gain_sums[0],
        s_in[:, :qk],
        s_in[:, qk : 2 * qk],
        s_in[:, 2 * qk : 2 * qk + vw],
        s_in[:, 2 * qk + vw :],
        s_out,
        gain_sums[1],
        s_gate,
        s_up,
        s_down,
    )


def solution(mesh):
    tokens = P((DP, CTX), TP)
    gain = P(TP)
    weight = P((DP, CTX), TP)

    return jax.shard_map(
        on_device,
        mesh=mesh,
        in_specs=(tokens, gain, weight, weight, weight, weight, weight, gain, weight, weight, weight, tokens),
        out_specs=(tokens, tokens, gain, weight, weight, weight, weight, weight, gain, weight, weight, weight),
        check_vma=False,
    )
```

```python
import math

import jax
import jax.numpy as jnp
from jax import lax
from jax.experimental import pallas as pl
from jax.experimental.pallas import tpu as pltpu
from jax.sharding import PartitionSpec as P


HK = 256
HV = 512
EPSILON = 1e-06
BLOCK = 512
TP, CTX, DP = "tp", "ctx", "dp"
F32 = jnp.float32
BF16 = jnp.bfloat16


def nn(a, b):
    return lax.dot_general(a, b, (((1,), (0,)), ((), ())), preferred_element_type=F32)


def tn(a, b):
    return lax.dot_general(a, b, (((0,), (0,)), ((), ())), preferred_element_type=F32)


def nt(a, b):
    return lax.dot_general(a, b, (((1,), (1,)), ((), ())), preferred_element_type=F32)


def after(x, *before):
    return lax.optimization_barrier((x, *before))[0]


def right(lo, hi):
    return [(i, i + 1) for i in range(lo, hi)]


def left(lo, hi):
    return [(i, i - 1) for i in range(hi, lo, -1)]


def line_gather(x, axis, before=()):
    n, i = lax.axis_size(axis), lax.axis_index(axis)
    rights, lefts = [x], [x]
    for k in range(1, n):
        r_pairs = right(k - 1, n - 1)
        l_pairs = left(0, n - k)
        if k == 2 and before:
            rights[-1] = after(rights[-1], *before)
        if 2 * k > n + 1:
            both = lax.ppermute(jnp.where(i >= k - 1, rights[-1], lefts[-1]), axis, r_pairs + l_pairs)
            rights.append(both)
            lefts.append(both)
        else:
            rights.append(lax.ppermute(rights[-1], axis, r_pairs))
            lefts.append(lax.ppermute(lefts[-1], axis, l_pairs))
    return [(rights[k], lefts[n - k]) for k in range(1, n)]


def place(blocks, axis, dtype):
    n, i = lax.axis_size(axis), lax.axis_index(axis)
    rows, width = blocks[0].shape
    full = jnp.zeros((rows, n * width), dtype)
    for k, block in enumerate(blocks):
        at = ((i - k) % n) * width
        full = lax.dynamic_update_slice(full, block.astype(dtype), (0, at))
    return full


def line_scatter(parts, axis):
    n, i = lax.axis_size(axis), lax.axis_index(axis)
    width = parts.shape[1] // n

    def block(j):
        return lax.dynamic_slice(parts, (0, jnp.clip(j, 0, n - 1) * width), (parts.shape[0], width))

    from_left = from_right = None
    early = []
    for k in range(1, n):
        r_pairs = right(0, k)
        l_pairs = left(n - 1 - k, n - 1)
        if 2 * k < n - 1:
            data = block(jnp.where(i < k, i + n - k, i - n + k))
            if from_left is not None:
                data = (data.astype(F32) + jnp.where(i < k, from_left, from_right).astype(F32)).astype(BF16)
            from_left = from_right = lax.ppermute(data, axis, r_pairs + l_pairs)
            from_left = jnp.where(i <= k, from_left, jnp.zeros_like(from_left))
            from_right = jnp.where(i >= n - 1 - k, from_right, jnp.zeros_like(from_right))
        elif 2 * k <= n:
            data = block(jnp.where(i < k, i + n - k, i - n + k))
            if from_left is not None:
                data = (data.astype(F32) + jnp.where(i < k, from_left, from_right).astype(F32)).astype(BF16)
            from_left = lax.ppermute(data, axis, r_pairs)
            from_right = lax.ppermute(data, axis, l_pairs)
        else:
            r_data, l_data = block(i + n - k), block(i - n + k)
            if from_left is not None:
                r_data = (r_data.astype(F32) + from_left.astype(F32)).astype(BF16)
                l_data = (l_data.astype(F32) + from_right.astype(F32)).astype(BF16)
            from_left = lax.ppermute(r_data, axis, r_pairs)
            from_right = lax.ppermute(l_data, axis, l_pairs)
        if k < n - 1:
            early.append((from_left, from_right))
    return block(i).astype(F32) + from_left.astype(F32) + from_right.astype(F32), early


def routed_scatter(parts, axis):
    n, i = lax.axis_size(axis), lax.axis_index(axis)
    width = parts.shape[1] // n

    def block(j):
        return lax.dynamic_slice(parts, (0, (j % n) * width), (parts.shape[0], width))

    total = block(i).astype(F32)
    for k in range(1, n):
        total = total + lax.ppermute(block(i + k), axis, [(j, (j + k) % n) for j in range(n)]).astype(F32)
    return total


def small_gather(x, axis):
    n = lax.axis_size(axis)
    blocks = [x] + [lax.ppermute(x, axis, [(j, (j + s) % n) for j in range(n)]) for s in range(1, n)]
    return place(blocks, axis, x.dtype)


def swap_sum(x, axis):
    n = lax.axis_size(axis)
    g = 1
    while g < n:
        x = x + lax.ppermute(x, axis, [(j, j ^ g) for j in range(n)])
        g *= 2
    return x


def state_factors(log_block, axis):
    n, b = lax.axis_size(axis), lax.axis_index(axis)
    before, behind, g = [], [], 1
    while g < n:
        upper = (b // g) % 2 == 1
        before.append(jnp.where(upper, jnp.exp((b % g).astype(F32) * log_block), 0.0))
        behind.append(jnp.where(upper, 0.0, jnp.exp((g - 1 - b % g).astype(F32) * log_block)))
        g *= 2
    return jnp.stack(before), jnp.stack(behind)


def states_before(local, rounded, log_block, axis):
    n, b = lax.axis_size(axis), lax.axis_index(axis)
    total, pieces, g = local, [], 1
    while g < n:
        got = lax.ppermute(rounded if g == 1 else total.astype(BF16), axis, [(j, j ^ g) for j in range(n)])
        upper = (b // g) % 2 == 1
        pieces.append(got)
        if 2 * g < n:
            whole = jnp.exp(g * log_block)[:, None, None]
            total = jnp.where(upper, whole, 1.0) * got.astype(F32) + jnp.where(upper, 1.0, whole) * total
        g *= 2
    return pieces


def states_after(local, rounded, log_block, axis):
    n, b = lax.axis_size(axis), lax.axis_index(axis)
    total, pieces, g = local, [], 1
    while g < n:
        got = lax.ppermute(rounded if g == 1 else total.astype(BF16), axis, [(j, j ^ g) for j in range(n)])
        upper = (b // g) % 2 == 1
        pieces.append(got)
        if 2 * g < n:
            whole = jnp.exp(g * log_block)[:, None, None]
            total = jnp.where(upper, 1.0, whole) * got.astype(F32) + jnp.where(upper, whole, 1.0) * total
        g *= 2
    return pieces


def whole_state(refs, factor_ref, head):
    state = refs[0][0].astype(F32) * factor_ref[0, head]
    for i in range(1, len(refs)):
        state = state + refs[i][0].astype(F32) * factor_ref[i, head]
    return state.astype(BF16)


def pair_swap(x):
    lane = lax.broadcasted_iota(jnp.int32, x.shape, 1)
    width = x.shape[1]
    return jnp.where(lane % 2 == 0, pltpu.roll(x, width - 1, 1), pltpu.roll(x, 1, 1))


def side_by_side(*arrays):
    rows = arrays[0].shape[0]
    widths = [a.shape[1] for a in arrays]

    def kernel(*refs):
        column = 0
        for ref, width in zip(refs, widths):
            refs[-1][:, column : column + width] = ref[...]
            column += width

    block = min(rows, 64)
    return pl.pallas_call(
        kernel,
        grid=(rows // block,),
        in_specs=[pl.BlockSpec((block, width), lambda r: (r, 0)) for width in widths],
        out_specs=pl.BlockSpec((block, sum(widths)), lambda r: (r, 0)),
        out_shape=jax.ShapeDtypeStruct((rows, sum(widths)), arrays[0].dtype),
        cost_estimate=pl.CostEstimate(flops=0, bytes_accessed=4 * rows * sum(widths), transcendentals=0),
        name="join",
    )(*arrays)


def gathered(at, refs, k, rows=slice(None)):
    if k == 0:
        return refs[0][rows, :]
    return jnp.where(at >= k, refs[2 * k - 1][rows, :], refs[2 * k][rows, :])


def columns_of(at, n, k, width):
    return pl.ds(pl.multiple_of(((at + n - k) % n) * width, width), width)


def fill_normed(at, refs, gain_ref, full_ref):
    n = len(refs) // 2 + 1
    width = refs[0].shape[1]
    blocks = [gathered(at, refs, k).astype(F32) for k in range(n)]
    squares = sum(jnp.sum(b * b, axis=1, keepdims=True) for b in blocks)
    scale = lax.rsqrt(squares / (n * width) + EPSILON)
    for k, b in enumerate(blocks):
        where = columns_of(at, n, k, width)
        full_ref[:, where] = (b * scale * gain_ref[:, where]).astype(BF16)
    return scale


def flat(x, pairs):
    return [x] + [p for pair in pairs for p in pair]


def project_kernel(part, parts, heads, count, at_ref, lg_ref, gain_ref, w_ref, cos_ref, sin_ref, *refs):
    blocks = refs[:count]
    full_ref, q_ref, k_ref, v_ref, scale_ref, state_ref, rounded_ref, kept_ref, sems = refs[-9:]
    qk, vw = heads * HK, heads * HV
    own = full_ref.shape[0]
    copies = []
    for i, (first, width) in enumerate(((qk, qk), (2 * qk, vw), (0, qk))):
        columns = slice(first, first + width)
        copies.append(pltpu.make_async_copy(w_ref.at[:, columns], kept_ref.at[:, columns], sems.at[i]))
        copies[-1].start()
    scale_ref[...] = fill_normed(at_ref[0], blocks, gain_ref, full_ref)
    x = full_ref[...]
    c, s = cos_ref[...], sin_ref[...]
    copies[0].wait()
    k_out = nn(x, kept_ref[:, qk : 2 * qk])
    copies[1].wait()
    v_out = nn(x, kept_ref[:, 2 * qk : 2 * qk + vw]).astype(BF16)
    copies[2].wait()
    q_out = nn(x, kept_ref[:, :qk])
    v_ref[...] = v_out
    m = lax.broadcasted_iota(jnp.int32, (own, 1), 0) + part * own
    for h in range(heads):
        at = slice(h * HK, (h + 1) * HK)
        one = k_out[:, at]
        key = ((one * c + pair_swap(one) * s) * (1.0 / math.sqrt(HK))).astype(BF16)
        k_ref[:, at] = key
        tail = jnp.exp((parts * own - m).astype(F32) * lg_ref[h])
        state = tn((key.astype(F32) * tail).astype(BF16), v_out[:, h * HV : (h + 1) * HV])
        if part:
            state = state + refs[count][h]
        state_ref[h] = state
        rounded_ref[h] = state.astype(BF16)
        one = q_out[:, at]
        q_ref[:, at] = (one * c + pair_swap(one) * s).astype(BF16)


def project(part, parts, at, log_gamma, gain, w, x, pairs, heads, cosine, sine, shared, state):
    own, width = x.shape
    features = w.shape[0]
    outs = 2 * heads * HK + heads * HV
    blocks = flat(x, pairs)
    rows = parts * own

    def here(columns):
        return pl.BlockSpec((own, columns), lambda i: (0, 0))

    def in_all(columns):
        return pl.BlockSpec((own, columns), lambda i: (part, 0))

    states = pl.BlockSpec((heads, HK, HV), lambda i: (0, 0, 0))
    before = [state] if part else []
    return pl.pallas_call(
        lambda *refs: project_kernel(part, parts, heads, len(blocks), *refs),
        grid=(1,),
        in_specs=[
            pl.BlockSpec(memory_space=pltpu.SMEM),
            pl.BlockSpec(memory_space=pltpu.SMEM),
            pl.BlockSpec((1, features), lambda i: (0, 0)),
            pl.BlockSpec(memory_space=pl.ANY),
            in_all(HK),
            in_all(HK),
            *[here(width)] * len(blocks),
            *[states] * len(before),
            *[pl.BlockSpec(memory_space=pl.ANY)] * len(shared),
        ],
        out_specs=[
            in_all(features),
            in_all(heads * HK),
            in_all(heads * HK),
            in_all(heads * HV),
            here(1),
            states,
            states,
        ],
        out_shape=[
            jax.ShapeDtypeStruct((rows, features), BF16),
            jax.ShapeDtypeStruct((rows, heads * HK), BF16),
            jax.ShapeDtypeStruct((rows, heads * HK), BF16),
            jax.ShapeDtypeStruct((rows, heads * HV), BF16),
            jax.ShapeDtypeStruct((own, 1), F32),
            jax.ShapeDtypeStruct((heads, HK, HV), F32),
            jax.ShapeDtypeStruct((heads, HK, HV), BF16),
        ],
        input_output_aliases={6 + len(blocks) + len(before) + i: i for i in range(len(shared))},
        scratch_shapes=[pltpu.VMEM((features, outs), BF16), pltpu.SemaphoreType.DMA((3,))],
        cost_estimate=pl.CostEstimate(
            flops=2 * own * features * outs, bytes_accessed=2 * features * outs + 12 * own * features, transcendentals=0
        ),
        name="proj",
    )(at, log_gamma, gain, w, cosine, sine, *blocks, *before, *shared)


def product_kernel(x_ref, w_ref, out_ref):
    out_ref[...] = nn(x_ref[...], w_ref[...])


def product(x, w, at, columns):
    rows, inner = x.shape
    return pl.pallas_call(
        product_kernel,
        grid=(rows // BLOCK,),
        in_specs=[
            pl.BlockSpec((BLOCK, inner), lambda r: (r, 0)),
            pl.BlockSpec((inner, columns), lambda r: (0, at)),
        ],
        out_specs=pl.BlockSpec((BLOCK, columns), lambda r: (r, 0)),
        out_shape=jax.ShapeDtypeStruct((rows, columns), F32),
        cost_estimate=pl.CostEstimate(
            flops=2 * rows * inner * columns, bytes_accessed=2 * inner * columns + 8 * rows * columns, transcendentals=0
        ),
        name="prod",
    )(x, w)


def mlp_kernel(units, count, at_ref, gain_ref, w_ref, *refs):
    blocks, grads = refs[:count], refs[count : 2 * count]
    full_ref, hidden_ref, acts_ref, grad_ref, scale_ref, inner_ref, back_ref, kept_ref, sems = refs[-9:]
    at, n = at_ref[0], count // 2 + 1
    first = pl.program_id(0) == 0

    def piece(i):
        columns = slice(i * units, (i + 1) * units)
        return pltpu.make_async_copy(w_ref.at[:, columns], kept_ref.at[:, columns], sems.at[i])

    @pl.when(first)
    def _():
        for i in range(3):
            piece(i).start()

    scale_ref[...] = fill_normed(at, blocks, gain_ref, full_ref)
    for k in range(n):
        grad_ref[:, columns_of(at, n, k, grads[0].shape[1])] = gathered(at, grads, k)
    x = full_ref[...]

    @pl.when(first)
    def _():
        for i in range(3):
            piece(i).wait()

    gate = nn(x, kept_ref[:, :units])
    up = nn(x, kept_ref[:, units : 2 * units])
    grad = nn(grad_ref[...], kept_ref[:, 2 * units :])
    cdf = 0.5 * (1.0 + lax.erf(gate * math.sqrt(0.5)))
    gelu = gate * cdf
    density = jnp.exp(-0.5 * gate * gate) * (1.0 / math.sqrt(2.0 * math.pi))
    hidden_ref[...] = (gelu * up).astype(BF16)
    g_gate = (grad * up * (cdf + gate * density)).astype(BF16)
    g_up = (grad * gelu).astype(BF16)
    acts_ref[:, :units] = g_gate
    acts_ref[:, units:] = g_up
    inner_ref[...] = jnp.sum(g_gate.astype(F32) * gate + g_up.astype(F32) * up, axis=1, keepdims=True)
    back_ref[...] = (nt(g_gate, kept_ref[:, :units]) + nt(g_up, kept_ref[:, units : 2 * units])).astype(BF16)


def mlp(at, gain, w, part, grads, x, pairs, shared):
    rows, width = x.shape
    features = w.shape[0]
    units = w.shape[1] // 3
    blocks = flat(x, pairs)
    block = BLOCK // 2
    steps = rows // block
    total = grads[0].shape[0]

    def by_rows(columns):
        return pl.BlockSpec((block, columns), lambda r: (r, 0))

    def own_rows(columns):
        return pl.BlockSpec((block, columns), lambda r: (part * steps + r, 0))

    return pl.pallas_call(
        lambda *refs: mlp_kernel(units, len(blocks), *refs),
        grid=(steps,),
        in_specs=[
            pl.BlockSpec(memory_space=pltpu.SMEM),
            pl.BlockSpec((1, features), lambda r: (0, 0)),
            pl.BlockSpec(memory_space=pl.ANY),
            *[by_rows(width)] * len(blocks),
            *[own_rows(width)] * len(grads),
            *[pl.BlockSpec(memory_space=pl.ANY)] * len(shared),
        ],
        out_specs=[
            own_rows(features),
            own_rows(units),
            own_rows(2 * units),
            own_rows(features),
            by_rows(1),
            by_rows(1),
            by_rows(features),
        ],
        out_shape=[
            jax.ShapeDtypeStruct((total, features), BF16),
            jax.ShapeDtypeStruct((total, units), BF16),
            jax.ShapeDtypeStruct((total, 2 * units), BF16),
            jax.ShapeDtypeStruct((total, features), BF16),
            jax.ShapeDtypeStruct((rows, 1), F32),
            jax.ShapeDtypeStruct((rows, 1), F32),
            jax.ShapeDtypeStruct((rows, features), BF16),
        ],
        input_output_aliases={3 + 2 * len(blocks) + i: i for i in range(len(shared))},
        scratch_shapes=[pltpu.VMEM((features, 3 * units), BF16), pltpu.SemaphoreType.DMA((3,))],
        cost_estimate=pl.CostEstimate(
            flops=10 * rows * features * units,
            bytes_accessed=6 * features * units + 14 * rows * features,
            transcendentals=2 * rows * units,
        ),
        name="mlp",
    )(at, gain, w, *blocks, *grads, *shared)


def decay_vectors(log_gamma):
    down = lax.broadcasted_iota(jnp.int32, (BLOCK, 1), 0).astype(F32)
    across = lax.broadcasted_iota(jnp.int32, (1, BLOCK), 1).astype(F32)
    return jnp.exp(down * log_gamma), jnp.exp(-across * log_gamma)


def block_decay(scores, r, j, log_gamma, down, across):
    out = scores * (down * jnp.exp(log_gamma * (BLOCK * (r - j)))) * across
    if r == j:
        n = lax.broadcasted_iota(jnp.int32, scores.shape, 0)
        m = lax.broadcasted_iota(jnp.int32, scores.shape, 1)
        out = jnp.where(n >= m, out, 0.0)
    return out.astype(BF16)


def cut(r):
    return slice(r * BLOCK, (r + 1) * BLOCK)


def forward_kernel(first, count, n_pieces, lg_ref, factor_ref, q_ref, k_ref, v_ref, gate_ref, w_ref, *refs):
    gated_ref, ret_ref, out_ref, acc_ref = refs[-4:]
    head = pl.program_id(0)
    log_gamma = lg_ref[head]
    down, across = decay_vectors(log_gamma)
    state = whole_state(refs[:n_pieces], factor_ref, head)
    for at in range(count):
        r = first + at
        q = q_ref[cut(at), :]
        ret = nn(q, state) * (down * jnp.exp(log_gamma * (BLOCK * r)))
        for j in range(r + 1):
            weights = block_decay(nt(q, k_ref[cut(j), :]), r, j, log_gamma, down, across)
            ret = ret + nn(weights, v_ref[cut(j), :])
        ret_ref[cut(at), :] = ret
        scale = lax.rsqrt(jnp.mean(ret * ret, axis=1, keepdims=True) + EPSILON)
        gate = gate_ref[cut(at), :]
        gated = (gate / (1.0 + jnp.exp(-gate)) * (ret * scale)).astype(BF16)
        gated_ref[cut(at), :] = gated
        out = nt(gated, w_ref[...])

        @pl.when(head == 0)
        def _(at=at, out=out):
            acc_ref[cut(at), :] = out

        @pl.when(head > 0)
        def _(at=at, out=out):
            acc_ref[cut(at), :] += out

        @pl.when(head == pl.num_programs(0) - 1)
        def _(at=at):
            out_ref[cut(at), :] = acc_ref[cut(at), :].astype(BF16)


def retention_forward(part, parts, log_gamma, q, k, v, gate, pieces, factors, w, shared):
    rows = q.shape[0]
    heads = q.shape[1] // HK
    features = w.shape[0]
    own = rows // parts
    seen = own * (part + 1)
    count = own // BLOCK
    pairs = sum(part * count + at + 1 for at in range(count))
    flops = heads * (pairs * 2 * BLOCK * BLOCK * (HK + HV) + 2 * own * HK * HV + 2 * own * HV * features)
    head_out = pl.BlockSpec((own, HV), lambda h: (part, h))
    return pl.pallas_call(
        lambda *refs: forward_kernel(part * count, count, len(pieces), *refs),
        grid=(heads,),
        in_specs=[
            pl.BlockSpec(memory_space=pltpu.SMEM),
            pl.BlockSpec(memory_space=pltpu.SMEM),
            pl.BlockSpec((own, HK), lambda h: (part, h)),
            pl.BlockSpec((seen, HK), lambda h: (0, h)),
            pl.BlockSpec((seen, HV), lambda h: (0, h)),
            pl.BlockSpec((own, HV), lambda h: (part, h)),
            pl.BlockSpec((features, HV), lambda h: (0, h)),
            *[pl.BlockSpec((1, HK, HV), lambda h: (h, 0, 0))] * len(pieces),
            *[pl.BlockSpec(memory_space=pl.ANY)] * len(shared),
        ],
        out_specs=[head_out, head_out, pl.BlockSpec((own, features), lambda h: (0, 0))],
        input_output_aliases={7 + len(pieces) + i: i for i in range(len(shared))},
        out_shape=[
            jax.ShapeDtypeStruct((rows, heads * HV), BF16),
            jax.ShapeDtypeStruct((rows, heads * HV), F32),
            jax.ShapeDtypeStruct((own, features), BF16),
        ],
        scratch_shapes=[pltpu.VMEM((own, features), F32)],
        cost_estimate=pl.CostEstimate(flops=flops, bytes_accessed=20 * own * heads * HV, transcendentals=own * heads * HV),
        name="fwd",
    )(log_gamma, factors, q, k, v, gate, w, *pieces, *shared)


def gate_backward_kernel(first, count, n_blocks, at_ref, lg_ref, q_ref, w_ref, gate_ref, ret_ref, *refs):
    blocks, (g_gate_ref, g_ret_ref, full_ref, state_ref, rounded_ref, inner_ref) = refs[:n_blocks], refs[-6:]
    head = pl.program_id(0)
    log_gamma = lg_ref[head]
    down, _ = decay_vectors(log_gamma)
    n = n_blocks // 2 + 1
    width = blocks[0].shape[1]
    here = at_ref[0]
    state = refs[n_blocks][0] if first else None
    for at in range(count):
        r = first + at

        @pl.when(head == 0)
        def _(at=at):
            for k in range(n):
                full_ref[cut(at), columns_of(here, n, k, width)] = gathered(here, blocks, k, cut(at))

        grad = nn(full_ref[cut(at), :], w_ref[...])
        ret = ret_ref[cut(at), :]
        gate = gate_ref[cut(at), :]
        scale = lax.rsqrt(jnp.mean(ret * ret, axis=1, keepdims=True) + EPSILON)
        grouped = ret * scale
        sig = 1.0 / (1.0 + jnp.exp(-gate))
        g_gate = (grad * grouped * (sig * (1.0 + gate * (1.0 - sig)))).astype(BF16)
        g = grad * (gate * sig)
        g_ret = (scale * (g - grouped * jnp.mean(g * grouped, axis=1, keepdims=True))).astype(BF16)
        g_gate_ref[cut(at), :] = g_gate
        g_ret_ref[cut(at), :] = g_ret
        inner_ref[0, cut(at), :] = jnp.sum(g_gate.astype(F32) * gate, axis=1, keepdims=True)
        q = (q_ref[cut(at), :].astype(F32) * (down * jnp.exp(log_gamma * (BLOCK * r)))).astype(BF16)
        add = tn(q, g_ret)
        state = add if state is None else state + add
    state_ref[0] = state
    rounded_ref[0] = state.astype(BF16)


def gate_backward(part, parts, here, log_gamma, q, w, gate, ret, x, pairs, shared, state):
    rows = q.shape[0]
    heads = q.shape[1] // HK
    features = w.shape[0]
    own = rows // parts
    count = own // BLOCK
    blocks = flat(x, pairs)
    head_out = pl.BlockSpec((own, HV), lambda h: (part, h))
    head_state = pl.BlockSpec((1, HK, HV), lambda h: (h, 0, 0))
    before = [state] if part else []
    return pl.pallas_call(
        lambda *refs: gate_backward_kernel(part * count, count, len(blocks), *refs),
        grid=(heads,),
        in_specs=[
            pl.BlockSpec(memory_space=pltpu.SMEM),
            pl.BlockSpec(memory_space=pltpu.SMEM),
            pl.BlockSpec((own, HK), lambda h: (part, h)),
            pl.BlockSpec((features, HV), lambda h: (0, h)),
            head_out,
            head_out,
            *[pl.BlockSpec((own, x.shape[1]), lambda h: (0, 0))] * len(blocks),
            *[head_state] * len(before),
            *[pl.BlockSpec(memory_space=pl.ANY)] * len(shared),
        ],
        out_specs=[
            head_out,
            head_out,
            pl.BlockSpec((own, features), lambda h: (part, 0)),
            head_state,
            head_state,
            pl.BlockSpec((1, own, 1), lambda h: (h, 0, 0)),
        ],
        input_output_aliases={6 + len(blocks) + len(before) + i: i for i in range(len(shared))},
        out_shape=[
            jax.ShapeDtypeStruct((rows, heads * HV), BF16),
            jax.ShapeDtypeStruct((rows, heads * HV), BF16),
            jax.ShapeDtypeStruct((rows, features), BF16),
            jax.ShapeDtypeStruct((heads, HK, HV), F32),
            jax.ShapeDtypeStruct((heads, HK, HV), BF16),
            jax.ShapeDtypeStruct((heads, own, 1), F32),
        ],
        cost_estimate=pl.CostEstimate(
            flops=heads * 2 * own * HV * (HK + features),
            bytes_accessed=16 * own * heads * HV,
            transcendentals=own * heads * HV,
        ),
        name="gate",
    )(here, log_gamma, q, w, gate, ret, *blocks, *before, *shared)


def backward_kernel(total, n_pieces, lg_ref, in_ref, out_ref, q_ref, k_ref, v_ref, cos_ref, sin_ref, *refs):
    earlier, later = refs[:n_pieces], refs[n_pieces : 2 * n_pieces]
    g_ref, gate_ref, all_ref, inner_ref, acc_k, acc_v, g_q_ref, g_k_ref, g_v_ref, sems = refs[2 * n_pieces :]
    head, heads = pl.program_id(0), pl.num_programs(0)
    log_gamma = lg_ref[head]
    down, across = decay_vectors(log_gamma)
    state_in, state_grad = whole_state(earlier, in_ref, head), whole_state(later, out_ref, head)
    key_scale = 1.0 / math.sqrt(HK)

    def send(ref, column, width, i):
        target = all_ref.at[:, pl.ds(pl.multiple_of(column, HK), width)]
        return pltpu.make_async_copy(ref, target, sems.at[i])

    gates = send(gate_ref, heads * (2 * HK + HV) + head * HV, HV, 0)
    gates.start()

    def put(ref, r, x, factor):
        turned = x * cos_ref[cut(r), :] - pair_swap(x) * sin_ref[cut(r), :]
        ref[cut(r), :] = (turned * factor).astype(BF16)

    for r in range(total):
        g = g_ref[cut(r), :]
        q, k, v = q_ref[cut(r), :], k_ref[cut(r), :], v_ref[cut(r), :]
        tail = down_tail(log_gamma, total * BLOCK - r * BLOCK)
        acc_v[cut(r), :] = nn((k.astype(F32) * tail).astype(BF16), state_grad)
        acc_k[cut(r), :] = nt(v, state_grad) * tail
        g_q = nt(g, state_in) * (down * jnp.exp(log_gamma * (BLOCK * r)))
        for j in range(r + 1):
            kj, vj = k_ref[cut(j), :], v_ref[cut(j), :]
            weights = block_decay(nt(q, kj), r, j, log_gamma, down, across)
            g_scores = block_decay(nt(g, vj), r, j, log_gamma, down, across)
            acc_v[cut(j), :] += tn(weights, g)
            acc_k[cut(j), :] += tn(g_scores, q)
            g_q = g_q + nn(g_scores, kj)
        inner_ref[0, cut(r), :] = jnp.sum(g_q * q.astype(F32), axis=1, keepdims=True)
        put(g_q_ref, r, g_q, 1.0)
    for r in range(total):
        g_k = acc_k[cut(r), :]
        g_v = acc_v[cut(r), :].astype(BF16)
        g_v_ref[cut(r), :] = g_v
        inner_ref[0, cut(r), :] += jnp.sum(g_k * k_ref[cut(r), :].astype(F32), axis=1, keepdims=True) + jnp.sum(
            g_v.astype(F32) * v_ref[cut(r), :].astype(F32), axis=1, keepdims=True
        )
        put(g_k_ref, r, g_k, key_scale)
    copies = [
        send(g_q_ref, head * HK, HK, 1),
        send(g_k_ref, (heads + head) * HK, HK, 2),
        send(g_v_ref, 2 * heads * HK + head * HV, HV, 3),
    ]
    for copy in copies:
        copy.start()
    for copy in [gates] + copies:
        copy.wait()


def down_tail(log_gamma, start):
    m = lax.broadcasted_iota(jnp.int32, (BLOCK, 1), 0).astype(F32)
    return jnp.exp((start - m) * log_gamma)


def retention_backward(log_gamma, q, k, v, before, behind, factors, cosine, sine, g_ret, g_gate):
    rows = q.shape[0]
    heads = q.shape[1] // HK
    blocks = rows // BLOCK
    pairs = blocks * (blocks + 1) // 2
    flops = heads * 2 * (pairs * BLOCK * BLOCK * (3 * HK + 2 * HV) + 3 * rows * HK * HV)
    head_keys = pl.BlockSpec((rows, HK), lambda h: (0, h))
    head_values = pl.BlockSpec((rows, HV), lambda h: (0, h))
    head_state = pl.BlockSpec((1, HK, HV), lambda h: (h, 0, 0))
    table = pl.BlockSpec((rows, HK), lambda h: (0, 0))
    return pl.pallas_call(
        lambda *refs: backward_kernel(blocks, len(before), *refs),
        grid=(heads,),
        in_specs=[
            *[pl.BlockSpec(memory_space=pltpu.SMEM)] * 3,
            head_keys,
            head_keys,
            head_values,
            table,
            table,
            *[head_state] * (2 * len(before)),
            head_values,
            head_values,
        ],
        out_specs=[pl.BlockSpec(memory_space=pl.ANY), pl.BlockSpec((1, rows, 1), lambda h: (h, 0, 0))],
        out_shape=[
            jax.ShapeDtypeStruct((rows, heads * 2 * (HK + HV)), BF16),
            jax.ShapeDtypeStruct((heads, rows, 1), F32),
        ],
        scratch_shapes=[
            pltpu.VMEM((rows, HK), F32),
            pltpu.VMEM((rows, HV), F32),
            pltpu.VMEM((rows, HK), BF16),
            pltpu.VMEM((rows, HK), BF16),
            pltpu.VMEM((rows, HV), BF16),
            pltpu.SemaphoreType.DMA((4,)),
        ],
        cost_estimate=pl.CostEstimate(flops=flops, bytes_accessed=24 * rows * heads * HK, transcendentals=0),
        name="bwd",
    )(log_gamma, *factors, q, k, v, cosine, sine, *before, *behind, g_ret, g_gate)


def on_device(
    layer_input,
    gain_attn,
    w_query,
    w_key,
    w_value,
    w_retgate,
    w_out,
    gain_mlp,
    w_gate,
    w_up,
    w_down,
    cotangent,
):
    data = (DP, CTX)
    rows, width = layer_input.shape
    n_tp, at_tp = lax.axis_size(TP), lax.axis_index(TP)
    features = width * n_tp
    heads = w_query.shape[1] // HK
    units = w_gate.shape[1]

    parts = 2
    own = rows // parts
    cuts = [slice(c * own, (c + 1) * own) for c in range(parts)]

    qk = heads * HK
    vw = heads * HV
    attn_shard = side_by_side(w_query, w_key, w_value, w_retgate)
    attn_full = lax.all_gather(attn_shard, data, axis=0, tiled=True)
    out_full = lax.all_gather(w_out, data, axis=0, tiled=True)

    gains = small_gather(jnp.stack([gain_attn, gain_mlp]), TP)

    log_gamma = jnp.log1p(-jnp.exp2(-5.0 - (at_tp * heads + jnp.arange(heads)).astype(F32)))
    log_block = rows * log_gamma
    positions = lax.axis_index(CTX) * rows + jnp.arange(rows)
    frequencies = jnp.exp(-math.log(10000.0) * jnp.linspace(0.0, 1.0, HK // 2, dtype=F32))
    angles = positions.astype(F32)[:, None] * jnp.repeat(frequencies, 2)[None, :]
    cosine = jnp.cos(angles)
    sine = jnp.sin(angles) * jnp.where(jnp.arange(HK) % 2 == 0, -1.0, 1.0)[None, :]
    here = at_tp.reshape(1)
    factors = state_factors(log_block, CTX)
    mlp_shard = side_by_side(w_gate, w_up, w_down)

    x_pairs = [
        line_gather(layer_input[cuts[c]], TP, () if c else (cosine, sine, mlp_shard, log_gamma, gains, *factors))
        for c in range(parts)
    ]
    tokens, scale_attn, local_state = [], [], None
    for c in range(parts):
        *tokens, scale, local_state, rounded = project(
            c,
            parts,
            here,
            log_gamma,
            gains[0:1],
            attn_full,
            layer_input[cuts[c]],
            x_pairs[c],
            heads,
            cosine,
            sine,
            tokens,
            local_state,
        )
        scale_attn.append(scale)
    normed, q, k, v = tokens
    cot = after(cotangent, x_pairs[-1][-1][0])
    cot_blocks = flat(cot, line_gather(cot, TP))
    gate_pre = product(after(normed, local_state), attn_full, (2 * qk + vw) // vw, vw)
    earlier = states_before(local_state, rounded, log_block, CTX)
    mlp_full = lax.all_gather(after(mlp_shard, earlier[-1]), data, axis=0, tiled=True)
    heads_out, branch = [], []
    for c in range(parts):
        *heads_out, out = retention_forward(
            c, parts, log_gamma, q, k, v, gate_pre, earlier, factors[0], out_full, heads_out
        )
        branch.append(out)
    gated, retained = heads_out

    x_own = layer_input.astype(F32)
    middle, mid_pairs, scale_mlp, inner_mlp, back, grad_middle, grad_own, grad_pairs = ([] for _ in range(8))
    gain_mlp_sum = 0.0

    def norm_back(own_rows, scale, gain, inner, grad_normed):
        hat = own_rows * scale
        grad = scale * (grad_normed * gain[None, :] - hat * (inner[:, None] / features))
        return grad, jnp.sum(grad_normed * hat, axis=0)

    def row_total(inner):
        lanes = 128
        return swap_sum(inner.reshape(-1, lanes), TP).reshape(-1)

    early = ()
    for c in range(parts):
        total, steps = line_scatter(after(branch[c], *early), TP)
        early = steps[-1]
        if c:
            total = after(total, mid_pairs[c - 1][0][0])
        middle.append(x_own[cuts[c]] + total)
        mid_pairs.append(line_gather(middle[c].astype(BF16), TP))
    shared = []
    for c in range(parts):
        *results, scale, inner, out = mlp(
            here, gains[1:2], mlp_full, c, cot_blocks, middle[c].astype(BF16), mid_pairs[c], shared
        )
        shared = results
        scale_mlp.append(scale)
        inner_mlp.append(inner[:, 0])
        back.append(out)
    normed_mlp, hidden, grad_acts, grad_full = shared
    early = ()
    for c in range(parts):
        inner = row_total(inner_mlp[c])
        total, steps = line_scatter(after(back[c], *early), TP)
        early = steps[-1]
        if c:
            total = after(total, grad_pairs[c - 1][0][0])
        grad_mid, gain_sum = norm_back(middle[c], scale_mlp[c], gain_mlp, inner, total)
        gain_mlp_sum = gain_mlp_sum + gain_sum
        grad_middle.append(cotangent[cuts[c]].astype(F32) + grad_mid)
        grad_own.append(grad_middle[c].astype(BF16))
        grad_pairs.append(line_gather(grad_own[c], TP))
    grad_down = tn(grad_full, hidden).astype(BF16)
    grad_gate_up = tn(after(normed_mlp, grad_down), grad_acts).astype(BF16)
    mlp_parts = nt(hidden, mlp_full[:, 2 * units :]).astype(BF16)

    grad_own[0] = after(grad_own[0], grad_gate_up, grad_down)
    mlp_out = routed_scatter(after(mlp_parts, grad_pairs[-1][-1][0]), TP)
    layer_output = (jnp.concatenate(middle) + mlp_out).astype(BF16)
    shared = []
    partial_state = None
    inner_attn = []
    for c in range(parts):
        *shared, partial_state, rounded, inner = gate_backward(
            c,
            parts,
            here,
            log_gamma,
            q,
            out_full,
            gate_pre,
            retained,
            grad_own[c],
            grad_pairs[c],
            shared,
            partial_state,
        )
        inner_attn.append(jnp.sum(inner[:, :, 0], axis=0))
    g_gate, g_ret, grad_attn = shared
    later = states_after(partial_state, rounded, log_block, CTX)
    grad_out = tn(after(grad_attn, later[0]), gated).astype(BF16)
    grads_attn, inner = retention_backward(
        log_gamma, q, k, v, earlier, [after(later[0], grad_out), *later[1:]], factors, cosine, sine, g_ret, g_gate
    )
    inner_attn = jnp.concatenate(inner_attn) + jnp.sum(inner[:, :, 0], axis=0)
    back = []
    for c in range(parts):
        rows_grads = after(grads_attn, *back, *([grad_in_w] if c else []))
        back.append(nt(rows_grads[cuts[c]], attn_full).astype(BF16))
        if c == 0:
            grad_in_w = tn(normed, after(grads_attn, *back)).astype(BF16)

    def shard(grad):
        return lax.psum_scatter(grad, data, scatter_dimension=0, tiled=True).astype(F32)

    s_down = shard(grad_down)
    s_gate_up = shard(grad_gate_up)
    s_gate, s_up = s_gate_up[:, :units], s_gate_up[:, units:]
    s_out = shard(grad_out)
    s_in = shard(grad_in_w)
    inner_attn, s_down, s_gate, s_up, s_out, layer_output = lax.optimization_barrier(
        (inner_attn, s_down, s_gate, s_up, s_out, layer_output)
    )
    inner_attn = row_total(inner_attn)
    grad_input, gain_attn_sum = [], 0.0
    early = ()
    for c in range(parts):
        total, steps = line_scatter(after(back[c], *early), TP)
        early = steps[0]
        grad_in, gain_sum = norm_back(x_own[cuts[c]], scale_attn[c], gain_attn, inner_attn[cuts[c]], total)
        grad_input.append((grad_middle[c] + grad_in).astype(BF16))
        gain_attn_sum = gain_attn_sum + gain_sum
    grad_input = jnp.concatenate(grad_input)

    gain_sums = swap_sum(swap_sum(jnp.stack([gain_attn_sum, gain_mlp_sum]), CTX), DP)
    return (
        layer_output,
        grad_input,
        gain_sums[0],
        s_in[:, :qk],
        s_in[:, qk : 2 * qk],
        s_in[:, 2 * qk : 2 * qk + vw],
        s_in[:, 2 * qk + vw :],
        s_out,
        gain_sums[1],
        s_gate,
        s_up,
        s_down,
    )


def solution(mesh):
    tokens = P((DP, CTX), TP)
    gain = P(TP)
    weight = P((DP, CTX), TP)

    return jax.shard_map(
        on_device,
        mesh=mesh,
        in_specs=(tokens, gain, weight, weight, weight, weight, weight, gain, weight, weight, weight, tokens),
        out_specs=(tokens, tokens, gain, weight, weight, weight, weight, weight, gain, weight, weight, weight),
        check_vma=False,
    )
```

```python
import math

import jax
import jax.numpy as jnp
from jax import lax
from jax.experimental import pallas as pl
from jax.experimental.pallas import tpu as pltpu
from jax.sharding import PartitionSpec as P


HK = 256
HV = 512
EPSILON = 1e-06
EXTRA = 16
BLOCK = 512
TP, CTX, DP = "tp", "ctx", "dp"
F32 = jnp.float32
BF16 = jnp.bfloat16


def nn(a, b):
    return lax.dot_general(a, b, (((1,), (0,)), ((), ())), preferred_element_type=F32)


def tn(a, b):
    return lax.dot_general(a, b, (((0,), (0,)), ((), ())), preferred_element_type=F32)


def nt(a, b):
    return lax.dot_general(a, b, (((1,), (1,)), ((), ())), preferred_element_type=F32)


def after(x, *before):
    return lax.optimization_barrier((x, *before))[0]


def right(lo, hi):
    return [(i, i + 1) for i in range(lo, hi)]


def left(lo, hi):
    return [(i, i - 1) for i in range(hi, lo, -1)]


def line_gather(x, axis, before=()):
    n, i = lax.axis_size(axis), lax.axis_index(axis)
    rights, lefts = [x], [x]
    for k in range(1, n):
        r_pairs = right(k - 1, n - 1)
        l_pairs = left(0, n - k)
        if k == 2 and before:
            rights[-1] = after(rights[-1], *before)
        if 2 * k > n + 1:
            both = lax.ppermute(jnp.where(i >= k - 1, rights[-1], lefts[-1]), axis, r_pairs + l_pairs)
            rights.append(both)
            lefts.append(both)
        else:
            rights.append(lax.ppermute(rights[-1], axis, r_pairs))
            lefts.append(lax.ppermute(lefts[-1], axis, l_pairs))
    return [(rights[k], lefts[n - k]) for k in range(1, n)]


def place(blocks, axis, dtype):
    n, i = lax.axis_size(axis), lax.axis_index(axis)
    rows, width = blocks[0].shape
    full = jnp.zeros((rows, n * width), dtype)
    for k, block in enumerate(blocks):
        at = ((i - k) % n) * width
        full = lax.dynamic_update_slice(full, block.astype(dtype), (0, at))
    return full


def line_scatter(parts, axis):
    n, i = lax.axis_size(axis), lax.axis_index(axis)
    width = parts.shape[1] // n

    def block(j):
        return lax.dynamic_slice(parts, (0, jnp.clip(j, 0, n - 1) * width), (parts.shape[0], width))

    from_left = from_right = None
    early = []
    for k in range(1, n):
        r_pairs = right(0, k)
        l_pairs = left(n - 1 - k, n - 1)
        if 2 * k < n - 1:
            data = block(jnp.where(i < k, i + n - k, i - n + k))
            if from_left is not None:
                data = (data.astype(F32) + jnp.where(i < k, from_left, from_right).astype(F32)).astype(BF16)
            from_left = from_right = lax.ppermute(data, axis, r_pairs + l_pairs)
            from_left = jnp.where(i <= k, from_left, jnp.zeros_like(from_left))
            from_right = jnp.where(i >= n - 1 - k, from_right, jnp.zeros_like(from_right))
        elif 2 * k <= n:
            data = block(jnp.where(i < k, i + n - k, i - n + k))
            if from_left is not None:
                data = (data.astype(F32) + jnp.where(i < k, from_left, from_right).astype(F32)).astype(BF16)
            from_left = lax.ppermute(data, axis, r_pairs)
            from_right = lax.ppermute(data, axis, l_pairs)
        else:
            r_data, l_data = block(i + n - k), block(i - n + k)
            if from_left is not None:
                r_data = (r_data.astype(F32) + from_left.astype(F32)).astype(BF16)
                l_data = (l_data.astype(F32) + from_right.astype(F32)).astype(BF16)
            from_left = lax.ppermute(r_data, axis, r_pairs)
            from_right = lax.ppermute(l_data, axis, l_pairs)
        if k < n - 1:
            early.append((from_left, from_right))
    return block(i).astype(F32) + from_left.astype(F32) + from_right.astype(F32), early


def routed_scatter(parts, axis):
    n, i = lax.axis_size(axis), lax.axis_index(axis)
    width = parts.shape[1] // n

    def block(j):
        return lax.dynamic_slice(parts, (0, (j % n) * width), (parts.shape[0], width))

    total = block(i).astype(F32)
    for k in range(1, n):
        total = total + lax.ppermute(block(i + k), axis, [(j, (j + k) % n) for j in range(n)]).astype(F32)
    return total


def small_gather(x, axis):
    n = lax.axis_size(axis)
    blocks = [x] + [lax.ppermute(x, axis, [(j, (j + s) % n) for j in range(n)]) for s in range(1, n)]
    return place(blocks, axis, x.dtype)


def swap_sum(x, axis):
    n = lax.axis_size(axis)
    g = 1
    while g < n:
        x = x + lax.ppermute(x, axis, [(j, j ^ g) for j in range(n)])
        g *= 2
    return x


def state_factors(log_block, axis):
    n, b = lax.axis_size(axis), lax.axis_index(axis)
    before, behind, g = [], [], 1
    while g < n:
        upper = (b // g) % 2 == 1
        before.append(jnp.where(upper, jnp.exp((b % g).astype(F32) * log_block), 0.0))
        behind.append(jnp.where(upper, 0.0, jnp.exp((g - 1 - b % g).astype(F32) * log_block)))
        g *= 2
    return jnp.stack(before), jnp.stack(behind)


def states_before(local, rounded, log_block, axis):
    n, b = lax.axis_size(axis), lax.axis_index(axis)
    total, pieces, g = local, [], 1
    while g < n:
        got = lax.ppermute(rounded if g == 1 else total.astype(BF16), axis, [(j, j ^ g) for j in range(n)])
        upper = (b // g) % 2 == 1
        pieces.append(got)
        if 2 * g < n:
            whole = jnp.exp(g * log_block)[:, None, None]
            total = jnp.where(upper, whole, 1.0) * got.astype(F32) + jnp.where(upper, 1.0, whole) * total
        g *= 2
    return pieces


def states_after(local, rounded, log_block, axis):
    n, b = lax.axis_size(axis), lax.axis_index(axis)
    total, pieces, g = local, [], 1
    while g < n:
        got = lax.ppermute(rounded if g == 1 else total.astype(BF16), axis, [(j, j ^ g) for j in range(n)])
        upper = (b // g) % 2 == 1
        pieces.append(got)
        if 2 * g < n:
            whole = jnp.exp(g * log_block)[:, None, None]
            total = jnp.where(upper, 1.0, whole) * got.astype(F32) + jnp.where(upper, whole, 1.0) * total
        g *= 2
    return pieces


def whole_state(refs, factor_ref, head):
    state = refs[0][0].astype(F32) * factor_ref[0, head]
    for i in range(1, len(refs)):
        state = state + refs[i][0].astype(F32) * factor_ref[i, head]
    return state.astype(BF16)


def pair_swap(x):
    lane = lax.broadcasted_iota(jnp.int32, x.shape, 1)
    width = x.shape[1]
    return jnp.where(lane % 2 == 0, pltpu.roll(x, width - 1, 1), pltpu.roll(x, 1, 1))


def side_by_side(*arrays):
    rows = arrays[0].shape[0]
    widths = [a.shape[1] for a in arrays]

    def kernel(*refs):
        column = 0
        for ref, width in zip(refs, widths):
            refs[-1][:, column : column + width] = ref[...]
            column += width

    block = min(rows, 64)
    return pl.pallas_call(
        kernel,
        grid=(rows // block,),
        in_specs=[pl.BlockSpec((block, width), lambda r: (r, 0)) for width in widths],
        out_specs=pl.BlockSpec((block, sum(widths)), lambda r: (r, 0)),
        out_shape=jax.ShapeDtypeStruct((rows, sum(widths)), arrays[0].dtype),
        cost_estimate=pl.CostEstimate(flops=0, bytes_accessed=4 * rows * sum(widths), transcendentals=0),
        name="join",
    )(*arrays)


def gathered(at, refs, k, rows=slice(None)):
    if k == 0:
        return refs[0][rows, :]
    return jnp.where(at >= k, refs[2 * k - 1][rows, :], refs[2 * k][rows, :])


def columns_of(at, n, k, width):
    return pl.ds(pl.multiple_of(((at + n - k) % n) * width, width), width)


def fill_normed(at, refs, gain_ref, full_ref):
    n = len(refs) // 2 + 1
    width = refs[0].shape[1]
    blocks = [gathered(at, refs, k).astype(F32) for k in range(n)]
    squares = sum(jnp.sum(b * b, axis=1, keepdims=True) for b in blocks)
    scale = lax.rsqrt(squares / (n * width) + EPSILON)
    for k, b in enumerate(blocks):
        where = columns_of(at, n, k, width)
        full_ref[:, where] = (b * scale * gain_ref[:, where]).astype(BF16)
    return scale


def flat(x, pairs):
    return [x] + [p for pair in pairs for p in pair]


def project_kernel(part, parts, heads, count, at_ref, lg_ref, gain_ref, w_ref, cos_ref, sin_ref, *refs):
    blocks = refs[:count]
    full_ref, q_ref, k_ref, v_ref, scale_ref, state_ref, rounded_ref, kept_ref, sems = refs[-9:]
    qk, vw = heads * HK, heads * HV
    own = full_ref.shape[0]
    copies = []
    for i, (first, width) in enumerate(((qk, qk), (2 * qk, vw), (0, qk))):
        columns = slice(first, first + width)
        copies.append(pltpu.make_async_copy(w_ref.at[:, columns], kept_ref.at[:, columns], sems.at[i]))
        copies[-1].start()
    scale_ref[...] = fill_normed(at_ref[0], blocks, gain_ref, full_ref)
    x = full_ref[...]
    c, s = cos_ref[...], sin_ref[...]
    copies[0].wait()
    k_out = nn(x, kept_ref[:, qk : 2 * qk])
    copies[1].wait()
    v_out = nn(x, kept_ref[:, 2 * qk : 2 * qk + vw]).astype(BF16)
    copies[2].wait()
    q_out = nn(x, kept_ref[:, :qk])
    v_ref[...] = v_out
    m = lax.broadcasted_iota(jnp.int32, (own, 1), 0) + part * own
    for h in range(heads):
        at = slice(h * HK, (h + 1) * HK)
        one = k_out[:, at]
        key = ((one * c + pair_swap(one) * s) * (1.0 / math.sqrt(HK))).astype(BF16)
        k_ref[:, at] = key
        tail = jnp.exp((parts * own - m).astype(F32) * lg_ref[h])
        state = tn((key.astype(F32) * tail).astype(BF16), v_out[:, h * HV : (h + 1) * HV])
        if part:
            state = state + refs[count][h]
        state_ref[h] = state
        rounded_ref[h] = state.astype(BF16)
        one = q_out[:, at]
        q_ref[:, at] = (one * c + pair_swap(one) * s).astype(BF16)


def project(part, parts, at, log_gamma, gain, w, x, pairs, heads, cosine, sine, shared, state):
    own, width = x.shape
    features = w.shape[0]
    outs = 2 * heads * HK + heads * HV
    blocks = flat(x, pairs)
    rows = parts * own

    def here(columns):
        return pl.BlockSpec((own, columns), lambda i: (0, 0))

    def in_all(columns):
        return pl.BlockSpec((own, columns), lambda i: (part, 0))

    states = pl.BlockSpec((heads, HK, HV), lambda i: (0, 0, 0))
    before = [state] if part else []
    return pl.pallas_call(
        lambda *refs: project_kernel(part, parts, heads, len(blocks), *refs),
        grid=(1,),
        in_specs=[
            pl.BlockSpec(memory_space=pltpu.SMEM),
            pl.BlockSpec(memory_space=pltpu.SMEM),
            pl.BlockSpec((1, features), lambda i: (0, 0)),
            pl.BlockSpec(memory_space=pl.ANY),
            in_all(HK),
            in_all(HK),
            *[here(width)] * len(blocks),
            *[states] * len(before),
            *[pl.BlockSpec(memory_space=pl.ANY)] * len(shared),
        ],
        out_specs=[
            in_all(features),
            in_all(heads * HK),
            in_all(heads * HK),
            in_all(heads * HV),
            here(1),
            states,
            states,
        ],
        out_shape=[
            jax.ShapeDtypeStruct((rows, features), BF16),
            jax.ShapeDtypeStruct((rows, heads * HK), BF16),
            jax.ShapeDtypeStruct((rows, heads * HK), BF16),
            jax.ShapeDtypeStruct((rows, heads * HV), BF16),
            jax.ShapeDtypeStruct((own, 1), F32),
            jax.ShapeDtypeStruct((heads, HK, HV), F32),
            jax.ShapeDtypeStruct((heads, HK, HV), BF16),
        ],
        input_output_aliases={6 + len(blocks) + len(before) + i: i for i in range(len(shared))},
        scratch_shapes=[pltpu.VMEM((features, outs), BF16), pltpu.SemaphoreType.DMA((3,))],
        cost_estimate=pl.CostEstimate(
            flops=2 * own * features * outs, bytes_accessed=2 * features * outs + 12 * own * features, transcendentals=0
        ),
        name="proj",
    )(at, log_gamma, gain, w, cosine, sine, *blocks, *before, *shared)


def product_kernel(x_ref, w_ref, out_ref):
    out_ref[...] = nn(x_ref[...], w_ref[...])


def product(x, w, at, columns):
    rows, inner = x.shape
    return pl.pallas_call(
        product_kernel,
        grid=(rows // BLOCK,),
        in_specs=[
            pl.BlockSpec((BLOCK, inner), lambda r: (r, 0)),
            pl.BlockSpec((inner, columns), lambda r: (0, at)),
        ],
        out_specs=pl.BlockSpec((BLOCK, columns), lambda r: (r, 0)),
        out_shape=jax.ShapeDtypeStruct((rows, columns), F32),
        cost_estimate=pl.CostEstimate(
            flops=2 * rows * inner * columns, bytes_accessed=2 * inner * columns + 8 * rows * columns, transcendentals=0
        ),
        name="prod",
    )(x, w)


def mlp_kernel(units, count, at_ref, gain_ref, w_ref, *refs):
    blocks, grads = refs[:count], refs[count : 2 * count]
    full_ref, hidden_ref, acts_ref, grad_ref, scale_ref, back_ref, kept_ref, sems = refs[-8:]
    at, n = at_ref[0], count // 2 + 1
    first = pl.program_id(0) == 0

    def piece(i):
        columns = slice(i * units, (i + 1) * units)
        return pltpu.make_async_copy(w_ref.at[:, columns], kept_ref.at[:, columns], sems.at[i])

    @pl.when(first)
    def _():
        for i in range(3):
            piece(i).start()

    scale_ref[...] = fill_normed(at, blocks, gain_ref, full_ref)
    for k in range(n):
        grad_ref[:, columns_of(at, n, k, grads[0].shape[1])] = gathered(at, grads, k)
    x = full_ref[...]

    @pl.when(first)
    def _():
        for i in range(3):
            piece(i).wait()

    gate = nn(x, kept_ref[:, :units])
    up = nn(x, kept_ref[:, units : 2 * units])
    grad = nn(grad_ref[...], kept_ref[:, 2 * units :])
    cdf = 0.5 * (1.0 + lax.erf(gate * math.sqrt(0.5)))
    gelu = gate * cdf
    density = jnp.exp(-0.5 * gate * gate) * (1.0 / math.sqrt(2.0 * math.pi))
    hidden_ref[...] = (gelu * up).astype(BF16)
    g_gate = (grad * up * (cdf + gate * density)).astype(BF16)
    g_up = (grad * gelu).astype(BF16)
    acts_ref[:, :units] = g_gate
    acts_ref[:, units:] = g_up
    back = (nt(g_gate, kept_ref[:, :units]) + nt(g_up, kept_ref[:, units : 2 * units])).astype(BF16)
    step, rows = pl.program_id(0), back.shape[0]
    back_ref[pl.ds(pl.multiple_of(step * rows, rows), rows), :] = back
    inner = jnp.sum(g_gate.astype(F32) * gate + g_up.astype(F32) * up, axis=1, keepdims=True)
    turned = jnp.transpose(jnp.broadcast_to(inner, (rows, 128)))[:EXTRA]
    first_row = lax.broadcasted_iota(jnp.int32, turned.shape, 0) == 0
    turned = jnp.where(first_row, turned, 0.0).astype(BF16)
    width = blocks[0].shape[1]
    total = pl.num_programs(0) * rows
    for k in range(n):
        where = pl.ds(pl.multiple_of(k * width + step * rows, rows), rows)
        back_ref[total:, where] = turned


def mlp(at, gain, w, part, grads, x, pairs, shared):
    rows, width = x.shape
    features = w.shape[0]
    units = w.shape[1] // 3
    blocks = flat(x, pairs)
    block = BLOCK // 2
    steps = rows // block
    total = grads[0].shape[0]

    def by_rows(columns):
        return pl.BlockSpec((block, columns), lambda r: (r, 0))

    def own_rows(columns):
        return pl.BlockSpec((block, columns), lambda r: (part * steps + r, 0))

    return pl.pallas_call(
        lambda *refs: mlp_kernel(units, len(blocks), *refs),
        grid=(steps,),
        in_specs=[
            pl.BlockSpec(memory_space=pltpu.SMEM),
            pl.BlockSpec((1, features), lambda r: (0, 0)),
            pl.BlockSpec(memory_space=pl.ANY),
            *[by_rows(width)] * len(blocks),
            *[own_rows(width)] * len(grads),
            *[pl.BlockSpec(memory_space=pl.ANY)] * len(shared),
        ],
        out_specs=[
            own_rows(features),
            own_rows(units),
            own_rows(2 * units),
            own_rows(features),
            by_rows(1),
            pl.BlockSpec((rows + EXTRA, features), lambda r: (0, 0)),
        ],
        out_shape=[
            jax.ShapeDtypeStruct((total, features), BF16),
            jax.ShapeDtypeStruct((total, units), BF16),
            jax.ShapeDtypeStruct((total, 2 * units), BF16),
            jax.ShapeDtypeStruct((total, features), BF16),
            jax.ShapeDtypeStruct((rows, 1), F32),
            jax.ShapeDtypeStruct((rows + EXTRA, features), BF16),
        ],
        input_output_aliases={3 + 2 * len(blocks) + i: i for i in range(len(shared))},
        scratch_shapes=[pltpu.VMEM((features, 3 * units), BF16), pltpu.SemaphoreType.DMA((3,))],
        cost_estimate=pl.CostEstimate(
            flops=10 * rows * features * units,
            bytes_accessed=6 * features * units + 14 * rows * features,
            transcendentals=2 * rows * units,
        ),
        name="mlp",
    )(at, gain, w, *blocks, *grads, *shared)


def decay_vectors(log_gamma):
    down = lax.broadcasted_iota(jnp.int32, (BLOCK, 1), 0).astype(F32)
    across = lax.broadcasted_iota(jnp.int32, (1, BLOCK), 1).astype(F32)
    return jnp.exp(down * log_gamma), jnp.exp(-across * log_gamma)


def block_decay(scores, r, j, log_gamma, down, across):
    out = scores * (down * jnp.exp(log_gamma * (BLOCK * (r - j)))) * across
    if r == j:
        n = lax.broadcasted_iota(jnp.int32, scores.shape, 0)
        m = lax.broadcasted_iota(jnp.int32, scores.shape, 1)
        out = jnp.where(n >= m, out, 0.0)
    return out.astype(BF16)


def cut(r):
    return slice(r * BLOCK, (r + 1) * BLOCK)


def forward_kernel(first, count, n_pieces, lg_ref, factor_ref, q_ref, k_ref, v_ref, gate_ref, w_ref, *refs):
    gated_ref, ret_ref, out_ref, acc_ref = refs[-4:]
    head = pl.program_id(0)
    log_gamma = lg_ref[head]
    down, across = decay_vectors(log_gamma)
    state = whole_state(refs[:n_pieces], factor_ref, head)
    for at in range(count):
        r = first + at
        q = q_ref[cut(at), :]
        ret = nn(q, state) * (down * jnp.exp(log_gamma * (BLOCK * r)))
        for j in range(r + 1):
            weights = block_decay(nt(q, k_ref[cut(j), :]), r, j, log_gamma, down, across)
            ret = ret + nn(weights, v_ref[cut(j), :])
        ret_ref[cut(at), :] = ret
        scale = lax.rsqrt(jnp.mean(ret * ret, axis=1, keepdims=True) + EPSILON)
        gate = gate_ref[cut(at), :]
        gated = (gate / (1.0 + jnp.exp(-gate)) * (ret * scale)).astype(BF16)
        gated_ref[cut(at), :] = gated
        out = nt(gated, w_ref[...])

        @pl.when(head == 0)
        def _(at=at, out=out):
            acc_ref[cut(at), :] = out

        @pl.when(head > 0)
        def _(at=at, out=out):
            acc_ref[cut(at), :] += out

        @pl.when(head == pl.num_programs(0) - 1)
        def _(at=at):
            out_ref[cut(at), :] = acc_ref[cut(at), :].astype(BF16)


def retention_forward(part, parts, log_gamma, q, k, v, gate, pieces, factors, w, shared):
    rows = q.shape[0]
    heads = q.shape[1] // HK
    features = w.shape[0]
    own = rows // parts
    seen = own * (part + 1)
    count = own // BLOCK
    pairs = sum(part * count + at + 1 for at in range(count))
    flops = heads * (pairs * 2 * BLOCK * BLOCK * (HK + HV) + 2 * own * HK * HV + 2 * own * HV * features)
    head_out = pl.BlockSpec((own, HV), lambda h: (part, h))
    return pl.pallas_call(
        lambda *refs: forward_kernel(part * count, count, len(pieces), *refs),
        grid=(heads,),
        in_specs=[
            pl.BlockSpec(memory_space=pltpu.SMEM),
            pl.BlockSpec(memory_space=pltpu.SMEM),
            pl.BlockSpec((own, HK), lambda h: (part, h)),
            pl.BlockSpec((seen, HK), lambda h: (0, h)),
            pl.BlockSpec((seen, HV), lambda h: (0, h)),
            pl.BlockSpec((own, HV), lambda h: (part, h)),
            pl.BlockSpec((features, HV), lambda h: (0, h)),
            *[pl.BlockSpec((1, HK, HV), lambda h: (h, 0, 0))] * len(pieces),
            *[pl.BlockSpec(memory_space=pl.ANY)] * len(shared),
        ],
        out_specs=[head_out, head_out, pl.BlockSpec((own, features), lambda h: (0, 0))],
        input_output_aliases={7 + len(pieces) + i: i for i in range(len(shared))},
        out_shape=[
            jax.ShapeDtypeStruct((rows, heads * HV), BF16),
            jax.ShapeDtypeStruct((rows, heads * HV), F32),
            jax.ShapeDtypeStruct((own, features), BF16),
        ],
        scratch_shapes=[pltpu.VMEM((own, features), F32)],
        cost_estimate=pl.CostEstimate(flops=flops, bytes_accessed=20 * own * heads * HV, transcendentals=own * heads * HV),
        name="fwd",
    )(log_gamma, factors, q, k, v, gate, w, *pieces, *shared)


def gate_backward_kernel(first, count, n_blocks, at_ref, lg_ref, q_ref, w_ref, gate_ref, ret_ref, *refs):
    blocks, (g_gate_ref, g_ret_ref, full_ref, state_ref, rounded_ref, inner_ref) = refs[:n_blocks], refs[-6:]
    head = pl.program_id(0)
    log_gamma = lg_ref[head]
    down, _ = decay_vectors(log_gamma)
    n = n_blocks // 2 + 1
    width = blocks[0].shape[1]
    here = at_ref[0]
    state = refs[n_blocks][0] if first else None
    for at in range(count):
        r = first + at

        @pl.when(head == 0)
        def _(at=at):
            for k in range(n):
                full_ref[cut(at), columns_of(here, n, k, width)] = gathered(here, blocks, k, cut(at))

        grad = nn(full_ref[cut(at), :], w_ref[...])
        ret = ret_ref[cut(at), :]
        gate = gate_ref[cut(at), :]
        scale = lax.rsqrt(jnp.mean(ret * ret, axis=1, keepdims=True) + EPSILON)
        grouped = ret * scale
        sig = 1.0 / (1.0 + jnp.exp(-gate))
        g_gate = (grad * grouped * (sig * (1.0 + gate * (1.0 - sig)))).astype(BF16)
        g = grad * (gate * sig)
        g_ret = (scale * (g - grouped * jnp.mean(g * grouped, axis=1, keepdims=True))).astype(BF16)
        g_gate_ref[cut(at), :] = g_gate
        g_ret_ref[cut(at), :] = g_ret
        inner_ref[0, cut(at), :] = jnp.sum(g_gate.astype(F32) * gate, axis=1, keepdims=True)
        q = (q_ref[cut(at), :].astype(F32) * (down * jnp.exp(log_gamma * (BLOCK * r)))).astype(BF16)
        add = tn(q, g_ret)
        state = add if state is None else state + add
    state_ref[0] = state
    rounded_ref[0] = state.astype(BF16)


def gate_backward(part, parts, here, log_gamma, q, w, gate, ret, x, pairs, shared, state):
    rows = q.shape[0]
    heads = q.shape[1] // HK
    features = w.shape[0]
    own = rows // parts
    count = own // BLOCK
    blocks = flat(x, pairs)
    head_out = pl.BlockSpec((own, HV), lambda h: (part, h))
    head_state = pl.BlockSpec((1, HK, HV), lambda h: (h, 0, 0))
    before = [state] if part else []
    return pl.pallas_call(
        lambda *refs: gate_backward_kernel(part * count, count, len(blocks), *refs),
        grid=(heads,),
        in_specs=[
            pl.BlockSpec(memory_space=pltpu.SMEM),
            pl.BlockSpec(memory_space=pltpu.SMEM),
            pl.BlockSpec((own, HK), lambda h: (part, h)),
            pl.BlockSpec((features, HV), lambda h: (0, h)),
            head_out,
            head_out,
            *[pl.BlockSpec((own, x.shape[1]), lambda h: (0, 0))] * len(blocks),
            *[head_state] * len(before),
            *[pl.BlockSpec(memory_space=pl.ANY)] * len(shared),
        ],
        out_specs=[
            head_out,
            head_out,
            pl.BlockSpec((own, features), lambda h: (part, 0)),
            head_state,
            head_state,
            pl.BlockSpec((1, own, 1), lambda h: (h, 0, 0)),
        ],
        input_output_aliases={6 + len(blocks) + len(before) + i: i for i in range(len(shared))},
        out_shape=[
            jax.ShapeDtypeStruct((rows, heads * HV), BF16),
            jax.ShapeDtypeStruct((rows, heads * HV), BF16),
            jax.ShapeDtypeStruct((rows, features), BF16),
            jax.ShapeDtypeStruct((heads, HK, HV), F32),
            jax.ShapeDtypeStruct((heads, HK, HV), BF16),
            jax.ShapeDtypeStruct((heads, own, 1), F32),
        ],
        cost_estimate=pl.CostEstimate(
            flops=heads * 2 * own * HV * (HK + features),
            bytes_accessed=16 * own * heads * HV,
            transcendentals=own * heads * HV,
        ),
        name="gate",
    )(here, log_gamma, q, w, gate, ret, *blocks, *before, *shared)


def backward_kernel(total, n_pieces, lg_ref, in_ref, out_ref, q_ref, k_ref, v_ref, cos_ref, sin_ref, *refs):
    earlier, later = refs[:n_pieces], refs[n_pieces : 2 * n_pieces]
    g_ref, gate_ref, all_ref, inner_ref, acc_k, acc_v, g_q_ref, g_k_ref, g_v_ref, sems = refs[2 * n_pieces :]
    head, heads = pl.program_id(0), pl.num_programs(0)
    log_gamma = lg_ref[head]
    down, across = decay_vectors(log_gamma)
    state_in, state_grad = whole_state(earlier, in_ref, head), whole_state(later, out_ref, head)
    key_scale = 1.0 / math.sqrt(HK)

    def send(ref, column, width, i):
        target = all_ref.at[:, pl.ds(pl.multiple_of(column, HK), width)]
        return pltpu.make_async_copy(ref, target, sems.at[i])

    gates = send(gate_ref, heads * (2 * HK + HV) + head * HV, HV, 0)
    gates.start()

    def put(ref, r, x, factor):
        turned = x * cos_ref[cut(r), :] - pair_swap(x) * sin_ref[cut(r), :]
        ref[cut(r), :] = (turned * factor).astype(BF16)

    for r in range(total):
        g = g_ref[cut(r), :]
        q, k, v = q_ref[cut(r), :], k_ref[cut(r), :], v_ref[cut(r), :]
        tail = down_tail(log_gamma, total * BLOCK - r * BLOCK)
        acc_v[cut(r), :] = nn((k.astype(F32) * tail).astype(BF16), state_grad)
        acc_k[cut(r), :] = nt(v, state_grad) * tail
        g_q = nt(g, state_in) * (down * jnp.exp(log_gamma * (BLOCK * r)))
        for j in range(r + 1):
            kj, vj = k_ref[cut(j), :], v_ref[cut(j), :]
            weights = block_decay(nt(q, kj), r, j, log_gamma, down, across)
            g_scores = block_decay(nt(g, vj), r, j, log_gamma, down, across)
            acc_v[cut(j), :] += tn(weights, g)
            acc_k[cut(j), :] += tn(g_scores, q)
            g_q = g_q + nn(g_scores, kj)
        inner_ref[0, cut(r), :] = jnp.sum(g_q * q.astype(F32), axis=1, keepdims=True)
        put(g_q_ref, r, g_q, 1.0)
    for r in range(total):
        g_k = acc_k[cut(r), :]
        g_v = acc_v[cut(r), :].astype(BF16)
        g_v_ref[cut(r), :] = g_v
        inner_ref[0, cut(r), :] += jnp.sum(g_k * k_ref[cut(r), :].astype(F32), axis=1, keepdims=True) + jnp.sum(
            g_v.astype(F32) * v_ref[cut(r), :].astype(F32), axis=1, keepdims=True
        )
        put(g_k_ref, r, g_k, key_scale)
    copies = [
        send(g_q_ref, head * HK, HK, 1),
        send(g_k_ref, (heads + head) * HK, HK, 2),
        send(g_v_ref, 2 * heads * HK + head * HV, HV, 3),
    ]
    for copy in copies:
        copy.start()
    for copy in [gates] + copies:
        copy.wait()


def down_tail(log_gamma, start):
    m = lax.broadcasted_iota(jnp.int32, (BLOCK, 1), 0).astype(F32)
    return jnp.exp((start - m) * log_gamma)


def retention_backward(log_gamma, q, k, v, before, behind, factors, cosine, sine, g_ret, g_gate):
    rows = q.shape[0]
    heads = q.shape[1] // HK
    blocks = rows // BLOCK
    pairs = blocks * (blocks + 1) // 2
    flops = heads * 2 * (pairs * BLOCK * BLOCK * (3 * HK + 2 * HV) + 3 * rows * HK * HV)
    head_keys = pl.BlockSpec((rows, HK), lambda h: (0, h))
    head_values = pl.BlockSpec((rows, HV), lambda h: (0, h))
    head_state = pl.BlockSpec((1, HK, HV), lambda h: (h, 0, 0))
    table = pl.BlockSpec((rows, HK), lambda h: (0, 0))
    return pl.pallas_call(
        lambda *refs: backward_kernel(blocks, len(before), *refs),
        grid=(heads,),
        in_specs=[
            *[pl.BlockSpec(memory_space=pltpu.SMEM)] * 3,
            head_keys,
            head_keys,
            head_values,
            table,
            table,
            *[head_state] * (2 * len(before)),
            head_values,
            head_values,
        ],
        out_specs=[pl.BlockSpec(memory_space=pl.ANY), pl.BlockSpec((1, rows, 1), lambda h: (h, 0, 0))],
        out_shape=[
            jax.ShapeDtypeStruct((rows, heads * 2 * (HK + HV)), BF16),
            jax.ShapeDtypeStruct((heads, rows, 1), F32),
        ],
        scratch_shapes=[
            pltpu.VMEM((rows, HK), F32),
            pltpu.VMEM((rows, HV), F32),
            pltpu.VMEM((rows, HK), BF16),
            pltpu.VMEM((rows, HK), BF16),
            pltpu.VMEM((rows, HV), BF16),
            pltpu.SemaphoreType.DMA((4,)),
        ],
        cost_estimate=pl.CostEstimate(flops=flops, bytes_accessed=24 * rows * heads * HK, transcendentals=0),
        name="bwd",
    )(log_gamma, *factors, q, k, v, cosine, sine, *before, *behind, g_ret, g_gate)


def on_device(
    layer_input,
    gain_attn,
    w_query,
    w_key,
    w_value,
    w_retgate,
    w_out,
    gain_mlp,
    w_gate,
    w_up,
    w_down,
    cotangent,
):
    data = (DP, CTX)
    rows, width = layer_input.shape
    n_tp, at_tp = lax.axis_size(TP), lax.axis_index(TP)
    features = width * n_tp
    heads = w_query.shape[1] // HK
    units = w_gate.shape[1]

    parts = 2
    own = rows // parts
    cuts = [slice(c * own, (c + 1) * own) for c in range(parts)]

    qk = heads * HK
    vw = heads * HV
    attn_shard = side_by_side(w_query, w_key, w_value, w_retgate)
    attn_full = lax.all_gather(attn_shard, data, axis=0, tiled=True)
    out_full = lax.all_gather(w_out, data, axis=0, tiled=True)

    gains = small_gather(jnp.stack([gain_attn, gain_mlp]), TP)

    log_gamma = jnp.log1p(-jnp.exp2(-5.0 - (at_tp * heads + jnp.arange(heads)).astype(F32)))
    log_block = rows * log_gamma
    positions = lax.axis_index(CTX) * rows + jnp.arange(rows)
    frequencies = jnp.exp(-math.log(10000.0) * jnp.linspace(0.0, 1.0, HK // 2, dtype=F32))
    angles = positions.astype(F32)[:, None] * jnp.repeat(frequencies, 2)[None, :]
    cosine = jnp.cos(angles)
    sine = jnp.sin(angles) * jnp.where(jnp.arange(HK) % 2 == 0, -1.0, 1.0)[None, :]
    here = at_tp.reshape(1)
    factors = state_factors(log_block, CTX)
    mlp_shard = side_by_side(w_gate, w_up, w_down)

    x_pairs = [
        line_gather(layer_input[cuts[c]], TP, () if c else (cosine, sine, mlp_shard, log_gamma, gains, *factors))
        for c in range(parts)
    ]
    tokens, scale_attn, local_state = [], [], None
    for c in range(parts):
        *tokens, scale, local_state, rounded = project(
            c,
            parts,
            here,
            log_gamma,
            gains[0:1],
            attn_full,
            layer_input[cuts[c]],
            x_pairs[c],
            heads,
            cosine,
            sine,
            tokens,
            local_state,
        )
        scale_attn.append(scale)
    normed, q, k, v = tokens
    cot = after(cotangent, x_pairs[-1][-1][0])
    cot_blocks = flat(cot, line_gather(cot, TP))
    gate_pre = product(after(normed, local_state), attn_full, (2 * qk + vw) // vw, vw)
    earlier = states_before(local_state, rounded, log_block, CTX)
    mlp_full = lax.all_gather(after(mlp_shard, earlier[-1]), data, axis=0, tiled=True)
    heads_out, branch = [], []
    for c in range(parts):
        *heads_out, out = retention_forward(
            c, parts, log_gamma, q, k, v, gate_pre, earlier, factors[0], out_full, heads_out
        )
        branch.append(out)
    gated, retained = heads_out

    x_own = layer_input.astype(F32)
    middle, mid_pairs, scale_mlp, back, grad_middle, grad_own, grad_pairs = ([] for _ in range(7))
    gain_mlp_sum = 0.0

    def norm_back(own_rows, scale, gain, inner, grad_normed):
        hat = own_rows * scale
        grad = scale * (grad_normed * gain[None, :] - hat * (inner[:, None] / features))
        return grad, jnp.sum(grad_normed * hat, axis=0)

    def row_total(inner):
        lanes = 128
        return swap_sum(inner.reshape(-1, lanes), TP).reshape(-1)

    early = ()
    for c in range(parts):
        total, steps = line_scatter(after(branch[c], *early), TP)
        early = steps[-1]
        if c:
            total = after(total, mid_pairs[c - 1][0][0])
        middle.append(x_own[cuts[c]] + total)
        mid_pairs.append(line_gather(middle[c].astype(BF16), TP))
    shared = []
    for c in range(parts):
        *results, scale, out = mlp(
            here, gains[1:2], mlp_full, c, cot_blocks, middle[c].astype(BF16), mid_pairs[c], shared
        )
        shared = results
        scale_mlp.append(scale)
        back.append(out)
    normed_mlp, hidden, grad_acts, grad_full = shared
    early = ()
    for c in range(parts):
        total, steps = line_scatter(after(back[c], *early), TP)
        early = steps[-1]
        if c:
            total = after(total, grad_pairs[c - 1][0][0])
        grad_mid, gain_sum = norm_back(middle[c], scale_mlp[c], gain_mlp, total[own], total[:own])
        gain_mlp_sum = gain_mlp_sum + gain_sum
        grad_middle.append(cotangent[cuts[c]].astype(F32) + grad_mid)
        grad_own.append(grad_middle[c].astype(BF16))
        grad_pairs.append(line_gather(grad_own[c], TP))
    grad_down = tn(grad_full, hidden).astype(BF16)
    grad_gate_up = tn(after(normed_mlp, grad_down), grad_acts).astype(BF16)
    mlp_parts = nt(hidden, mlp_full[:, 2 * units :]).astype(BF16)

    grad_own[0] = after(grad_own[0], grad_gate_up, grad_down)
    mlp_out = routed_scatter(after(mlp_parts, grad_pairs[-1][0][0]), TP)
    layer_output = (jnp.concatenate(middle) + mlp_out).astype(BF16)
    shared = []
    partial_state = None
    inner_attn = []
    for c in range(parts):
        *shared, partial_state, rounded, inner = gate_backward(
            c,
            parts,
            here,
            log_gamma,
            q,
            out_full,
            gate_pre,
            retained,
            grad_own[c],
            grad_pairs[c],
            shared,
            partial_state,
        )
        inner_attn.append(jnp.sum(inner[:, :, 0], axis=0))
    g_gate, g_ret, grad_attn = shared
    later = states_after(partial_state, rounded, log_block, CTX)
    grad_out = tn(after(grad_attn, later[0]), gated).astype(BF16)
    grads_attn, inner = retention_backward(
        log_gamma, q, k, v, earlier, [after(later[0], grad_out), *later[1:]], factors, cosine, sine, g_ret, g_gate
    )
    inner_attn = jnp.concatenate(inner_attn) + jnp.sum(inner[:, :, 0], axis=0)
    back = []
    for c in range(parts):
        rows_grads = after(grads_attn, *back, *([grad_in_w] if c else []))
        back.append(nt(rows_grads[cuts[c]], attn_full).astype(BF16))
        if c == 0:
            grad_in_w = tn(normed, after(grads_attn, *back)).astype(BF16)

    def shard(grad):
        return lax.psum_scatter(grad, data, scatter_dimension=0, tiled=True).astype(F32)

    s_down = shard(grad_down)
    s_gate_up = shard(grad_gate_up)
    s_gate, s_up = s_gate_up[:, :units], s_gate_up[:, units:]
    s_out = shard(grad_out)
    s_in = shard(grad_in_w)
    inner_attn, s_down, s_gate, s_up = lax.optimization_barrier((inner_attn, s_down, s_gate, s_up))
    inner_attn = row_total(inner_attn)
    grad_input, gain_attn_sum = [], 0.0
    early = ()
    for c in range(parts):
        total, steps = line_scatter(after(back[c], *early), TP)
        early = steps[0]
        grad_in, gain_sum = norm_back(x_own[cuts[c]], scale_attn[c], gain_attn, inner_attn[cuts[c]], total)
        grad_input.append((grad_middle[c] + grad_in).astype(BF16))
        gain_attn_sum = gain_attn_sum + gain_sum
    grad_input = jnp.concatenate(grad_input)

    gain_sums = swap_sum(swap_sum(jnp.stack([gain_attn_sum, gain_mlp_sum]), CTX), DP)
    return (
        layer_output,
        grad_input,
        gain_sums[0],
        s_in[:, :qk],
        s_in[:, qk : 2 * qk],
        s_in[:, 2 * qk : 2 * qk + vw],
        s_in[:, 2 * qk + vw :],
        s_out,
        gain_sums[1],
        s_gate,
        s_up,
        s_down,
    )


def solution(mesh):
    tokens = P((DP, CTX), TP)
    gain = P(TP)
    weight = P((DP, CTX), TP)

    return jax.shard_map(
        on_device,
        mesh=mesh,
        in_specs=(tokens, gain, weight, weight, weight, weight, weight, gain, weight, weight, weight, tokens),
        out_specs=(tokens, tokens, gain, weight, weight, weight, weight, weight, gain, weight, weight, weight),
        check_vma=False,
    )
```

```python
import math

import jax
import jax.numpy as jnp
from jax import lax
from jax.experimental import pallas as pl
from jax.experimental.pallas import tpu as pltpu
from jax.sharding import PartitionSpec as P


HK = 256
HV = 512
EPSILON = 1e-06
EXTRA = 16
BLOCK = 512
TP, CTX, DP = "tp", "ctx", "dp"
F32 = jnp.float32
BF16 = jnp.bfloat16


def nn(a, b):
    return lax.dot_general(a, b, (((1,), (0,)), ((), ())), preferred_element_type=F32)


def tn(a, b):
    return lax.dot_general(a, b, (((0,), (0,)), ((), ())), preferred_element_type=F32)


def nt(a, b):
    return lax.dot_general(a, b, (((1,), (1,)), ((), ())), preferred_element_type=F32)


def after(x, *before):
    return lax.optimization_barrier((x, *before))[0]


def right(lo, hi):
    return [(i, i + 1) for i in range(lo, hi)]


def left(lo, hi):
    return [(i, i - 1) for i in range(hi, lo, -1)]


def line_gather(x, axis, before=()):
    n, i = lax.axis_size(axis), lax.axis_index(axis)
    rights, lefts = [x], [x]
    for k in range(1, n):
        r_pairs = right(k - 1, n - 1)
        l_pairs = left(0, n - k)
        if k == 2 and before:
            rights[-1] = after(rights[-1], *before)
        if 2 * k > n + 1:
            both = lax.ppermute(jnp.where(i >= k - 1, rights[-1], lefts[-1]), axis, r_pairs + l_pairs)
            rights.append(both)
            lefts.append(both)
        else:
            rights.append(lax.ppermute(rights[-1], axis, r_pairs))
            lefts.append(lax.ppermute(lefts[-1], axis, l_pairs))
    return [(rights[k], lefts[n - k]) for k in range(1, n)]


def place(blocks, axis, dtype):
    n, i = lax.axis_size(axis), lax.axis_index(axis)
    rows, width = blocks[0].shape
    full = jnp.zeros((rows, n * width), dtype)
    for k, block in enumerate(blocks):
        at = ((i - k) % n) * width
        full = lax.dynamic_update_slice(full, block.astype(dtype), (0, at))
    return full


def line_scatter(parts, axis):
    n, i = lax.axis_size(axis), lax.axis_index(axis)
    width = parts.shape[1] // n

    def block(j):
        return lax.dynamic_slice(parts, (0, jnp.clip(j, 0, n - 1) * width), (parts.shape[0], width))

    from_left = from_right = None
    early = []
    for k in range(1, n):
        r_pairs = right(0, k)
        l_pairs = left(n - 1 - k, n - 1)
        if 2 * k < n - 1:
            data = block(jnp.where(i < k, i + n - k, i - n + k))
            if from_left is not None:
                data = (data.astype(F32) + jnp.where(i < k, from_left, from_right).astype(F32)).astype(BF16)
            from_left = from_right = lax.ppermute(data, axis, r_pairs + l_pairs)
            from_left = jnp.where(i <= k, from_left, jnp.zeros_like(from_left))
            from_right = jnp.where(i >= n - 1 - k, from_right, jnp.zeros_like(from_right))
        elif 2 * k <= n:
            data = block(jnp.where(i < k, i + n - k, i - n + k))
            if from_left is not None:
                data = (data.astype(F32) + jnp.where(i < k, from_left, from_right).astype(F32)).astype(BF16)
            from_left = lax.ppermute(data, axis, r_pairs)
            from_right = lax.ppermute(data, axis, l_pairs)
        else:
            r_data, l_data = block(i + n - k), block(i - n + k)
            if from_left is not None:
                r_data = (r_data.astype(F32) + from_left.astype(F32)).astype(BF16)
                l_data = (l_data.astype(F32) + from_right.astype(F32)).astype(BF16)
            from_left = lax.ppermute(r_data, axis, r_pairs)
            from_right = lax.ppermute(l_data, axis, l_pairs)
        if k < n - 1:
            early.append((from_left, from_right))
    return block(i).astype(F32) + from_left.astype(F32) + from_right.astype(F32), early


def routed_scatter(parts, axis):
    n, i = lax.axis_size(axis), lax.axis_index(axis)
    width = parts.shape[1] // n

    def block(j):
        return lax.dynamic_slice(parts, (0, (j % n) * width), (parts.shape[0], width))

    total = block(i).astype(F32)
    for k in range(1, n):
        total = total + lax.ppermute(block(i + k), axis, [(j, (j + k) % n) for j in range(n)]).astype(F32)
    return total


def small_gather(x, axis):
    n = lax.axis_size(axis)
    blocks = [x] + [lax.ppermute(x, axis, [(j, (j + s) % n) for j in range(n)]) for s in range(1, n)]
    return place(blocks, axis, x.dtype)


def swap_sum(x, axis):
    n = lax.axis_size(axis)
    g = 1
    while g < n:
        x = x + lax.ppermute(x, axis, [(j, j ^ g) for j in range(n)])
        g *= 2
    return x


def state_factors(log_block, axis):
    n, b = lax.axis_size(axis), lax.axis_index(axis)
    before, behind, g = [], [], 1
    while g < n:
        upper = (b // g) % 2 == 1
        before.append(jnp.where(upper, jnp.exp((b % g).astype(F32) * log_block), 0.0))
        behind.append(jnp.where(upper, 0.0, jnp.exp((g - 1 - b % g).astype(F32) * log_block)))
        g *= 2
    return jnp.stack(before), jnp.stack(behind)


def states_before(local, rounded, log_block, axis):
    n, b = lax.axis_size(axis), lax.axis_index(axis)
    total, pieces, g = local, [], 1
    while g < n:
        got = lax.ppermute(rounded if g == 1 else total.astype(BF16), axis, [(j, j ^ g) for j in range(n)])
        upper = (b // g) % 2 == 1
        pieces.append(got)
        if 2 * g < n:
            whole = jnp.exp(g * log_block)[:, None, None]
            total = jnp.where(upper, whole, 1.0) * got.astype(F32) + jnp.where(upper, 1.0, whole) * total
        g *= 2
    return pieces


def states_after(local, rounded, log_block, axis):
    n, b = lax.axis_size(axis), lax.axis_index(axis)
    total, pieces, g = local, [], 1
    while g < n:
        got = lax.ppermute(rounded if g == 1 else total.astype(BF16), axis, [(j, j ^ g) for j in range(n)])
        upper = (b // g) % 2 == 1
        pieces.append(got)
        if 2 * g < n:
            whole = jnp.exp(g * log_block)[:, None, None]
            total = jnp.where(upper, 1.0, whole) * got.astype(F32) + jnp.where(upper, whole, 1.0) * total
        g *= 2
    return pieces


def whole_state(refs, factor_ref, head):
    state = refs[0][0].astype(F32) * factor_ref[0, head]
    for i in range(1, len(refs)):
        state = state + refs[i][0].astype(F32) * factor_ref[i, head]
    return state.astype(BF16)


def pair_swap(x):
    lane = lax.broadcasted_iota(jnp.int32, x.shape, 1)
    width = x.shape[1]
    return jnp.where(lane % 2 == 0, pltpu.roll(x, width - 1, 1), pltpu.roll(x, 1, 1))


def side_by_side(*arrays):
    rows = arrays[0].shape[0]
    widths = [a.shape[1] for a in arrays]

    def kernel(*refs):
        column = 0
        for ref, width in zip(refs, widths):
            refs[-1][:, column : column + width] = ref[...]
            column += width

    block = min(rows, 64)
    return pl.pallas_call(
        kernel,
        grid=(rows // block,),
        in_specs=[pl.BlockSpec((block, width), lambda r: (r, 0)) for width in widths],
        out_specs=pl.BlockSpec((block, sum(widths)), lambda r: (r, 0)),
        out_shape=jax.ShapeDtypeStruct((rows, sum(widths)), arrays[0].dtype),
        cost_estimate=pl.CostEstimate(flops=0, bytes_accessed=4 * rows * sum(widths), transcendentals=0),
        name="join",
    )(*arrays)


def gathered(at, refs, k, rows=slice(None)):
    if k == 0:
        return refs[0][rows, :]
    return jnp.where(at >= k, refs[2 * k - 1][rows, :], refs[2 * k][rows, :])


def columns_of(at, n, k, width):
    return pl.ds(pl.multiple_of(((at + n - k) % n) * width, width), width)


def fill_normed(at, refs, gain_ref, full_ref):
    n = len(refs) // 2 + 1
    width = refs[0].shape[1]
    blocks = [gathered(at, refs, k).astype(F32) for k in range(n)]
    squares = sum(jnp.sum(b * b, axis=1, keepdims=True) for b in blocks)
    scale = lax.rsqrt(squares / (n * width) + EPSILON)
    for k, b in enumerate(blocks):
        where = columns_of(at, n, k, width)
        full_ref[:, where] = (b * scale * gain_ref[:, where]).astype(BF16)
    return scale


def flat(x, pairs):
    return [x] + [p for pair in pairs for p in pair]


def project_kernel(part, parts, heads, count, at_ref, lg_ref, gain_ref, w_ref, cos_ref, sin_ref, *refs):
    blocks = refs[:count]
    full_ref, q_ref, k_ref, v_ref, scale_ref, state_ref, rounded_ref, kept_ref, sems = refs[-9:]
    qk, vw = heads * HK, heads * HV
    own = full_ref.shape[0]
    copies = []
    for i, (first, width) in enumerate(((qk, qk), (2 * qk, vw), (0, qk))):
        columns = slice(first, first + width)
        copies.append(pltpu.make_async_copy(w_ref.at[:, columns], kept_ref.at[:, columns], sems.at[i]))
        copies[-1].start()
    scale_ref[...] = fill_normed(at_ref[0], blocks, gain_ref, full_ref)
    x = full_ref[...]
    c, s = cos_ref[...], sin_ref[...]
    copies[0].wait()
    k_out = nn(x, kept_ref[:, qk : 2 * qk])
    copies[1].wait()
    v_out = nn(x, kept_ref[:, 2 * qk : 2 * qk + vw]).astype(BF16)
    copies[2].wait()
    q_out = nn(x, kept_ref[:, :qk])
    v_ref[...] = v_out
    m = lax.broadcasted_iota(jnp.int32, (own, 1), 0) + part * own
    for h in range(heads):
        at = slice(h * HK, (h + 1) * HK)
        one = k_out[:, at]
        key = ((one * c + pair_swap(one) * s) * (1.0 / math.sqrt(HK))).astype(BF16)
        k_ref[:, at] = key
        tail = jnp.exp((parts * own - m).astype(F32) * lg_ref[h])
        state = tn((key.astype(F32) * tail).astype(BF16), v_out[:, h * HV : (h + 1) * HV])
        if part:
            state = state + refs[count][h]
        state_ref[h] = state
        rounded_ref[h] = state.astype(BF16)
        one = q_out[:, at]
        q_ref[:, at] = (one * c + pair_swap(one) * s).astype(BF16)


def project(part, parts, at, log_gamma, gain, w, x, pairs, heads, cosine, sine, shared, state):
    own, width = x.shape
    features = w.shape[0]
    outs = 2 * heads * HK + heads * HV
    blocks = flat(x, pairs)
    rows = parts * own

    def here(columns):
        return pl.BlockSpec((own, columns), lambda i: (0, 0))

    def in_all(columns):
        return pl.BlockSpec((own, columns), lambda i: (part, 0))

    states = pl.BlockSpec((heads, HK, HV), lambda i: (0, 0, 0))
    before = [state] if part else []
    return pl.pallas_call(
        lambda *refs: project_kernel(part, parts, heads, len(blocks), *refs),
        grid=(1,),
        in_specs=[
            pl.BlockSpec(memory_space=pltpu.SMEM),
            pl.BlockSpec(memory_space=pltpu.SMEM),
            pl.BlockSpec((1, features), lambda i: (0, 0)),
            pl.BlockSpec(memory_space=pl.ANY),
            in_all(HK),
            in_all(HK),
            *[here(width)] * len(blocks),
            *[states] * len(before),
            *[pl.BlockSpec(memory_space=pl.ANY)] * len(shared),
        ],
        out_specs=[
            in_all(features),
            in_all(heads * HK),
            in_all(heads * HK),
            in_all(heads * HV),
            here(1),
            states,
            states,
        ],
        out_shape=[
            jax.ShapeDtypeStruct((rows, features), BF16),
            jax.ShapeDtypeStruct((rows, heads * HK), BF16),
            jax.ShapeDtypeStruct((rows, heads * HK), BF16),
            jax.ShapeDtypeStruct((rows, heads * HV), BF16),
            jax.ShapeDtypeStruct((own, 1), F32),
            jax.ShapeDtypeStruct((heads, HK, HV), F32),
            jax.ShapeDtypeStruct((heads, HK, HV), BF16),
        ],
        input_output_aliases={6 + len(blocks) + len(before) + i: i for i in range(len(shared))},
        scratch_shapes=[pltpu.VMEM((features, outs), BF16), pltpu.SemaphoreType.DMA((3,))],
        cost_estimate=pl.CostEstimate(
            flops=2 * own * features * outs, bytes_accessed=2 * features * outs + 12 * own * features, transcendentals=0
        ),
        name="proj",
    )(at, log_gamma, gain, w, cosine, sine, *blocks, *before, *shared)


def product_kernel(x_ref, w_ref, out_ref):
    out_ref[...] = nn(x_ref[...], w_ref[...])


def product(x, w, at, columns):
    rows, inner = x.shape
    return pl.pallas_call(
        product_kernel,
        grid=(rows // BLOCK,),
        in_specs=[
            pl.BlockSpec((BLOCK, inner), lambda r: (r, 0)),
            pl.BlockSpec((inner, columns), lambda r: (0, at)),
        ],
        out_specs=pl.BlockSpec((BLOCK, columns), lambda r: (r, 0)),
        out_shape=jax.ShapeDtypeStruct((rows, columns), F32),
        cost_estimate=pl.CostEstimate(
            flops=2 * rows * inner * columns, bytes_accessed=2 * inner * columns + 8 * rows * columns, transcendentals=0
        ),
        name="prod",
    )(x, w)


def mlp_kernel(units, count, at_ref, gain_ref, w_ref, *refs):
    blocks, grads = refs[:count], refs[count : 2 * count]
    full_ref, hidden_ref, acts_ref, grad_ref, scale_ref, back_ref, kept_ref, sems = refs[-8:]
    at, n = at_ref[0], count // 2 + 1
    first = pl.program_id(0) == 0

    def piece(i):
        columns = slice(i * units, (i + 1) * units)
        return pltpu.make_async_copy(w_ref.at[:, columns], kept_ref.at[:, columns], sems.at[i])

    @pl.when(first)
    def _():
        for i in range(3):
            piece(i).start()

    scale_ref[...] = fill_normed(at, blocks, gain_ref, full_ref)
    for k in range(n):
        grad_ref[:, columns_of(at, n, k, grads[0].shape[1])] = gathered(at, grads, k)
    x = full_ref[...]

    @pl.when(first)
    def _():
        for i in range(3):
            piece(i).wait()

    gate = nn(x, kept_ref[:, :units])
    up = nn(x, kept_ref[:, units : 2 * units])
    grad = nn(grad_ref[...], kept_ref[:, 2 * units :])
    cdf = 0.5 * (1.0 + lax.erf(gate * math.sqrt(0.5)))
    gelu = gate * cdf
    density = jnp.exp(-0.5 * gate * gate) * (1.0 / math.sqrt(2.0 * math.pi))
    hidden_ref[...] = (gelu * up).astype(BF16)
    g_gate = (grad * up * (cdf + gate * density)).astype(BF16)
    g_up = (grad * gelu).astype(BF16)
    acts_ref[:, :units] = g_gate
    acts_ref[:, units:] = g_up
    back = (nt(g_gate, kept_ref[:, :units]) + nt(g_up, kept_ref[:, units : 2 * units])).astype(BF16)
    step, rows = pl.program_id(0), back.shape[0]
    back_ref[pl.ds(pl.multiple_of(step * rows, rows), rows), :] = back
    inner = jnp.sum(g_gate.astype(F32) * gate + g_up.astype(F32) * up, axis=1, keepdims=True)
    turned = jnp.transpose(jnp.broadcast_to(inner, (rows, 128)))[:EXTRA]
    first_row = lax.broadcasted_iota(jnp.int32, turned.shape, 0) == 0
    turned = jnp.where(first_row, turned, 0.0).astype(BF16)
    width = blocks[0].shape[1]
    total = pl.num_programs(0) * rows
    for k in range(n):
        where = pl.ds(pl.multiple_of(k * width + step * rows, rows), rows)
        back_ref[total:, where] = turned


def mlp(at, gain, w, part, grads, x, pairs, shared):
    rows, width = x.shape
    features = w.shape[0]
    units = w.shape[1] // 3
    blocks = flat(x, pairs)
    block = BLOCK // 2
    steps = rows // block
    total = grads[0].shape[0]

    def by_rows(columns):
        return pl.BlockSpec((block, columns), lambda r: (r, 0))

    def own_rows(columns):
        return pl.BlockSpec((block, columns), lambda r: (part * steps + r, 0))

    return pl.pallas_call(
        lambda *refs: mlp_kernel(units, len(blocks), *refs),
        grid=(steps,),
        in_specs=[
            pl.BlockSpec(memory_space=pltpu.SMEM),
            pl.BlockSpec((1, features), lambda r: (0, 0)),
            pl.BlockSpec(memory_space=pl.ANY),
            *[by_rows(width)] * len(blocks),
            *[own_rows(width)] * len(grads),
            *[pl.BlockSpec(memory_space=pl.ANY)] * len(shared),
        ],
        out_specs=[
            own_rows(features),
            own_rows(units),
            own_rows(2 * units),
            own_rows(features),
            by_rows(1),
            pl.BlockSpec((rows + EXTRA, features), lambda r: (0, 0)),
        ],
        out_shape=[
            jax.ShapeDtypeStruct((total, features), BF16),
            jax.ShapeDtypeStruct((total, units), BF16),
            jax.ShapeDtypeStruct((total, 2 * units), BF16),
            jax.ShapeDtypeStruct((total, features), BF16),
            jax.ShapeDtypeStruct((rows, 1), F32),
            jax.ShapeDtypeStruct((rows + EXTRA, features), BF16),
        ],
        input_output_aliases={3 + 2 * len(blocks) + i: i for i in range(len(shared))},
        scratch_shapes=[pltpu.VMEM((features, 3 * units), BF16), pltpu.SemaphoreType.DMA((3,))],
        cost_estimate=pl.CostEstimate(
            flops=10 * rows * features * units,
            bytes_accessed=6 * features * units + 14 * rows * features,
            transcendentals=2 * rows * units,
        ),
        name="mlp",
    )(at, gain, w, *blocks, *grads, *shared)


def decay_vectors(log_gamma):
    down = lax.broadcasted_iota(jnp.int32, (BLOCK, 1), 0).astype(F32)
    across = lax.broadcasted_iota(jnp.int32, (1, BLOCK), 1).astype(F32)
    return jnp.exp(down * log_gamma), jnp.exp(-across * log_gamma)


def block_decay(scores, r, j, log_gamma, down, across):
    out = scores * (down * jnp.exp(log_gamma * (BLOCK * (r - j)))) * across
    if r == j:
        n = lax.broadcasted_iota(jnp.int32, scores.shape, 0)
        m = lax.broadcasted_iota(jnp.int32, scores.shape, 1)
        out = jnp.where(n >= m, out, 0.0)
    return out.astype(BF16)


def cut(r):
    return slice(r * BLOCK, (r + 1) * BLOCK)


def forward_kernel(first, count, n_pieces, lg_ref, factor_ref, q_ref, k_ref, v_ref, gate_ref, w_ref, *refs):
    gated_ref, ret_ref, out_ref, acc_ref = refs[-4:]
    head = pl.program_id(0)
    log_gamma = lg_ref[head]
    down, across = decay_vectors(log_gamma)
    state = whole_state(refs[:n_pieces], factor_ref, head)
    for at in range(count):
        r = first + at
        q = q_ref[cut(at), :]
        ret = nn(q, state) * (down * jnp.exp(log_gamma * (BLOCK * r)))
        for j in range(r + 1):
            weights = block_decay(nt(q, k_ref[cut(j), :]), r, j, log_gamma, down, across)
            ret = ret + nn(weights, v_ref[cut(j), :])
        ret_ref[cut(at), :] = ret
        scale = lax.rsqrt(jnp.mean(ret * ret, axis=1, keepdims=True) + EPSILON)
        gate = gate_ref[cut(at), :]
        gated = (gate / (1.0 + jnp.exp(-gate)) * (ret * scale)).astype(BF16)
        gated_ref[cut(at), :] = gated
        out = nt(gated, w_ref[...])

        @pl.when(head == 0)
        def _(at=at, out=out):
            acc_ref[cut(at), :] = out

        @pl.when(head > 0)
        def _(at=at, out=out):
            acc_ref[cut(at), :] += out

        @pl.when(head == pl.num_programs(0) - 1)
        def _(at=at):
            out_ref[cut(at), :] = acc_ref[cut(at), :].astype(BF16)


def retention_forward(part, parts, log_gamma, q, k, v, gate, pieces, factors, w, shared):
    rows = q.shape[0]
    heads = q.shape[1] // HK
    features = w.shape[0]
    own = rows // parts
    seen = own * (part + 1)
    count = own // BLOCK
    pairs = sum(part * count + at + 1 for at in range(count))
    flops = heads * (pairs * 2 * BLOCK * BLOCK * (HK + HV) + 2 * own * HK * HV + 2 * own * HV * features)
    head_out = pl.BlockSpec((own, HV), lambda h: (part, h))
    return pl.pallas_call(
        lambda *refs: forward_kernel(part * count, count, len(pieces), *refs),
        grid=(heads,),
        in_specs=[
            pl.BlockSpec(memory_space=pltpu.SMEM),
            pl.BlockSpec(memory_space=pltpu.SMEM),
            pl.BlockSpec((own, HK), lambda h: (part, h)),
            pl.BlockSpec((seen, HK), lambda h: (0, h)),
            pl.BlockSpec((seen, HV), lambda h: (0, h)),
            pl.BlockSpec((own, HV), lambda h: (part, h)),
            pl.BlockSpec((features, HV), lambda h: (0, h)),
            *[pl.BlockSpec((1, HK, HV), lambda h: (h, 0, 0))] * len(pieces),
            *[pl.BlockSpec(memory_space=pl.ANY)] * len(shared),
        ],
        out_specs=[head_out, head_out, pl.BlockSpec((own, features), lambda h: (0, 0))],
        input_output_aliases={7 + len(pieces) + i: i for i in range(len(shared))},
        out_shape=[
            jax.ShapeDtypeStruct((rows, heads * HV), BF16),
            jax.ShapeDtypeStruct((rows, heads * HV), F32),
            jax.ShapeDtypeStruct((own, features), BF16),
        ],
        scratch_shapes=[pltpu.VMEM((own, features), F32)],
        cost_estimate=pl.CostEstimate(flops=flops, bytes_accessed=20 * own * heads * HV, transcendentals=own * heads * HV),
        name="fwd",
    )(log_gamma, factors, q, k, v, gate, w, *pieces, *shared)


def gate_backward_kernel(first, count, n_blocks, at_ref, lg_ref, q_ref, w_ref, gate_ref, ret_ref, *refs):
    blocks, (g_gate_ref, g_ret_ref, full_ref, state_ref, rounded_ref, inner_ref) = refs[:n_blocks], refs[-6:]
    head = pl.program_id(0)
    log_gamma = lg_ref[head]
    down, _ = decay_vectors(log_gamma)
    n = n_blocks // 2 + 1
    width = blocks[0].shape[1]
    here = at_ref[0]
    state = refs[n_blocks][0] if first else None
    for at in range(count):
        r = first + at

        @pl.when(head == 0)
        def _(at=at):
            for k in range(n):
                full_ref[cut(at), columns_of(here, n, k, width)] = gathered(here, blocks, k, cut(at))

        grad = nn(full_ref[cut(at), :], w_ref[...])
        ret = ret_ref[cut(at), :]
        gate = gate_ref[cut(at), :]
        scale = lax.rsqrt(jnp.mean(ret * ret, axis=1, keepdims=True) + EPSILON)
        grouped = ret * scale
        sig = 1.0 / (1.0 + jnp.exp(-gate))
        g_gate = (grad * grouped * (sig * (1.0 + gate * (1.0 - sig)))).astype(BF16)
        g = grad * (gate * sig)
        g_ret = (scale * (g - grouped * jnp.mean(g * grouped, axis=1, keepdims=True))).astype(BF16)
        g_gate_ref[cut(at), :] = g_gate
        g_ret_ref[cut(at), :] = g_ret
        inner_ref[0, cut(at), :] = jnp.sum(g_gate.astype(F32) * gate, axis=1, keepdims=True)
        q = (q_ref[cut(at), :].astype(F32) * (down * jnp.exp(log_gamma * (BLOCK * r)))).astype(BF16)
        add = tn(q, g_ret)
        state = add if state is None else state + add
    state_ref[0] = state
    rounded_ref[0] = state.astype(BF16)


def gate_backward(part, parts, here, log_gamma, q, w, gate, ret, x, pairs, shared, state):
    rows = q.shape[0]
    heads = q.shape[1] // HK
    features = w.shape[0]
    own = rows // parts
    count = own // BLOCK
    blocks = flat(x, pairs)
    head_out = pl.BlockSpec((own, HV), lambda h: (part, h))
    head_state = pl.BlockSpec((1, HK, HV), lambda h: (h, 0, 0))
    before = [state] if part else []
    return pl.pallas_call(
        lambda *refs: gate_backward_kernel(part * count, count, len(blocks), *refs),
        grid=(heads,),
        in_specs=[
            pl.BlockSpec(memory_space=pltpu.SMEM),
            pl.BlockSpec(memory_space=pltpu.SMEM),
            pl.BlockSpec((own, HK), lambda h: (part, h)),
            pl.BlockSpec((features, HV), lambda h: (0, h)),
            head_out,
            head_out,
            *[pl.BlockSpec((own, x.shape[1]), lambda h: (0, 0))] * len(blocks),
            *[head_state] * len(before),
            *[pl.BlockSpec(memory_space=pl.ANY)] * len(shared),
        ],
        out_specs=[
            head_out,
            head_out,
            pl.BlockSpec((own, features), lambda h: (part, 0)),
            head_state,
            head_state,
            pl.BlockSpec((1, own, 1), lambda h: (h, 0, 0)),
        ],
        input_output_aliases={6 + len(blocks) + len(before) + i: i for i in range(len(shared))},
        out_shape=[
            jax.ShapeDtypeStruct((rows, heads * HV), BF16),
            jax.ShapeDtypeStruct((rows, heads * HV), BF16),
            jax.ShapeDtypeStruct((rows, features), BF16),
            jax.ShapeDtypeStruct((heads, HK, HV), F32),
            jax.ShapeDtypeStruct((heads, HK, HV), BF16),
            jax.ShapeDtypeStruct((heads, own, 1), F32),
        ],
        cost_estimate=pl.CostEstimate(
            flops=heads * 2 * own * HV * (HK + features),
            bytes_accessed=16 * own * heads * HV,
            transcendentals=own * heads * HV,
        ),
        name="gate",
    )(here, log_gamma, q, w, gate, ret, *blocks, *before, *shared)


def backward_kernel(total, n_pieces, lg_ref, in_ref, out_ref, q_ref, k_ref, v_ref, cos_ref, sin_ref, *refs):
    earlier, later = refs[:n_pieces], refs[n_pieces : 2 * n_pieces]
    g_ref, gate_ref, all_ref, inner_ref, acc_k, acc_v, g_q_ref, g_k_ref, g_v_ref, sems = refs[2 * n_pieces :]
    head, heads = pl.program_id(0), pl.num_programs(0)
    log_gamma = lg_ref[head]
    down, across = decay_vectors(log_gamma)
    state_in, state_grad = whole_state(earlier, in_ref, head), whole_state(later, out_ref, head)
    key_scale = 1.0 / math.sqrt(HK)

    def send(ref, column, width, i):
        target = all_ref.at[:, pl.ds(pl.multiple_of(column, HK), width)]
        return pltpu.make_async_copy(ref, target, sems.at[i])

    gates = send(gate_ref, heads * (2 * HK + HV) + head * HV, HV, 0)
    gates.start()

    def put(ref, r, x, factor):
        turned = x * cos_ref[cut(r), :] - pair_swap(x) * sin_ref[cut(r), :]
        ref[cut(r), :] = (turned * factor).astype(BF16)

    for r in range(total):
        g = g_ref[cut(r), :]
        q, k, v = q_ref[cut(r), :], k_ref[cut(r), :], v_ref[cut(r), :]
        tail = down_tail(log_gamma, total * BLOCK - r * BLOCK)
        acc_v[cut(r), :] = nn((k.astype(F32) * tail).astype(BF16), state_grad)
        acc_k[cut(r), :] = nt(v, state_grad) * tail
        g_q = nt(g, state_in) * (down * jnp.exp(log_gamma * (BLOCK * r)))
        for j in range(r + 1):
            kj, vj = k_ref[cut(j), :], v_ref[cut(j), :]
            weights = block_decay(nt(q, kj), r, j, log_gamma, down, across)
            g_scores = block_decay(nt(g, vj), r, j, log_gamma, down, across)
            acc_v[cut(j), :] += tn(weights, g)
            acc_k[cut(j), :] += tn(g_scores, q)
            g_q = g_q + nn(g_scores, kj)
        inner_ref[0, cut(r), :] = jnp.sum(g_q * q.astype(F32), axis=1, keepdims=True)
        put(g_q_ref, r, g_q, 1.0)
    for r in range(total):
        g_k = acc_k[cut(r), :]
        g_v = acc_v[cut(r), :].astype(BF16)
        g_v_ref[cut(r), :] = g_v
        inner_ref[0, cut(r), :] += jnp.sum(g_k * k_ref[cut(r), :].astype(F32), axis=1, keepdims=True) + jnp.sum(
            g_v.astype(F32) * v_ref[cut(r), :].astype(F32), axis=1, keepdims=True
        )
        put(g_k_ref, r, g_k, key_scale)
    copies = [
        send(g_q_ref, head * HK, HK, 1),
        send(g_k_ref, (heads + head) * HK, HK, 2),
        send(g_v_ref, 2 * heads * HK + head * HV, HV, 3),
    ]
    for copy in copies:
        copy.start()
    for copy in [gates] + copies:
        copy.wait()


def down_tail(log_gamma, start):
    m = lax.broadcasted_iota(jnp.int32, (BLOCK, 1), 0).astype(F32)
    return jnp.exp((start - m) * log_gamma)


def retention_backward(log_gamma, q, k, v, before, behind, factors, cosine, sine, g_ret, g_gate):
    rows = q.shape[0]
    heads = q.shape[1] // HK
    blocks = rows // BLOCK
    pairs = blocks * (blocks + 1) // 2
    flops = heads * 2 * (pairs * BLOCK * BLOCK * (3 * HK + 2 * HV) + 3 * rows * HK * HV)
    head_keys = pl.BlockSpec((rows, HK), lambda h: (0, h))
    head_values = pl.BlockSpec((rows, HV), lambda h: (0, h))
    head_state = pl.BlockSpec((1, HK, HV), lambda h: (h, 0, 0))
    table = pl.BlockSpec((rows, HK), lambda h: (0, 0))
    return pl.pallas_call(
        lambda *refs: backward_kernel(blocks, len(before), *refs),
        grid=(heads,),
        in_specs=[
            *[pl.BlockSpec(memory_space=pltpu.SMEM)] * 3,
            head_keys,
            head_keys,
            head_values,
            table,
            table,
            *[head_state] * (2 * len(before)),
            head_values,
            head_values,
        ],
        out_specs=[pl.BlockSpec(memory_space=pl.ANY), pl.BlockSpec((1, rows, 1), lambda h: (h, 0, 0))],
        out_shape=[
            jax.ShapeDtypeStruct((rows, heads * 2 * (HK + HV)), BF16),
            jax.ShapeDtypeStruct((heads, rows, 1), F32),
        ],
        scratch_shapes=[
            pltpu.VMEM((rows, HK), F32),
            pltpu.VMEM((rows, HV), F32),
            pltpu.VMEM((rows, HK), BF16),
            pltpu.VMEM((rows, HK), BF16),
            pltpu.VMEM((rows, HV), BF16),
            pltpu.SemaphoreType.DMA((4,)),
        ],
        cost_estimate=pl.CostEstimate(flops=flops, bytes_accessed=24 * rows * heads * HK, transcendentals=0),
        name="bwd",
    )(log_gamma, *factors, q, k, v, cosine, sine, *before, *behind, g_ret, g_gate)


def on_device(
    layer_input,
    gain_attn,
    w_query,
    w_key,
    w_value,
    w_retgate,
    w_out,
    gain_mlp,
    w_gate,
    w_up,
    w_down,
    cotangent,
):
    data = (DP, CTX)
    rows, width = layer_input.shape
    n_tp, at_tp = lax.axis_size(TP), lax.axis_index(TP)
    features = width * n_tp
    heads = w_query.shape[1] // HK
    units = w_gate.shape[1]

    parts = 2
    own = rows // parts
    cuts = [slice(c * own, (c + 1) * own) for c in range(parts)]

    qk = heads * HK
    vw = heads * HV
    attn_shard = side_by_side(w_query, w_key, w_value, w_retgate)
    attn_full = lax.all_gather(attn_shard, data, axis=0, tiled=True)
    out_full = lax.all_gather(w_out, data, axis=0, tiled=True)

    gains = small_gather(jnp.stack([gain_attn, gain_mlp]), TP)

    log_gamma = jnp.log1p(-jnp.exp2(-5.0 - (at_tp * heads + jnp.arange(heads)).astype(F32)))
    log_block = rows * log_gamma
    positions = lax.axis_index(CTX) * rows + jnp.arange(rows)
    frequencies = jnp.exp(-math.log(10000.0) * jnp.linspace(0.0, 1.0, HK // 2, dtype=F32))
    angles = positions.astype(F32)[:, None] * jnp.repeat(frequencies, 2)[None, :]
    cosine = jnp.cos(angles)
    sine = jnp.sin(angles) * jnp.where(jnp.arange(HK) % 2 == 0, -1.0, 1.0)[None, :]
    here = at_tp.reshape(1)
    factors = state_factors(log_block, CTX)
    mlp_shard = side_by_side(w_gate, w_up, w_down)

    x_pairs = [
        line_gather(layer_input[cuts[c]], TP, () if c else (cosine, sine, mlp_shard, log_gamma, gains, *factors))
        for c in range(parts)
    ]
    tokens, scale_attn, local_state = [], [], None
    for c in range(parts):
        *tokens, scale, local_state, rounded = project(
            c,
            parts,
            here,
            log_gamma,
            gains[0:1],
            attn_full,
            layer_input[cuts[c]],
            x_pairs[c],
            heads,
            cosine,
            sine,
            tokens,
            local_state,
        )
        scale_attn.append(scale)
    normed, q, k, v = tokens
    cot = after(cotangent, x_pairs[-1][-1][0])
    cot_blocks = flat(cot, line_gather(cot, TP))
    gate_pre = product(after(normed, local_state), attn_full, (2 * qk + vw) // vw, vw)
    earlier = states_before(local_state, rounded, log_block, CTX)
    mlp_full = lax.all_gather(after(mlp_shard, earlier[-1]), data, axis=0, tiled=True)
    heads_out, branch = [], []
    for c in range(parts):
        *heads_out, out = retention_forward(
            c, parts, log_gamma, q, k, v, gate_pre, earlier, factors[0], out_full, heads_out
        )
        branch.append(out)
    gated, retained = heads_out

    x_own = layer_input.astype(F32)
    middle, mid_pairs, scale_mlp, back, grad_middle, grad_own, grad_pairs = ([] for _ in range(7))
    gain_mlp_sum = 0.0

    def norm_back(own_rows, scale, gain, inner, grad_normed):
        hat = own_rows * scale
        grad = scale * (grad_normed * gain[None, :] - hat * (inner[:, None] / features))
        return grad, jnp.sum(grad_normed * hat, axis=0)

    def row_total(inner):
        lanes = 128
        return swap_sum(inner.reshape(-1, lanes), TP).reshape(-1)

    early = ()
    for c in range(parts):
        total, steps = line_scatter(after(branch[c], *early), TP)
        early = steps[-1]
        if c:
            total = after(total, mid_pairs[c - 1][0][0])
        middle.append(x_own[cuts[c]] + total)
        mid_pairs.append(line_gather(middle[c].astype(BF16), TP))
    shared = []
    for c in range(parts):
        *results, scale, out = mlp(
            here, gains[1:2], mlp_full, c, cot_blocks, middle[c].astype(BF16), mid_pairs[c], shared
        )
        shared = results
        scale_mlp.append(scale)
        back.append(out)
    normed_mlp, hidden, grad_acts, grad_full = shared
    early = ()
    for c in range(parts):
        total, steps = line_scatter(after(back[c], *early), TP)
        early = steps[-1]
        if c:
            total = after(total, grad_pairs[c - 1][0][0])
        grad_mid, gain_sum = norm_back(middle[c], scale_mlp[c], gain_mlp, total[own], total[:own])
        gain_mlp_sum = gain_mlp_sum + gain_sum
        grad_middle.append(cotangent[cuts[c]].astype(F32) + grad_mid)
        grad_own.append(grad_middle[c].astype(BF16))
        grad_pairs.append(line_gather(grad_own[c], TP))
    grad_down = tn(grad_full, hidden).astype(BF16)
    grad_gate_up = tn(after(normed_mlp, grad_down), grad_acts).astype(BF16)
    mlp_parts = nt(hidden, mlp_full[:, 2 * units :]).astype(BF16)

    grad_own[0] = after(grad_own[0], grad_gate_up, grad_down)
    mlp_out = routed_scatter(after(mlp_parts, grad_pairs[-1][-1][0]), TP)
    layer_output = (jnp.concatenate(middle) + mlp_out).astype(BF16)
    shared = []
    partial_state = None
    inner_attn = []
    for c in range(parts):
        *shared, partial_state, rounded, inner = gate_backward(
            c,
            parts,
            here,
            log_gamma,
            q,
            out_full,
            gate_pre,
            retained,
            grad_own[c],
            grad_pairs[c],
            shared,
            partial_state,
        )
        inner_attn.append(jnp.sum(inner[:, :, 0], axis=0))
    g_gate, g_ret, grad_attn = shared
    later = states_after(partial_state, rounded, log_block, CTX)
    grad_out = tn(after(grad_attn, later[0]), gated).astype(BF16)
    grads_attn, inner = retention_backward(
        log_gamma, q, k, v, earlier, [after(later[0], grad_out), *later[1:]], factors, cosine, sine, g_ret, g_gate
    )
    inner_attn = jnp.concatenate(inner_attn) + jnp.sum(inner[:, :, 0], axis=0)
    back = []
    for c in range(parts):
        rows_grads = after(grads_attn, *back, *([grad_in_w] if c else []))
        back.append(nt(rows_grads[cuts[c]], attn_full).astype(BF16))
        if c == 0:
            grad_in_w = tn(normed, after(grads_attn, *back)).astype(BF16)

    def shard(grad):
        return lax.psum_scatter(grad, data, scatter_dimension=0, tiled=True).astype(F32)

    s_down = shard(grad_down)
    s_gate_up = shard(grad_gate_up)
    s_gate, s_up = s_gate_up[:, :units], s_gate_up[:, units:]
    s_out = shard(grad_out)
    s_in = shard(grad_in_w)
    inner_attn, s_down, s_gate, s_up, s_out, layer_output = lax.optimization_barrier(
        (inner_attn, s_down, s_gate, s_up, s_out, layer_output)
    )
    inner_attn = row_total(inner_attn)
    grad_input, gain_attn_sum = [], 0.0
    early = ()
    for c in range(parts):
        total, steps = line_scatter(after(back[c], *early), TP)
        early = steps[0]
        grad_in, gain_sum = norm_back(x_own[cuts[c]], scale_attn[c], gain_attn, inner_attn[cuts[c]], total)
        grad_input.append((grad_middle[c] + grad_in).astype(BF16))
        gain_attn_sum = gain_attn_sum + gain_sum
    grad_input = jnp.concatenate(grad_input)

    gain_sums = swap_sum(swap_sum(jnp.stack([gain_attn_sum, gain_mlp_sum]), CTX), DP)
    return (
        layer_output,
        grad_input,
        gain_sums[0],
        s_in[:, :qk],
        s_in[:, qk : 2 * qk],
        s_in[:, 2 * qk : 2 * qk + vw],
        s_in[:, 2 * qk + vw :],
        s_out,
        gain_sums[1],
        s_gate,
        s_up,
        s_down,
    )


def solution(mesh):
    tokens = P((DP, CTX), TP)
    gain = P(TP)
    weight = P((DP, CTX), TP)

    return jax.shard_map(
        on_device,
        mesh=mesh,
        in_specs=(tokens, gain, weight, weight, weight, weight, weight, gain, weight, weight, weight, tokens),
        out_specs=(tokens, tokens, gain, weight, weight, weight, weight, weight, gain, weight, weight, weight),
        check_vma=False,
    )
```
